32 devices in a mesh: head: 2 (over core), blk: 16 (over z, y, x).
Axes of the slice: x: 2, y: 2, z: 4, core: 2. Of those that a mesh axis runs over, the one named last changes fastest.
Arguments:
- tokens: bfloat16 [16, 2048, 768], P('blk', 'head'), may hold values from -6 to 6
- lengths: int32 [8], replicated, may hold values from 2049 to 4096, as said below
- pair_flip: int32 [8, 12], replicated, may hold values from 0 to 1
- w_qkv: bfloat16 [768, 2304], P(('head', 'blk')), may hold values from -0.21875 to 0.21875
- q_bias: bfloat16 [768], P(('head', 'blk')), may hold values from -3 to 3
- v_bias: bfloat16 [768], P(('head', 'blk')), may hold values from -3 to 3
- w_out: bfloat16 [768, 768], P(('head', 'blk')), may hold values from -6 to 6
- out_bias: bfloat16 [768], P(('head', 'blk')), may hold values from -3 to 3
- norm1_gain: bfloat16 [768], P(('head', 'blk')), may hold values from 0.5 to 1.5
- norm1_shift: bfloat16 [768], P(('head', 'blk')), may hold values from -3 to 3
- w_in: bfloat16 [768, 3072], P(('head', 'blk')), may hold values from -0.21875 to 0.21875
- in_bias: bfloat16 [3072], P(('head', 'blk')), may hold values from -3 to 3
- w_back: bfloat16 [3072, 768], P(('head', 'blk')), may hold values from -0.109375 to 0.109375
- back_bias: bfloat16 [768], P(('head', 'blk')), may hold values from -3 to 3
- norm2_gain: bfloat16 [768], P(('head', 'blk')), may hold values from 0.5 to 1.5
- norm2_shift: bfloat16 [768], P(('head', 'blk')), may hold values from -3 to 3
- cotangent: bfloat16 [16, 2048, 768], P('blk', 'head'), may hold values from -6 to 6
Outputs:
- out: bfloat16 [16, 2048, 768], P('blk', 'head')
- grad_tokens: float32 [16, 2048, 768], P('blk', 'head')
- grad_w_qkv: float32 [768, 2304], P(('head', 'blk'))
- grad_q_bias: float32 [768], P(('head', 'blk'))
- grad_v_bias: float32 [768], P(('head', 'blk'))
- grad_w_out: float32 [768, 768], P(('head', 'blk'))
- grad_out_bias: float32 [768], P(('head', 'blk'))
- grad_norm1_gain: float32 [768], P(('head', 'blk'))
- grad_norm1_shift: float32 [768], P(('head', 'blk'))
- grad_w_in: float32 [768, 3072], P(('head', 'blk'))
- grad_in_bias: float32 [3072], P(('head', 'blk'))
- grad_w_back: float32 [3072, 768], P(('head', 'blk'))
- grad_back_bias: float32 [768], P(('head', 'blk'))
- grad_norm2_gain: float32 [768], P(('head', 'blk'))
- grad_norm2_shift: float32 [768], P(('head', 'blk'))
The draws below stay inside these ranges and needn't reach their ends.
Inputs may be any that keep to these rules, and one draw needn't show every extreme that they name: Keys at positions of lengths[s] or more in sequence s are padding; some sequence is full and some has only 2049 tokens.
All inputs are finite; a program needn't handle non-finite values.
Results may differ from the reference program's by a relative error of at most 0.013.
Values may be sent and summed in bfloat16 or wider, within the bound.
No kernel may reach another device: no remote copies, remote signals or barrier semaphores. Data moves between devices by JAX's collectives and lax.ppermute only.
A program may use at most 512 MiB of HBM per device.

```python
import jax
import jax.numpy as jnp
from jax import lax

D = 768
HEADS = 12
HD = 64
FF = 3072
HALF = 2048
SEQ = 4096
HALVES = 16
SEQS = 8


def draw_lengths(key, part):
    spans = jax.random.randint(key, (SEQS,), HALF + 1, SEQ + 1)
    first = jax.random.randint(jax.random.fold_in(key, 11), (), 0, SEQS)
    offset = jax.random.randint(jax.random.fold_in(key, 13), (), 1, SEQS)
    second = (first + offset) % SEQS
    spans = spans.at[first].set(SEQ)
    spans = spans.at[second].set(HALF + 1)
    return spans.astype(jnp.int32)


def with_ends(array, key, least, largest):
    longest = array.shape.index(max(array.shape))
    spots = []
    for shift in (0, 1):
        where = [jax.random.randint(jax.random.fold_in(key, axis), (), 0, length) for axis, length in enumerate(array.shape)]
        where[longest] = (where[longest] + shift) % array.shape[longest]
        spots.append(tuple(where))
    return array.at[spots[0]].set(least).at[spots[1]].set(largest)


def steps_of(rng, dims, shards, smallest, top_value):
    factor_of, own = 1.0, jax.random.fold_in(rng, 6)
    for axis_at, blocks in shards:
        heights = jnp.exp(jax.random.uniform(jax.random.fold_in(own, axis_at), (blocks,), jnp.float32, smallest / len(shards), top_value / len(shards)))
        factor_of = factor_of * jnp.repeat(heights, dims[axis_at] // blocks).reshape([-1 if axis == axis_at else 1 for axis in range(len(dims))])
    return factor_of


def normal_values(key, shape, scale, bound, cuts=(), dtype=jnp.bfloat16):
    drawn = jax.random.normal(key, shape, jnp.float32) * scale
    if len(cuts) > 0:
        drawn = steps_of(key, shape, cuts, -0.22, 0.18) * drawn
    return jnp.clip(drawn, min=-bound, max=bound).astype(dtype)


def setup_inputs(seed: int = 0) -> dict:
    streams_of = jax.random.split(jax.random.key(seed), 18)
    tokens = normal_values(streams_of[0], (HALVES, HALF, D), 1.0, 6.0, ((0, 16), (1, 2)))
    lengths = draw_lengths(jax.random.fold_in(streams_of[17], 71), 0)
    pair_flip = with_ends(jax.random.randint(streams_of[2], (SEQS, HEADS), 0, 2), jax.random.fold_in(streams_of[2], 1), 0, 1).astype(jnp.int32)
    w_qkv = normal_values(streams_of[3], (D, 3 * D), D ** -0.5, 0.21875, ((0, 32),))
    q_bias = normal_values(streams_of[4], (D,), 0.3, 3.0, ((0, 32),))
    v_bias = normal_values(streams_of[5], (D,), 0.3, 3.0, ((0, 32),))
    w_out = normal_values(streams_of[6], (D, D), (max(1, D // HALF)) ** -0.5, 6.0, ((0, 32),))
    out_bias = normal_values(streams_of[7], (D,), 0.3, 3.0, ((0, 32),))
    norm1_gain = jnp.clip(1.0 + 0.1 * jax.random.normal(streams_of[8], (D,), jnp.float32), 0.5, 1.5).astype(jnp.bfloat16)
    norm1_shift = normal_values(streams_of[9], (D,), 0.3, 3.0, ((0, 32),))
    w_in = normal_values(streams_of[10], (D, FF), D ** -0.5, 0.21875, ((0, 32),))
    in_bias = normal_values(streams_of[11], (FF,), 0.3, 3.0, ((0, 32),))
    w_back = normal_values(streams_of[12], (FF, D), FF ** -0.5, 0.109375, ((0, 32),))
    back_bias = normal_values(streams_of[13], (D,), 0.3, 3.0, ((0, 32),))
    norm2_gain = jnp.clip(1.0 + 0.1 * jax.random.normal(streams_of[14], (D,), jnp.float32), 0.5, 1.5).astype(jnp.bfloat16)
    norm2_shift = normal_values(streams_of[15], (D,), 0.3, 3.0, ((0, 32),))
    cotangent = normal_values(streams_of[16], (HALVES, HALF, D), 1.0, 6.0, ((0, 16), (1, 2)))
    return dict(tokens=tokens, lengths=lengths, pair_flip=pair_flip, w_qkv=w_qkv, q_bias=q_bias, v_bias=v_bias, w_out=w_out, out_bias=out_bias, norm1_gain=norm1_gain, norm1_shift=norm1_shift, w_in=w_in, in_bias=in_bias, w_back=w_back, back_bias=back_bias, norm2_gain=norm2_gain, norm2_shift=norm2_shift, cotangent=cotangent)


@jax.custom_vjp
def low(v):
    return lax.optimization_barrier(v.astype(jnp.bfloat16)).astype(jnp.float32)

@jax.custom_vjp
def low_back(v):
    return v

def low_keep(v):
    return (low(v), None)

def low_pass(kept, grad):
    return (grad,)

def back_keep(v):
    return (v, None)

def back_low(kept, grad):
    return (low(grad),)
low.defvjp(low_keep, low_pass)
low_back.defvjp(back_keep, back_low)

def layer_norm(value, gain, shift):
    center = value - lax.optimization_barrier(jnp.mean(value, axis=-1, keepdims=True))
    spread = lax.optimization_barrier(jnp.mean(center * center, axis=-1, keepdims=True))
    return center * lax.rsqrt(spread + 1e-06) * gain + shift

def make_attend(keys_used, values_used, key_valid):
    exact = lax.Precision.HIGHEST
    scale = HD ** (-0.5)

    def attend(query_block):
        scores = jnp.einsum('qhd,khd->hqk', query_block, keys_used, precision=exact)
        logits = jnp.where(key_valid[:, None, :], low_back(scores) * scale, -1e+30)
        peak = lax.optimization_barrier(jnp.max(logits, axis=-1, keepdims=True))
        expo = jnp.exp(logits - peak)
        probs = expo / lax.optimization_barrier(jnp.sum(expo, axis=-1, keepdims=True))
        return jnp.einsum('hqk,khd->qhd', low(probs), values_used, precision=exact)
    return attend

def forward(inputs, weights, length, flags):
    w_qkv, q_bias, v_bias, w_out, out_bias, norm1_gain, norm1_shift, w_in, in_bias, w_back, back_bias, norm2_gain, norm2_shift = weights
    exact = lax.Precision.HIGHEST
    zero_bias = jnp.zeros_like(q_bias)
    projected = jnp.dot(inputs, w_qkv, precision=exact) + jnp.concatenate([q_bias, zero_bias, v_bias])
    projected = low_back(low(projected))
    split = projected.reshape(2, HALF, 3, HEADS, HD)
    queries = split[:, :, 0]
    keys = split[:, :, 1]
    values = split[:, :, 2]
    swapped = (flags == 1)[None, :, None]
    block_rows = min(512, HALF)
    contexts = []
    for half_index in range(2):
        keys_used = jnp.where(swapped, keys[1 - half_index], keys[half_index])
        values_used = jnp.where(swapped, values[1 - half_index], values[half_index])
        source_half = jnp.where(flags == 1, 1 - half_index, half_index)
        key_valid = source_half[:, None] * HALF + jnp.arange(HALF)[None, :] < length
        attend = make_attend(keys_used, values_used, key_valid)
        blocks = queries[half_index].reshape(HALF // block_rows, block_rows, HEADS, HD)
        contexts.append(lax.map(jax.checkpoint(attend), blocks).reshape(HALF, HEADS * HD))
    context = low_back(low(jnp.concatenate(contexts, axis=0)))
    attended = low_back(jnp.dot(context, w_out, precision=exact) + out_bias)
    normed1 = layer_norm(inputs + attended, norm1_gain, norm1_shift)
    hidden = low_back(jnp.dot(low(normed1), w_in, precision=exact) + in_bias)
    activ = low(jax.nn.gelu(hidden, approximate=False))
    branch = low_back(jnp.dot(activ, w_back, precision=exact) + back_bias)
    return layer_norm(normed1 + branch, norm2_gain, norm2_shift)

def reference(tokens, lengths, pair_flip, w_qkv, q_bias, v_bias, w_out, out_bias, norm1_gain, norm1_shift, w_in, in_bias, w_back, back_bias, norm2_gain, norm2_shift, cotangent):
    weights = tuple((item.astype(jnp.float32) for item in (w_qkv, q_bias, v_bias, w_out, out_bias, norm1_gain, norm1_shift, w_in, in_bias, w_back, back_bias, norm2_gain, norm2_shift)))
    inputs = tokens.astype(jnp.float32).reshape(SEQS, SEQ, D)
    cotangents = cotangent.astype(jnp.float32).reshape(SEQS, SEQ, D)

    def one_sequence(totals, sample):
        seq_inputs, seq_cot, length, flags = sample

        def local_forward(input_rows, weight_set):
            return forward(input_rows, weight_set, length, flags)
        result, pullback = jax.vjp(local_forward, seq_inputs, weights)
        grad_inputs, grad_weights = pullback(seq_cot)
        new_totals = tuple((total_item + grad_item for total_item, grad_item in zip(totals, grad_weights)))
        return (new_totals, (result, grad_inputs))
    zeros = tuple((jnp.zeros(item.shape, jnp.float32) for item in weights))
    totals, (outputs, grad_inputs) = lax.scan(one_sequence, zeros, (inputs, cotangents, lengths, pair_flip))
    return (outputs.reshape(HALVES, HALF, D).astype(jnp.bfloat16), grad_inputs.reshape(HALVES, HALF, D), totals[0], totals[1], totals[2], totals[3], totals[4], totals[5], totals[6], totals[7], totals[8], totals[9], totals[10], totals[11], totals[12])
```

```python
import functools

import jax
import jax.numpy as jnp
from jax import lax
from jax.experimental import pallas as pl
from jax.experimental.pallas import tpu as pltpu
from jax.sharding import PartitionSpec as P

HEADS = 12
HD = 64
LANES = 128
NEG = -1e30
EPS = 1e-06
SAFE_LOGIT = 60.0
BF16 = jnp.bfloat16
F32 = jnp.float32
NT = (((1,), (1,)), ((), ()))
VMEM_BYTES = 58 << 20


def dot(a, b):
    return jnp.dot(a, b, preferred_element_type=F32)


def dot_nt(a, b):
    return lax.dot_general(a, b, NT, preferred_element_type=F32)


def swap(value, axis, apart):
    pairs = [(source, source ^ apart) for source in range(lax.axis_size(axis))]
    return lax.ppermute(value, axis, pairs)


def place(mine, theirs, upper, axis):
    return jnp.stack([jnp.where(upper, theirs, mine), jnp.where(upper, mine, theirs)], axis=axis)


def gather_blk(pair):
    count = lax.axis_size("blk")
    index = lax.axis_index("blk")
    bits = [1 << b for b in range(count.bit_length() - 1)][::-1]
    held = pair
    depth = 1
    for bit in bits[:-2]:
        held = place(held, swap(held, "blk", bit), (index & bit) != 0, depth)
        depth += 1
    first, second = held[0], held[1]
    depth -= 1
    high, low = bits[-2], bits[-1]
    first_in = swap(first, "blk", high)
    second_in = swap(second, "blk", low)
    first = place(first, first_in, (index & high) != 0, depth)
    second = place(second, second_in, (index & low) != 0, depth)
    first_in = swap(first, "blk", low)
    second_in = swap(second, "blk", high)
    first = place(first, first_in, (index & low) != 0, depth + 1)
    second = place(second, second_in, (index & high) != 0, depth)
    return tuple(a.reshape((count,) + pair.shape[1:]) for a in (first, second))


def first_head(rows):
    lane = lax.broadcasted_iota(jnp.int32, (rows, LANES), 1)
    return lane < HD, lane % HD


def key_rows(own, sub, keys, row, sc, source, heads):
    at = lax.broadcasted_iota(jnp.int32, keys.shape, 0) + row
    bound, local, core = sc[heads + source], sc[heads + 2], sc[heads + 3]
    position = jnp.where(at < local, at + core * local, at - core * local)
    bias = jnp.where(position < bound, 0.0, NEG)
    extra = jnp.where(sub < 3, -1.0, jnp.where(sub == 3, bias, 0.0))
    return jnp.where(own, keys.astype(F32), extra).astype(BF16)


def three_parts(value):
    first = value.astype(BF16).astype(F32)
    rest = value - first
    second = rest.astype(BF16).astype(F32)
    return first, second, rest - second


def attend_kernel(
    sc, q_ref, ka_ref, kb_ref, va_ref, vb_ref, o_ref, lse_ref, keys, values, key_norm, *, heads, step
):
    pair = pl.program_id(0)
    count = keys.shape[1]
    rows = q_ref.shape[1]
    scale = HD ** (-0.5)

    @pl.when(pl.program_id(1) == 0)
    def _():
        piece = min(512, count)
        own0, sub = first_head(piece)
        for h, (k_ref, v_ref) in enumerate(((ka_ref, va_ref), (kb_ref, vb_ref))):
            source = sc[2 * pair + h]
            own = own0 if h == 0 else jnp.logical_not(own0)
            largest = jnp.float32(0.0)
            for r in range(0, count, piece):
                k = k_ref[0, r : r + piece, :]
                keys[h, r : r + piece, :] = key_rows(own, sub, k, r, sc, source, heads)
                values[h, :HD, r : r + piece] = v_ref[0, r : r + piece, :].T[h * HD : (h + 1) * HD, :]
                values[h, HD:, r : r + piece] = jnp.ones((16, piece), BF16)
                k = jnp.where(own, k.astype(F32), 0.0)
                largest = jnp.maximum(largest, jnp.max(jnp.sum(k * k, axis=1, keepdims=True)))
            key_norm[h] = largest

    q = q_ref[0].astype(F32) * scale
    own0, sub = first_head(rows)
    one = jnp.where(sub == 3, 1.0, 0.0)
    square = q * q
    norm_a = jnp.max(jnp.sum(jnp.where(own0, square, 0.0), axis=1, keepdims=True))
    norm_b = jnp.max(jnp.sum(jnp.where(own0, 0.0, square), axis=1, keepdims=True))
    largest = jnp.maximum(norm_a * key_norm[0], norm_b * key_norm[1])
    small = largest < SAFE_LOGIT * SAFE_LOGIT

    def queries(h):
        return (jnp.where(own0, q, one) if h == 0 else jnp.where(own0, one, q)).astype(BF16)

    def finish(outs, peaks):
        totals = [jnp.broadcast_to(o[HD : HD + 1, :], (HD, rows)) for o in outs]
        o_ref[...] = (
            jnp.concatenate([o[:HD, :] / t for o, t in zip(outs, totals)], axis=0).T.astype(BF16)
        )
        lse = jnp.concatenate([jnp.log(totals[1]), jnp.log(totals[0])], axis=0).T
        if peaks is not None:
            lse = lse + jnp.where(own0, peaks[1], peaks[0])
        lse_ref[...] = lse

    @pl.when(small)
    def _():
        outs = []
        for h in (0, 1):
            qa = queries(h)
            out = None
            for c in range(0, count, step):
                p = jnp.exp(dot_nt(qa, keys[h, c : c + step, :])).astype(BF16)
                part = dot_nt(values[h, :, c : c + step], p)
                out = part if out is None else out + part
            outs.append(out)
        finish(outs, None)

    @pl.when(jnp.logical_not(small))
    def _():
        outs, peaks = [], []
        for h in (0, 1):
            s = dot_nt(queries(h), keys[h])
            peak = jnp.max(s, axis=1, keepdims=True)
            outs.append(dot_nt(values[h], jnp.exp(s - peak).astype(BF16)))
            peaks.append(peak)
        finish(outs, peaks)


def pair_specs(count, width):
    pairs = width // LANES

    def key_value(h, base):
        return pl.BlockSpec((1, count, LANES), lambda p, i, sc: (sc[2 * p + h], 0, base * pairs + p))

    return [key_value(0, 1), key_value(1, 1), key_value(0, 2), key_value(1, 2)]


def attend(sc, qkv, width):
    count = qkv.shape[1]
    rows = min(1024, count)
    row_spec = pl.BlockSpec((rows, LANES), lambda p, i, sc: (i, p))
    q_spec = pl.BlockSpec((1, rows, LANES), lambda p, i, sc: (0, i, p))
    heads = width // HD
    return pl.pallas_call(
        functools.partial(attend_kernel, heads=heads, step=min(512, count)),
        grid_spec=pltpu.PrefetchScalarGridSpec(
            num_scalar_prefetch=1,
            grid=(width // LANES, count // rows),
            in_specs=[q_spec] + pair_specs(count, width),
            out_specs=[row_spec, row_spec],
            scratch_shapes=[
                pltpu.VMEM((2, count, LANES), BF16),
                pltpu.VMEM((2, HD + 16, count), BF16),
                pltpu.SMEM((2,), F32),
            ],
        ),
        out_shape=[
            jax.ShapeDtypeStruct((count, width), BF16),
            jax.ShapeDtypeStruct((count, width), F32),
        ],
        compiler_params=pltpu.CompilerParams(vmem_limit_bytes=VMEM_BYTES),
        cost_estimate=pl.CostEstimate(
            flops=4 * 4 * count * count * width,
            bytes_accessed=2 * 6 * count * width,
            transcendentals=heads * count * count,
        ),
        name="attend",
    )(sc, qkv, qkv, qkv, qkv, qkv)


def attend_back_kernel(
    sc,
    q_ref,
    ka_ref,
    kb_ref,
    va_ref,
    vb_ref,
    o_ref,
    lse_ref,
    do_ref,
    dq_ref,
    dk_ref,
    dv_ref,
    keys,
    values,
    dk_sum,
    dv_sum,
    *,
    heads,
    step,
):
    pair = pl.program_id(0)
    block = pl.program_id(1)
    count = keys.shape[1]
    rows = q_ref.shape[1]
    scale = HD ** (-0.5)

    @pl.when(block == 0)
    def _():
        piece = min(512, count)
        own0, sub = first_head(piece)
        for h, (k_ref, v_ref) in enumerate(((ka_ref, va_ref), (kb_ref, vb_ref))):
            source = sc[2 * pair + h]
            own = own0 if h == 0 else jnp.logical_not(own0)
            for r in range(0, count, piece):
                k = k_ref[0, r : r + piece, :]
                keys[h, r : r + piece, :] = key_rows(own, sub, k, r, sc, source, heads)
                v = v_ref[0, r : r + piece, :].astype(F32)
                values[h, r : r + piece, :] = jnp.where(own, v, 1.0).astype(BF16)
        dk_sum[...] = jnp.zeros_like(dk_sum)
        dv_sum[...] = jnp.zeros_like(dv_sum)

    q = q_ref[0]
    do = do_ref[...]
    own0, sub = first_head(rows)
    qf = q.astype(F32) * scale
    first, second, third = three_parts(lse_ref[...])
    q_extra = jnp.where(
        sub == 0, first, jnp.where(sub == 1, second, jnp.where(sub == 2, third, jnp.where(sub == 3, 1.0, 0.0)))
    )
    dof = do.astype(F32)
    product = dof * o_ref[...].astype(F32)
    inner_a = jnp.sum(jnp.where(own0, product, 0.0), axis=1, keepdims=True)
    inner_b = jnp.sum(jnp.where(own0, 0.0, product), axis=1, keepdims=True)
    first, second, third = three_parts(jnp.where(own0, -inner_b, -inner_a))
    do_extra = jnp.where(sub == 0, first, jnp.where(sub == 1, second, jnp.where(sub == 2, third, 0.0)))
    q_t = q.T
    do_t = do.T
    grads = []
    for h in (0, 1):
        qa = (jnp.where(own0, qf, q_extra) if h == 0 else jnp.where(own0, q_extra, qf)).astype(BF16)
        da = (jnp.where(own0, dof, do_extra) if h == 0 else jnp.where(own0, do_extra, dof)).astype(BF16)
        own_rows = slice(h * HD, (h + 1) * HD)
        dq = None
        for c in range(0, count, step):
            part = slice(c, c + step)
            p = jnp.exp(dot_nt(qa, keys[h, part, :]))
            ds = (p * dot_nt(da, values[h, part, :])).astype(BF16)
            p = p.astype(BF16)
            t = dot(ds, keys[h, part, :])
            dq = t if dq is None else dq + t
            dk_sum[own_rows, part] += dot(q_t[own_rows, :], ds)
            dv_sum[own_rows, part] += dot(do_t[own_rows, :], p)
        grads.append(dq)
    dq_ref[...] = (jnp.where(own0, grads[0], grads[1]) * scale).astype(BF16)

    @pl.when(block == pl.num_programs(1) - 1)
    def _():
        for h in (0, 1):
            source = sc[2 * pair + h]
            own_rows = slice(h * HD, (h + 1) * HD)
            dk = dk_sum[own_rows, :] * scale
            dv = dv_sum[own_rows, :]
            for half in (0, 1):
                here = source == half
                dk_ref[half, own_rows, :] = jnp.where(here, dk, 0.0).astype(BF16)
                dv_ref[half, own_rows, :] = jnp.where(here, dv, 0.0).astype(BF16)


def attend_back(sc, qkv, context, lse, grad_context, width):
    count = qkv.shape[1]
    rows = min(1024, count)
    row_spec = pl.BlockSpec((rows, LANES), lambda p, i, sc: (i, p))
    q_spec = pl.BlockSpec((1, rows, LANES), lambda p, i, sc: (0, i, p))
    grad_spec = pl.BlockSpec((2, LANES, count), lambda p, i, sc: (0, p, 0))
    heads = width // HD
    return pl.pallas_call(
        functools.partial(attend_back_kernel, heads=heads, step=min(512, count)),
        grid_spec=pltpu.PrefetchScalarGridSpec(
            num_scalar_prefetch=1,
            grid=(width // LANES, count // rows),
            in_specs=[q_spec] + pair_specs(count, width) + [row_spec, row_spec, row_spec],
            out_specs=[row_spec, grad_spec, grad_spec],
            scratch_shapes=[
                pltpu.VMEM((2, count, LANES), BF16),
                pltpu.VMEM((2, count, LANES), BF16),
                pltpu.VMEM((LANES, count), F32),
                pltpu.VMEM((LANES, count), F32),
            ],
        ),
        out_shape=[
            jax.ShapeDtypeStruct((count, width), BF16),
            jax.ShapeDtypeStruct((2, width, count), BF16),
            jax.ShapeDtypeStruct((2, width, count), BF16),
        ],
        compiler_params=pltpu.CompilerParams(vmem_limit_bytes=VMEM_BYTES),
        cost_estimate=pl.CostEstimate(
            flops=10 * 4 * count * count * width,
            bytes_accessed=2 * 12 * count * width,
            transcendentals=heads * count * count,
        ),
        name="attend_back",
    )(sc, qkv, qkv, qkv, qkv, qkv, context, lse, grad_context)


def mean_of(value):
    return jnp.mean(value, axis=-1, keepdims=True)


def norm_of(value):
    center = value - mean_of(value)
    inverse = lax.rsqrt(mean_of(center * center) + EPS)
    return center * inverse, inverse


def norm_back(grad, normed, inverse, gain):
    dn = grad * gain
    return inverse * (dn - mean_of(dn) - normed * mean_of(dn * normed))


def sum_rows(value):
    return jnp.sum(value, axis=0, keepdims=True)


def middle_kernel(
    core,
    x_ref,
    own_ref,
    other_ref,
    cot_ref,
    wo_own,
    wo_other,
    w_in,
    w_back,
    vec,
    out_ref,
    resid_ref,
    gc_own,
    gc_other,
    low_ref,
    act_ref,
    gh_ref,
    gb_ref,
    attn_ref,
    sums,
    slope,
    *,
    width,
    ff,
):
    chunk = width
    in_bias = lambda c: vec[0:1, c : c + chunk]
    row = lambda r, s: vec[r : r + 1, s * width : (s + 1) * width]
    out_bias, back_bias, gain1, shift1 = (row(1, s) for s in range(4))
    gain2, shift2 = row(2, 0), row(2, 1)

    @pl.when(pl.program_id(0) == 0)
    def _():
        sums[...] = jnp.zeros_like(sums)

    attended = dot(own_ref[...], wo_own[...]) + dot(other_ref[...], wo_other[...]) + out_bias
    hat1, inverse1 = norm_of(x_ref[...].astype(F32) + attended)
    normed = hat1 * gain1 + shift1
    low = normed.astype(BF16)
    low_ref[...] = low
    branch = None
    for c in range(0, ff, chunk):
        hidden = dot(low, w_in[:, c : c + chunk]) + in_bias(c)
        cumulative = 0.5 * (1.0 + lax.erf(hidden * 0.7071067811865476))
        density = 0.3989422804014327 * jnp.exp(-0.5 * hidden * hidden)
        slope[:, c : c + chunk] = cumulative + hidden * density
        act = (hidden * cumulative).astype(BF16)
        act_ref[:, c : c + chunk] = act
        part = dot(act, w_back[c : c + chunk, :])
        branch = part if branch is None else branch + part
    hat2, inverse2 = norm_of(normed + (branch + back_bias))
    out_ref[...] = (hat2 * gain2 + shift2).astype(BF16)
    cot = cot_ref[...].astype(F32)
    grad2 = norm_back(cot, hat2, inverse2, gain2)
    gb = grad2.astype(BF16)
    gb_ref[...] = gb
    grad_normed = grad2
    for c in range(0, ff, chunk):
        gh = (dot_nt(gb, w_back[c : c + chunk, :]) * slope[:, c : c + chunk]).astype(BF16)
        gh_ref[:, c : c + chunk] = gh
        sums[0:1, c : c + chunk] += sum_rows(gh.astype(F32))
        grad_normed = grad_normed + dot_nt(gh, w_in[:, c : c + chunk])
    grad1 = norm_back(grad_normed, hat1, inverse1, gain1)
    resid_ref[...] = grad1
    attn = grad1.astype(BF16)
    attn_ref[...] = attn
    gc_own[...] = dot_nt(attn, wo_own[...]).astype(BF16)
    gc_other[...] = dot_nt(attn, wo_other[...]).astype(BF16)
    at = lambda r, s, v: sums.__setitem__(
        (slice(r, r + 1), slice(s * width, (s + 1) * width)),
        sums[r : r + 1, s * width : (s + 1) * width] + sum_rows(v),
    )
    at(1, 0, attn.astype(F32))
    at(1, 1, gb.astype(F32))
    at(1, 2, grad_normed * hat1)
    at(1, 3, grad_normed)
    at(2, 0, cot * hat2)
    at(2, 1, cot)


def middle(core, x, own, other, cot, w_out, w_in, w_back, vec):
    count, width = x.shape
    ff = w_in.shape[1]
    half = own.shape[1]
    rows = min(256, count)
    tile = lambda w: pl.BlockSpec((rows, w), lambda i, core: (i, 0))
    once = pl.Buffered(1)
    whole = lambda a: pl.BlockSpec(a.shape, lambda i, core: (0, 0), pipeline_mode=once)
    return pl.pallas_call(
        functools.partial(middle_kernel, width=width, ff=ff),
        grid_spec=pltpu.PrefetchScalarGridSpec(
            num_scalar_prefetch=1,
            grid=(count // rows,),
            in_specs=[
                tile(width),
                tile(half),
                tile(half),
                tile(width),
                pl.BlockSpec((half, width), lambda i, core: (core[0], 0), pipeline_mode=once),
                pl.BlockSpec((half, width), lambda i, core: (1 - core[0], 0), pipeline_mode=once),
                whole(w_in),
                whole(w_back),
                whole(vec),
            ],
            out_specs=[
                tile(width),
                tile(width),
                tile(half),
                tile(half),
                tile(width),
                tile(ff),
                tile(ff),
                tile(width),
                tile(width),
                pl.BlockSpec((8, ff), lambda i, core: (0, 0)),
            ],
            scratch_shapes=[pltpu.VMEM((rows, ff), F32)],
        ),
        out_shape=[
            jax.ShapeDtypeStruct((count, width), BF16),
            jax.ShapeDtypeStruct((count, width), F32),
            jax.ShapeDtypeStruct((count, half), BF16),
            jax.ShapeDtypeStruct((count, half), BF16),
            jax.ShapeDtypeStruct((count, width), BF16),
            jax.ShapeDtypeStruct((count, ff), BF16),
            jax.ShapeDtypeStruct((count, ff), BF16),
            jax.ShapeDtypeStruct((count, width), BF16),
            jax.ShapeDtypeStruct((count, width), BF16),
            jax.ShapeDtypeStruct((8, ff), F32),
        ],
        compiler_params=pltpu.CompilerParams(vmem_limit_bytes=VMEM_BYTES),
        cost_estimate=pl.CostEstimate(
            flops=2 * count * width * (4 * ff + 2 * width),
            bytes_accessed=2 * (4 * width * ff + 2 * count * ff + 8 * count * width),
            transcendentals=2 * count * ff,
        ),
        name="middle",
    )(core, x, own, other, cot, w_out, w_out, w_in, w_back, vec)


def dot_tn(a, b):
    return lax.dot_general(a, b, (((0,), (0,)), ((), ())), preferred_element_type=F32)


def per_device(
    tokens,
    lengths,
    pair_flip,
    w_qkv,
    q_bias,
    v_bias,
    w_out,
    out_bias,
    norm1_gain,
    norm1_shift,
    w_in,
    in_bias,
    w_back,
    back_bias,
    norm2_gain,
    norm2_shift,
    cotangent,
):
    both = ("head", "blk")
    cores = lax.axis_size("head")
    blocks = lax.axis_size("blk")
    core = lax.axis_index("head")
    block = lax.axis_index("blk")
    local, width = tokens.shape[1:]
    half = local * cores
    heads = HEADS // cores
    group = heads * HD
    ff = w_in.shape[1]
    parts = ff // width
    rows = w_qkv.shape[0]
    x = tokens[0]

    shard = jnp.concatenate(
        [w_in, w_back.reshape(parts, rows, width).transpose(1, 0, 2).reshape(rows, ff), w_out], axis=1
    )
    gathered = lax.all_gather(shard, both, axis=0, tiled=True)
    full_in = gathered[:, :ff]
    full_back = (
        gathered[:, ff : 2 * ff]
        .reshape(cores * blocks, rows, parts, width)
        .transpose(0, 2, 1, 3)
        .reshape(ff, width)
    )
    full_out = gathered[:, 2 * ff :]

    x_sib = swap(x, "head", 1)
    x_far = swap(x, "blk", 1)
    vectors = jnp.concatenate(
        [q_bias, v_bias, out_bias, back_bias, norm1_gain, norm1_shift, norm2_gain, norm2_shift, in_bias]
    )
    vectors = jnp.pad(vectors, (0, 3 * group - vectors.shape[0]))
    extra = jnp.pad(vectors[None], ((0, 7), (0, 0)))
    columns = w_qkv.reshape(rows, 3, cores, group)
    kept = lax.dynamic_index_in_dim(columns, core, 2, keepdims=False).reshape(rows, 3 * group)
    given = lax.dynamic_index_in_dim(columns, 1 - core, 2, keepdims=False).reshape(rows, 3 * group)
    mine = jnp.concatenate([kept, extra], axis=0)
    theirs = swap(jnp.concatenate([given, extra], axis=0), "head", 1)
    first, second = gather_blk(place(mine, theirs, core == 1, 0))
    x_far_sib = swap(x_far, "head", 1)
    weight = jnp.concatenate([first[:, :rows], second[:, :rows]], axis=0).reshape(width, 3 * group)
    small = jnp.concatenate([first[:, rows], second[:, rows]], axis=0)

    def vector(slot, size=rows):
        return small[:, slot * rows : slot * rows + size].reshape(-1).astype(F32)

    bias = jnp.concatenate(
        [
            lax.dynamic_slice_in_dim(vector(0), core * group, group),
            jnp.zeros((group,), F32),
            lax.dynamic_slice_in_dim(vector(1), core * group, group),
        ]
    )
    vec = jnp.concatenate(
        [
            vector(8, parts * rows)[None],
            jnp.pad(jnp.concatenate([vector(2), vector(3), vector(4), vector(5)]), (0, ff - 4 * width))[None],
            jnp.pad(jnp.concatenate([vector(6), vector(7)]), (0, ff - 2 * width))[None],
            jnp.zeros((5, ff), F32),
        ],
        axis=0,
    )

    xs = jnp.concatenate([x, x_sib, x_far, x_far_sib], axis=0)
    qkv = (dot(xs, weight) + bias).astype(BF16).reshape(2, half, 3 * group)

    sequence = block // 2
    own_half = block % 2
    length = lax.dynamic_index_in_dim(lengths, sequence, 0, keepdims=False)
    flags = lax.dynamic_index_in_dim(pair_flip, sequence, 0, keepdims=False)
    flags = lax.dynamic_slice_in_dim(flags, core * heads, heads)
    bounds = [jnp.clip(length - h * half, 0, half) for h in (own_half, 1 - own_half)]
    sc = jnp.concatenate([flags, jnp.stack(bounds + [jnp.int32(local), core])]).astype(jnp.int32)

    context, lse = attend(sc, qkv, group)
    other = swap(context[local:], "head", 1)
    out, grad_resid1, gc_own, gc_other, low, act, gh, gb, attn, sums = middle(
        core.reshape(1).astype(jnp.int32),
        x,
        context[:local],
        other,
        cotangent[0],
        full_out,
        full_in,
        full_back,
        vec,
    )
    grad_context = jnp.concatenate([gc_own, swap(gc_other, "head", 1)], axis=0)

    context_rows = place(context[:local], other, core == 1, 1).reshape(local, width)
    grad_in = dot_tn(low, gh).astype(BF16)
    grad_back = dot_tn(act, gb).astype(BF16)
    grad_out = dot_tn(context_rows, attn).astype(BF16)
    packed = jnp.concatenate(
        [
            grad_in,
            grad_back.reshape(cores * blocks, parts, rows, width).transpose(0, 2, 1, 3).reshape(width, ff),
            grad_out,
        ],
        axis=1,
    )
    reduced = lax.psum_scatter(packed, both, scatter_dimension=0, tiled=True)
    sum_win = reduced[:, :ff].astype(F32)
    sum_wback = (
        reduced[:, ff : 2 * ff].reshape(rows, parts, width).transpose(1, 0, 2).reshape(parts * rows, width)
    ).astype(F32)
    sum_wout = reduced[:, 2 * ff :].astype(F32)

    dq, dk, dv = attend_back(sc, qkv, context, lse, grad_context, group)
    wq, wk, wv = weight[:, :group], weight[:, group : 2 * group], weight[:, 2 * group :]

    def back_rows(which):
        return lax.dot_general(dk[which], wk, (((0,), (1,)), ((), ())), preferred_element_type=F32) + (
            lax.dot_general(dv[which], wv, (((0,), (1,)), ((), ())), preferred_element_type=F32)
        )

    dx_far = back_rows(1)
    dx_near = back_rows(0) + dot_nt(dq, wq)
    far_sib = swap(dx_far[local:].astype(BF16), "head", 1)
    far_in = swap((dx_far[:local] + far_sib.astype(F32)).astype(BF16), "blk", 1)
    near_sib = swap(dx_near[local:].astype(BF16), "head", 1)
    grad_tokens = grad_resid1 + dx_near[:local] + near_sib.astype(F32) + far_in.astype(F32)

    both_halves = xs.reshape(2, half, width)
    over = (((0, 1), (0, 2)), ((), ()))
    grad_w = jnp.concatenate(
        [
            dot_tn(both_halves[0], dq),
            lax.dot_general(both_halves, dk, over, preferred_element_type=F32),
            lax.dot_general(both_halves, dv, over, preferred_element_type=F32),
        ],
        axis=1,
    ).astype(BF16)
    at_group = lambda v: lax.dynamic_update_slice_in_dim(jnp.zeros((width,), F32), v, core * group, 0)
    grad_small = [
        at_group(jnp.sum(dq.astype(F32), axis=0)),
        at_group(jnp.sum(dv.astype(F32), axis=(0, 2))),
        sums[1, :width],
        sums[1, width : 2 * width],
        sums[1, 2 * width : 3 * width],
        sums[1, 3 * width : 4 * width],
        sums[2, :width],
        sums[2, width : 2 * width],
    ]
    grad_small = jnp.concatenate(
        [jnp.stack(grad_small, 0).reshape(8, cores, blocks, rows).transpose(1, 2, 0, 3).reshape(cores, blocks, -1)]
        + [sums[0].reshape(cores, blocks, parts * rows)],
        axis=2,
    )
    small_size = grad_small.shape[2]
    grad_small = jnp.pad(grad_small, ((0, 0), (0, 0), (0, 3 * group - small_size)))
    high = grad_small.astype(BF16)
    low_part = (grad_small - high.astype(F32)).astype(BF16)
    small_rows = jnp.pad(jnp.stack([high, low_part], axis=2), ((0, 0), (0, 0), (0, 6), (0, 0)))
    outgoing = jnp.concatenate([grad_w.reshape(cores, blocks, rows, 3 * group), small_rows], axis=2)
    keep = lax.dynamic_index_in_dim(outgoing, core, 0, keepdims=False)
    send = lax.dynamic_index_in_dim(outgoing, 1 - core, 0, keepdims=False)
    came = swap(send, "head", 1)
    exchanged = lax.all_to_all(jnp.stack([keep, came], axis=1), "blk", 0, 0, tiled=True).astype(F32)
    total = jnp.sum(exchanged, axis=0)
    own_w, other_w = (total[s, :rows].reshape(rows, 3, group) for s in (0, 1))
    sum_wqkv = place(own_w, other_w, core == 1, 2).reshape(rows, 3 * width)
    vectors = total[0, rows] + total[0, rows + 1] + total[1, rows] + total[1, rows + 1]

    def summed(slot, size=rows):
        return vectors[slot * rows : slot * rows + size]

    return (
        out[None],
        grad_tokens[None],
        sum_wqkv,
        summed(0),
        summed(1),
        sum_wout,
        summed(2),
        summed(4),
        summed(5),
        sum_win,
        summed(8, parts * rows),
        sum_wback,
        summed(3),
        summed(6),
        summed(7),
    )


def solution(mesh):
    split = P(("head", "blk"))
    matrix = P(("head", "blk"), None)
    rows = P("blk", "head", None)
    return jax.shard_map(
        per_device,
        mesh=mesh,
        in_specs=(
            rows,
            P(),
            P(),
            matrix,
            split,
            split,
            matrix,
            split,
            split,
            split,
            matrix,
            split,
            matrix,
            split,
            split,
            split,
            rows,
        ),
        out_specs=(
            rows,
            rows,
            matrix,
            split,
            split,
            matrix,
            split,
            split,
            split,
            matrix,
            split,
            matrix,
            split,
            split,
            split,
        ),
        check_vma=False,
    )
```

```python
import functools

import jax
import jax.numpy as jnp
from jax import lax
from jax.experimental import pallas as pl
from jax.experimental.pallas import tpu as pltpu
from jax.sharding import PartitionSpec as P

HEADS = 12
HD = 64
LANES = 128
NEG = -1e30
EPS = 1e-06
SAFE_LOGIT = 60.0
BF16 = jnp.bfloat16
F32 = jnp.float32
NT = (((1,), (1,)), ((), ()))
VMEM_BYTES = 58 << 20


def dot(a, b):
    return jnp.dot(a, b, preferred_element_type=F32)


def dot_nt(a, b):
    return lax.dot_general(a, b, NT, preferred_element_type=F32)


def swap(value, axis, apart):
    pairs = [(source, source ^ apart) for source in range(lax.axis_size(axis))]
    return lax.ppermute(value, axis, pairs)


def place(mine, theirs, upper, axis):
    return jnp.stack([jnp.where(upper, theirs, mine), jnp.where(upper, mine, theirs)], axis=axis)


def gather_blk(pair, also):
    count = lax.axis_size("blk")
    index = lax.axis_index("blk")
    bits = [1 << b for b in range(count.bit_length() - 1)][::-1]
    held = pair
    depth = 1
    for bit in bits[:-2]:
        held = place(held, swap(held, "blk", bit), (index & bit) != 0, depth)
        depth += 1
    if GATE >= 4:
        held, also = lax.optimization_barrier((held, also))
    first, second = held[0], held[1]
    depth -= 1
    high, low = bits[-2], bits[-1]
    first_in = swap(first, "blk", high)
    second_in = swap(second, "blk", low)
    first = place(first, first_in, (index & high) != 0, depth)
    second = place(second, second_in, (index & low) != 0, depth)
    first_in = swap(first, "blk", low)
    second_in = swap(second, "blk", high)
    first = place(first, first_in, (index & low) != 0, depth + 1)
    second = place(second, second_in, (index & high) != 0, depth)
    return tuple(a.reshape((count,) + pair.shape[1:]) for a in (first, second)) + (also,)


def first_head(rows):
    lane = lax.broadcasted_iota(jnp.int32, (rows, LANES), 1)
    return lane < HD, lane % HD


def key_rows(own, sub, keys, row, sc, source, heads):
    at = lax.broadcasted_iota(jnp.int32, keys.shape, 0) + row
    bound, local, core = sc[heads + source], sc[heads + 2], sc[heads + 3]
    position = jnp.where(at < local, at + core * local, at - core * local)
    bias = jnp.where(position < bound, 0.0, NEG)
    extra = jnp.where(sub < 3, -1.0, jnp.where(sub == 3, bias, 0.0))
    return jnp.where(own, keys.astype(F32), extra).astype(BF16)


def three_parts(value):
    first = value.astype(BF16).astype(F32)
    rest = value - first
    second = rest.astype(BF16).astype(F32)
    return first, second, rest - second


def attend_kernel(
    sc, q_ref, ka_ref, kb_ref, va_ref, vb_ref, o_ref, lse_ref, keys, values, key_norm, *, heads, step
):
    pair = pl.program_id(0)
    count = keys.shape[1]
    rows = q_ref.shape[1]
    scale = HD ** (-0.5)

    @pl.when(pl.program_id(1) == 0)
    def _():
        piece = min(512, count)
        own0, sub = first_head(piece)
        for h, (k_ref, v_ref) in enumerate(((ka_ref, va_ref), (kb_ref, vb_ref))):
            source = sc[2 * pair + h]
            own = own0 if h == 0 else jnp.logical_not(own0)
            largest = jnp.float32(0.0)
            for r in range(0, count, piece):
                k = k_ref[0, r : r + piece, :]
                keys[h, r : r + piece, :] = key_rows(own, sub, k, r, sc, source, heads)
                values[h, :HD, r : r + piece] = v_ref[0, r : r + piece, :].T[h * HD : (h + 1) * HD, :]
                values[h, HD:, r : r + piece] = jnp.ones((16, piece), BF16)
                k = jnp.where(own, k.astype(F32), 0.0)
                largest = jnp.maximum(largest, jnp.max(jnp.sum(k * k, axis=1, keepdims=True)))
            key_norm[h] = largest

    q = q_ref[0].astype(F32) * scale
    own0, sub = first_head(rows)
    one = jnp.where(sub == 3, 1.0, 0.0)
    square = q * q
    norm_a = jnp.max(jnp.sum(jnp.where(own0, square, 0.0), axis=1, keepdims=True))
    norm_b = jnp.max(jnp.sum(jnp.where(own0, 0.0, square), axis=1, keepdims=True))
    largest = jnp.maximum(norm_a * key_norm[0], norm_b * key_norm[1])
    small = largest < SAFE_LOGIT * SAFE_LOGIT

    def queries(h):
        return (jnp.where(own0, q, one) if h == 0 else jnp.where(own0, one, q)).astype(BF16)

    def finish(outs, peaks):
        totals = [jnp.broadcast_to(o[HD : HD + 1, :], (HD, rows)) for o in outs]
        o_ref[...] = (
            jnp.concatenate([o[:HD, :] / t for o, t in zip(outs, totals)], axis=0).T.astype(BF16)
        )
        lse = jnp.concatenate([jnp.log(totals[1]), jnp.log(totals[0])], axis=0).T
        if peaks is not None:
            lse = lse + jnp.where(own0, peaks[1], peaks[0])
        lse_ref[...] = lse

    @pl.when(small)
    def _():
        outs = []
        for h in (0, 1):
            qa = queries(h)
            out = None
            for c in range(0, count, step):
                p = jnp.exp(dot_nt(qa, keys[h, c : c + step, :])).astype(BF16)
                part = dot_nt(values[h, :, c : c + step], p)
                out = part if out is None else out + part
            outs.append(out)
        finish(outs, None)

    @pl.when(jnp.logical_not(small))
    def _():
        outs, peaks = [], []
        for h in (0, 1):
            s = dot_nt(queries(h), keys[h])
            peak = jnp.max(s, axis=1, keepdims=True)
            outs.append(dot_nt(values[h], jnp.exp(s - peak).astype(BF16)))
            peaks.append(peak)
        finish(outs, peaks)


def pair_specs(count, width):
    pairs = width // LANES

    def key_value(h, base):
        return pl.BlockSpec((1, count, LANES), lambda p, i, sc: (sc[2 * p + h], 0, base * pairs + p))

    return [key_value(0, 1), key_value(1, 1), key_value(0, 2), key_value(1, 2)]


def attend(sc, qkv, width):
    count = qkv.shape[1]
    rows = min(1024, count)
    row_spec = pl.BlockSpec((rows, LANES), lambda p, i, sc: (i, p))
    q_spec = pl.BlockSpec((1, rows, LANES), lambda p, i, sc: (0, i, p))
    heads = width // HD
    return pl.pallas_call(
        functools.partial(attend_kernel, heads=heads, step=min(512, count)),
        grid_spec=pltpu.PrefetchScalarGridSpec(
            num_scalar_prefetch=1,
            grid=(width // LANES, count // rows),
            in_specs=[q_spec] + pair_specs(count, width),
            out_specs=[row_spec, row_spec],
            scratch_shapes=[
                pltpu.VMEM((2, count, LANES), BF16),
                pltpu.VMEM((2, HD + 16, count), BF16),
                pltpu.SMEM((2,), F32),
            ],
        ),
        out_shape=[
            jax.ShapeDtypeStruct((count, width), BF16),
            jax.ShapeDtypeStruct((count, width), F32),
        ],
        compiler_params=pltpu.CompilerParams(vmem_limit_bytes=VMEM_BYTES),
        cost_estimate=pl.CostEstimate(
            flops=4 * 4 * count * count * width,
            bytes_accessed=2 * 6 * count * width,
            transcendentals=heads * count * count,
        ),
        name="attend",
    )(sc, qkv, qkv, qkv, qkv, qkv)


def attend_back_kernel(
    sc,
    q_ref,
    ka_ref,
    kb_ref,
    va_ref,
    vb_ref,
    o_ref,
    lse_ref,
    do_ref,
    dq_ref,
    dkv_ref,
    sum_ref,
    keys,
    keys_t,
    values,
    dk_sum,
    dv_sum,
    *,
    heads,
    step,
):
    pair = pl.program_id(0)
    block = pl.program_id(1)
    count = keys.shape[1]
    rows = q_ref.shape[1]
    scale = HD ** (-0.5)

    @pl.when(block == 0)
    def _():
        piece = min(512, count)
        own0, sub = first_head(piece)
        for h, (k_ref, v_ref) in enumerate(((ka_ref, va_ref), (kb_ref, vb_ref))):
            source = sc[2 * pair + h]
            own = own0 if h == 0 else jnp.logical_not(own0)
            for r in range(0, count, piece):
                k = k_ref[0, r : r + piece, :]
                keys[h, r : r + piece, :] = key_rows(own, sub, k, r, sc, source, heads)
                keys_t[h, :, r : r + piece] = k.T[h * HD : (h + 1) * HD, :]
                v = v_ref[0, r : r + piece, :].astype(F32)
                values[h, r : r + piece, :] = jnp.where(own, v, 1.0).astype(BF16)
        sum_ref[...] = jnp.zeros_like(sum_ref)
        dk_sum[...] = jnp.zeros_like(dk_sum)
        dv_sum[...] = jnp.zeros_like(dv_sum)

    q = q_ref[0]
    do = do_ref[...]
    own0, sub = first_head(rows)
    qf = q.astype(F32) * scale
    first, second, third = three_parts(lse_ref[...])
    q_extra = jnp.where(
        sub == 0, first, jnp.where(sub == 1, second, jnp.where(sub == 2, third, jnp.where(sub == 3, 1.0, 0.0)))
    )
    dof = do.astype(F32)
    product = dof * o_ref[...].astype(F32)
    inner_a = jnp.sum(jnp.where(own0, product, 0.0), axis=1, keepdims=True)
    inner_b = jnp.sum(jnp.where(own0, 0.0, product), axis=1, keepdims=True)
    first, second, third = three_parts(jnp.where(own0, -inner_b, -inner_a))
    do_extra = jnp.where(sub == 0, first, jnp.where(sub == 1, second, jnp.where(sub == 2, third, 0.0)))
    q_t = q.T
    do_t = do.T
    grads = []
    for h in (0, 1):
        qa = (jnp.where(own0, qf, q_extra) if h == 0 else jnp.where(own0, q_extra, qf)).astype(BF16)
        da = (jnp.where(own0, dof, do_extra) if h == 0 else jnp.where(own0, do_extra, dof)).astype(BF16)
        own_rows = slice(h * HD, (h + 1) * HD)
        dq = None
        for c in range(0, count, step):
            part = slice(c, c + step)
            p = jnp.exp(dot_nt(qa, keys[h, part, :]))
            ds = (p * dot_nt(da, values[h, part, :])).astype(BF16)
            p = p.astype(BF16)
            t = dot_nt(keys_t[h, :, part], ds)
            dq = t if dq is None else dq + t
            dk_sum[own_rows, part] += dot(q_t[own_rows, :], ds)
            dv_sum[own_rows, part] += dot(do_t[own_rows, :], p)
        grads.append(dq)
    dq = (jnp.concatenate(grads, axis=0) * scale).astype(BF16)
    dq_ref[...] = dq
    for c in range(0, rows, LANES):
        sum_ref[...] += dq[:, c : c + LANES].astype(F32)

    @pl.when(block == pl.num_programs(1) - 1)
    def _():
        for h in (0, 1):
            source = sc[2 * pair + h]
            own_rows = slice(h * HD, (h + 1) * HD)
            dk = dk_sum[own_rows, :] * scale
            dv = dv_sum[own_rows, :]
            for half in (0, 1):
                here = source == half
                dkv_ref[half, 0, own_rows, :] = jnp.where(here, dk, 0.0).astype(BF16)
                dkv_ref[half, 1, own_rows, :] = jnp.where(here, dv, 0.0).astype(BF16)


def attend_back(sc, qkv, context, lse, grad_context, width):
    count = qkv.shape[1]
    rows = min(1024, count)
    row_spec = pl.BlockSpec((rows, LANES), lambda p, i, sc: (i, p))
    q_spec = pl.BlockSpec((1, rows, LANES), lambda p, i, sc: (0, i, p))
    dq_spec = pl.BlockSpec((LANES, rows), lambda p, i, sc: (p, i))
    dkv_spec = pl.BlockSpec((2, 2, LANES, count), lambda p, i, sc: (0, 0, p, 0))
    heads = width // HD
    return pl.pallas_call(
        functools.partial(attend_back_kernel, heads=heads, step=min(512, count)),
        grid_spec=pltpu.PrefetchScalarGridSpec(
            num_scalar_prefetch=1,
            grid=(width // LANES, count // rows),
            in_specs=[q_spec] + pair_specs(count, width) + [row_spec, row_spec, row_spec],
            out_specs=[dq_spec, dkv_spec, pl.BlockSpec((LANES, LANES), lambda p, i, sc: (p, 0))],
            scratch_shapes=[
                pltpu.VMEM((2, count, LANES), BF16),
                pltpu.VMEM((2, HD, count), BF16),
                pltpu.VMEM((2, count, LANES), BF16),
                pltpu.VMEM((LANES, count), F32),
                pltpu.VMEM((LANES, count), F32),
            ],
        ),
        out_shape=[
            jax.ShapeDtypeStruct((width, count), BF16),
            jax.ShapeDtypeStruct((2, 2, width, count), BF16),
            jax.ShapeDtypeStruct((width, LANES), F32),
        ],
        compiler_params=pltpu.CompilerParams(vmem_limit_bytes=VMEM_BYTES),
        cost_estimate=pl.CostEstimate(
            flops=10 * 4 * count * count * width,
            bytes_accessed=2 * 12 * count * width,
            transcendentals=heads * count * count,
        ),
        name="attend_back",
    )(sc, qkv, qkv, qkv, qkv, qkv, context, lse, grad_context)


def mean_of(value):
    return jnp.mean(value, axis=-1, keepdims=True)


def norm_of(value):
    center = value - mean_of(value)
    inverse = lax.rsqrt(mean_of(center * center) + EPS)
    return center * inverse, inverse


def norm_back(grad, normed, inverse, gain):
    dn = grad * gain
    return inverse * (dn - mean_of(dn) - normed * mean_of(dn * normed))


def sum_rows(value):
    return jnp.sum(value, axis=0, keepdims=True)


def middle_kernel(
    core,
    x_ref,
    own_ref,
    other_ref,
    cot_ref,
    wo_own_ref,
    wo_other_ref,
    *refs,
    width,
    ff,
):
    chunk = width
    parts = ff // width
    w_in_refs = refs[:parts]
    (
        w_back_ref,
        vec,
        out_ref,
        resid_ref,
        gc_own,
        gc_other,
        low_ref,
        act_ref,
        gh_ref,
        gb_ref,
        attn_ref,
        sums,
        slope,
        wo_own,
        wo_other,
        w_in,
        w_back,
    ) = refs[parts:]
    in_bias = lambda c: vec[0:1, c : c + chunk]
    row = lambda r, s: vec[r : r + 1, s * width : (s + 1) * width]
    out_bias, back_bias, gain1, shift1 = (row(1, s) for s in range(4))
    gain2, shift2 = row(2, 0), row(2, 1)

    @pl.when(pl.program_id(0) == 0)
    def _():
        sums[...] = jnp.zeros_like(sums)
        wo_own[...] = wo_own_ref[...].reshape(wo_own.shape)
        wo_other[...] = wo_other_ref[...].reshape(wo_other.shape)
        for j in range(parts):
            w_in[j] = w_in_refs[j][...].reshape(w_in.shape[1:])
        devices, rows = w_back_ref.shape[:2]
        some = devices // parts
        for j in range(parts):
            w_back[j] = w_back_ref[j * some : (j + 1) * some].reshape(some * rows, width)

    attended = dot(own_ref[...], wo_own[...]) + dot(other_ref[...], wo_other[...]) + out_bias
    hat1, inverse1 = norm_of(x_ref[...].astype(F32) + attended)
    normed = hat1 * gain1 + shift1
    low = normed.astype(BF16)
    low_ref[...] = low
    branch = None
    for c in range(0, ff, chunk):
        hidden = dot(low, w_in[c // chunk]) + in_bias(c)
        cumulative = 0.5 * (1.0 + lax.erf(hidden * 0.7071067811865476))
        density = 0.3989422804014327 * jnp.exp(-0.5 * hidden * hidden)
        slope[:, c : c + chunk] = cumulative + hidden * density
        act = (hidden * cumulative).astype(BF16)
        act_ref[:, c : c + chunk] = act
        part = dot(act, w_back[c // chunk])
        branch = part if branch is None else branch + part
    hat2, inverse2 = norm_of(normed + (branch + back_bias))
    out_ref[...] = (hat2 * gain2 + shift2).astype(BF16)
    cot = cot_ref[...].astype(F32)
    grad2 = norm_back(cot, hat2, inverse2, gain2)
    gb = grad2.astype(BF16)
    gb_ref[...] = gb
    grad_normed = grad2
    for c in range(0, ff, chunk):
        gh = (dot_nt(gb, w_back[c // chunk]) * slope[:, c : c + chunk]).astype(BF16)
        gh_ref[:, c : c + chunk] = gh
        sums[0:1, c : c + chunk] += sum_rows(gh.astype(F32))
        grad_normed = grad_normed + dot_nt(gh, w_in[c // chunk])
    grad1 = norm_back(grad_normed, hat1, inverse1, gain1)
    resid_ref[...] = grad1
    attn = grad1.astype(BF16)
    attn_ref[...] = attn
    gc_own[...] = dot_nt(attn, wo_own[...]).astype(BF16)
    gc_other[...] = dot_nt(attn, wo_other[...]).astype(BF16)
    at = lambda r, s, v: sums.__setitem__(
        (slice(r, r + 1), slice(s * width, (s + 1) * width)),
        sums[r : r + 1, s * width : (s + 1) * width] + sum_rows(v),
    )
    at(1, 0, attn.astype(F32))
    at(1, 1, gb.astype(F32))
    at(1, 2, grad_normed * hat1)
    at(1, 3, grad_normed)
    at(2, 0, cot * hat2)
    at(2, 1, cot)
    for s, ref in enumerate((gc_own, gc_other)):
        half = ref.shape[1]
        lane = slice(2 * width + s * half, 2 * width + (s + 1) * half)
        sums[2:3, lane] += sum_rows(ref[...].astype(F32))


def middle(core, x, own, other, cot, weights, vec):
    count, width = x.shape
    ff = vec.shape[1]
    parts = ff // width
    devices = weights.shape[0]
    unit = width // devices
    once = pl.Buffered(1)
    half_spec = lambda at: pl.BlockSpec(
        (devices // 2, unit, width), lambda i, core: (at(core[0]), 2 * parts, 0), pipeline_mode=once
    )
    in_spec = lambda j: pl.BlockSpec(
        (devices, unit, width), lambda i, core: (0, parts + j, 0), pipeline_mode=once
    )
    half = own.shape[1]
    rows = min(256, count)
    tile = lambda w: pl.BlockSpec((rows, w), lambda i, core: (i, 0))
    whole = lambda a: pl.BlockSpec(a.shape, lambda i, core: (0, 0), pipeline_mode=once)
    return pl.pallas_call(
        functools.partial(middle_kernel, width=width, ff=ff),
        grid_spec=pltpu.PrefetchScalarGridSpec(
            num_scalar_prefetch=1,
            grid=(count // rows,),
            in_specs=[
                tile(width),
                tile(half),
                tile(half),
                tile(width),
                half_spec(lambda c: c),
                half_spec(lambda c: 1 - c),
                *[in_spec(j) for j in range(parts)],
                pl.BlockSpec((devices, parts * unit, width), lambda i, core: (0, 0, 0), pipeline_mode=once),
                whole(vec),
            ],
            out_specs=[
                tile(width),
                tile(width),
                tile(half),
                tile(half),
                tile(width),
                tile(ff),
                tile(ff),
                tile(width),
                tile(width),
                pl.BlockSpec((8, ff), lambda i, core: (0, 0)),
            ],
            scratch_shapes=[
                pltpu.VMEM((rows, ff), F32),
                pltpu.VMEM((half, width), BF16),
                pltpu.VMEM((half, width), BF16),
                pltpu.VMEM((parts, width, width), BF16),
                pltpu.VMEM((parts, width, width), BF16),
            ],
        ),
        out_shape=[
            jax.ShapeDtypeStruct((count, width), BF16),
            jax.ShapeDtypeStruct((count, width), F32),
            jax.ShapeDtypeStruct((count, half), BF16),
            jax.ShapeDtypeStruct((count, half), BF16),
            jax.ShapeDtypeStruct((count, width), BF16),
            jax.ShapeDtypeStruct((count, ff), BF16),
            jax.ShapeDtypeStruct((count, ff), BF16),
            jax.ShapeDtypeStruct((count, width), BF16),
            jax.ShapeDtypeStruct((count, width), BF16),
            jax.ShapeDtypeStruct((8, ff), F32),
        ],
        compiler_params=pltpu.CompilerParams(vmem_limit_bytes=VMEM_BYTES),
        cost_estimate=pl.CostEstimate(
            flops=2 * count * width * (4 * ff + 2 * width),
            bytes_accessed=2 * (4 * width * ff + 2 * count * ff + 8 * count * width),
            transcendentals=2 * count * ff,
        ),
        name="middle",
    )(core, x, own, other, cot, *([weights] * (3 + parts)), vec)


def weight_grads_kernel(
    core, act, gb, low, gh, own, other, attn, keep_ref, send_ref, stage_a, stage_b, sems, *, parts
):
    step = pl.program_id(0)
    inner, outer, _, unit, width = keep_ref.shape
    last = 2 * parts

    def tn(a, b):
        return lax.dot_general(a, b, (((0,), (0,)), ((), ())), preferred_element_type=F32).astype(BF16)

    def copies(t):
        slot = t % 2
        runs = 2 * outer // parts if t < parts else 2 * outer
        found = []
        for r in range(runs):
            g = t * runs + r if t < parts else r
            take = slice(r * inner, (r + 1) * inner)
            at = (slice(None), g % outer, slice(0, parts) if t < parts else t)
            source = (stage_a if t < parts else stage_b).at[slot, take]
            found.append(
                (g // outer,)
                + tuple(
                    functools.partial(pltpu.make_async_copy, source, ref.at[at], sems.at[slot])
                    for ref in (keep_ref, send_ref)
                )
            )
        return found

    def finish(t):
        for _, keep, _ in copies(t):
            keep().wait()

    for t in range(2, last + 1):

        @pl.when(step == t)
        def _():
            finish(t - 2)

    slot = lax.rem(step, 2)

    @pl.when(step < parts)
    def _():
        stage_a[slot] = tn(act[...], gb[...]).reshape(stage_a.shape[1:])

    @pl.when(jnp.logical_and(step >= parts, step < last))
    def _():
        stage_b[slot] = tn(low[...], gh[...]).reshape(stage_b.shape[1:])

    @pl.when(step == last)
    def _():
        half = stage_b.shape[1] // 2
        stage_b[slot, :half] = tn(own[...], attn[...]).reshape((half,) + stage_b.shape[2:])
        stage_b[slot, half:] = tn(other[...], attn[...]).reshape((half,) + stage_b.shape[2:])

    for t in range(last + 1):

        @pl.when(step == t)
        def _():
            for c, keep, send in copies(t):
                if t == last:
                    (keep if c == 0 else send)().start()
                    continue

                @pl.when(core[0] == c)
                def _():
                    keep().start()

                @pl.when(core[0] != c)
                def _():
                    send().start()

    @pl.when(step == last)
    def _():
        finish(last - 1)
        finish(last)


def weight_grads(core, act, gb, low, gh, own, other, attn, inner, outer):
    count, width = low.shape
    parts = act.shape[1] // width
    unit = width // (2 * inner * outer)
    once = pl.Buffered(1)
    whole = lambda a: pl.BlockSpec(a.shape, lambda t, core: (0, 0), pipeline_mode=once)
    shape = jax.ShapeDtypeStruct((inner, outer, 2 * parts + 1, unit, width), BF16)
    return pl.pallas_call(
        functools.partial(weight_grads_kernel, parts=parts),
        grid_spec=pltpu.PrefetchScalarGridSpec(
            num_scalar_prefetch=1,
            grid=(2 * parts + 1,),
            in_specs=[
                pl.BlockSpec((count, width), lambda t, core: (0, jnp.minimum(t, parts - 1))),
                whole(gb),
                whole(low),
                pl.BlockSpec((count, width), lambda t, core: (0, jnp.clip(t - parts, 0, parts - 1))),
                whole(own),
                whole(other),
                whole(attn),
            ],
            out_specs=[pl.BlockSpec(memory_space=pl.ANY)] * 2,
            scratch_shapes=[
                pltpu.VMEM((2, 2 * inner * outer // parts, parts, unit, width), BF16),
                pltpu.VMEM((2, 2 * inner * outer, unit, width), BF16),
                pltpu.SemaphoreType.DMA((2,)),
            ],
        ),
        out_shape=[shape, shape],
        compiler_params=pltpu.CompilerParams(vmem_limit_bytes=VMEM_BYTES),
        cost_estimate=pl.CostEstimate(
            flops=2 * count * width * width * (2 * parts + 1),
            bytes_accessed=2 * width * (2 * parts + 4) * (count + width),
            transcendentals=0,
        ),
        name="weight_grads",
    )(core, act, gb, low, gh, own, other, attn)


def project_kernel(x0, x1, x2, x3, first, second, bias, out_ref, weight_ref, *, group):
    step = pl.program_id(0)
    blocks, width = pl.num_programs(0) // 4, x0.shape[1]
    rows = first.shape[0] * (weight_ref.shape[0] // first.shape[0] // 2)

    @pl.when(step == 0)
    def _():
        unit = weight_ref.shape[0] // (2 * first.shape[0])
        weight_ref[:rows, :] = first[:, :unit, :].reshape(rows, 3 * group)
        weight_ref[rows:, :] = second[:, :unit, :].reshape(rows, 3 * group)

    for p, ref in enumerate((x0, x1, x2, x3)):

        @pl.when(step // blocks == p)
        def _():
            start = 0 if p < 2 else group
            got = dot(ref[...], weight_ref[:, start:]) + bias[0:1, start:]
            out_ref[0, :, start:] = got.astype(BF16)


def project(pieces, first, second, bias):
    count, width = pieces[0].shape
    wide = first.shape[2]
    rows = min(512, count)
    blocks = count // rows
    once = pl.Buffered(1)
    piece = lambda p: pl.BlockSpec((rows, width), lambda i: (jnp.clip(i - p * blocks, 0, blocks - 1), 0))
    whole = lambda a: pl.BlockSpec(a.shape, lambda i: (0,) * a.ndim, pipeline_mode=once)
    return pl.pallas_call(
        functools.partial(project_kernel, group=wide // 3),
        grid=(4 * blocks,),
        in_specs=[piece(p) for p in range(4)] + [whole(first), whole(second), whole(bias)],
        out_specs=[
            pl.BlockSpec((1, rows, wide), lambda i: (i // (2 * blocks), i % (2 * blocks), 0)),
            pl.BlockSpec((width, wide), lambda i: (0, 0)),
        ],
        out_shape=[
            jax.ShapeDtypeStruct((2, 2 * count, wide), BF16),
            jax.ShapeDtypeStruct((width, wide), BF16),
        ],
        compiler_params=pltpu.CompilerParams(vmem_limit_bytes=VMEM_BYTES),
        cost_estimate=pl.CostEstimate(
            flops=2 * 4 * count * width * wide, bytes_accessed=8 * count * (width + wide), transcendentals=0
        ),
        name="project",
    )(*pieces, first, second, bias)


def far_rows_kernel(dkv, weight, keep_ref, send_ref, *, group):
    step = pl.program_id(0)
    got = dot_nt(dkv[0].T, weight[:, group:]).astype(BF16)

    @pl.when(step < pl.num_programs(0) // 2)
    def _():
        keep_ref[...] = got

    @pl.when(step >= pl.num_programs(0) // 2)
    def _():
        send_ref[...] = got


def far_rows(dkv, weight):
    count, (width, wide) = dkv.shape[2], weight.shape
    rows = min(512, count // 2)
    blocks = count // rows
    return pl.pallas_call(
        functools.partial(far_rows_kernel, group=wide // 3),
        grid=(blocks,),
        in_specs=[
            pl.BlockSpec((1, dkv.shape[1], rows), lambda i: (1, 0, i)),
            pl.BlockSpec((width, wide), lambda i: (0, 0), pipeline_mode=pl.Buffered(1)),
        ],
        out_specs=[
            pl.BlockSpec((rows, width), lambda i: (jnp.minimum(i, blocks // 2 - 1), 0)),
            pl.BlockSpec((rows, width), lambda i: (jnp.maximum(i - blocks // 2, 0), 0)),
        ],
        out_shape=[jax.ShapeDtypeStruct((count // 2, width), BF16)] * 2,
        compiler_params=pltpu.CompilerParams(vmem_limit_bytes=VMEM_BYTES),
        cost_estimate=pl.CostEstimate(
            flops=2 * count * width * dkv.shape[1], bytes_accessed=8 * count * width, transcendentals=0
        ),
        name="far_rows",
    )(dkv, weight)


def near_rows_kernel(dq, dkv, weight, resid, keep_ref, send_ref, *, group):
    step = pl.program_id(0)
    got = dot_nt(dq[...].T, weight[:, :group]) + dot_nt(dkv[0].T, weight[:, group:])

    @pl.when(step < pl.num_programs(0) // 2)
    def _():
        keep_ref[...] = got + resid[...]

    @pl.when(step >= pl.num_programs(0) // 2)
    def _():
        send_ref[...] = got.astype(BF16)


def near_rows(dq, dkv, weight, resid):
    count, (width, wide) = dkv.shape[2], weight.shape
    rows = min(512, count // 2)
    blocks = count // rows
    return pl.pallas_call(
        functools.partial(near_rows_kernel, group=wide // 3),
        grid=(blocks,),
        in_specs=[
            pl.BlockSpec((dq.shape[0], rows), lambda i: (0, i)),
            pl.BlockSpec((1, dkv.shape[1], rows), lambda i: (0, 0, i)),
            pl.BlockSpec((width, wide), lambda i: (0, 0), pipeline_mode=pl.Buffered(1)),
            pl.BlockSpec((rows, width), lambda i: (jnp.minimum(i, blocks // 2 - 1), 0)),
        ],
        out_specs=[
            pl.BlockSpec((rows, width), lambda i: (jnp.minimum(i, blocks // 2 - 1), 0)),
            pl.BlockSpec((rows, width), lambda i: (jnp.maximum(i - blocks // 2, 0), 0)),
        ],
        out_shape=[
            jax.ShapeDtypeStruct((count // 2, width), F32),
            jax.ShapeDtypeStruct((count // 2, width), BF16),
        ],
        compiler_params=pltpu.CompilerParams(vmem_limit_bytes=VMEM_BYTES),
        cost_estimate=pl.CostEstimate(
            flops=2 * count * width * wide, bytes_accessed=12 * count * width, transcendentals=0
        ),
        name="near_rows",
    )(dq, dkv, weight, resid)


def qkv_grads_kernel(core, dq, dkv, x0, x1, x2, x3, small, out_ref):
    step = pl.program_id(0)
    blocks, unit = out_ref.shape[1], x0.shape[1] // (2 * out_ref.shape[1])
    local = x0.shape[0]

    def put(value):
        value = value.T.astype(BF16)
        half = value.shape[0] // 2
        for h in (0, 1):
            place_at = (core[0] + h) % 2
            out_ref[place_at, :, :unit, :] = value[h * half : (h + 1) * half].reshape(blocks, unit, -1)

    @pl.when(step == 0)
    def _():
        put(dot(dq[:, :local], x0[...]) + dot(dq[:, local:], x1[...]))

    @pl.when(step > 0)
    def _():
        near, far = dkv[0, 0], dkv[1, 0]
        put(
            dot(near[:, :local], x0[...])
            + dot(near[:, local:], x1[...])
            + dot(far[:, :local], x2[...])
            + dot(far[:, local:], x3[...])
        )

    out_ref[:, :, unit:, :] = small[...]


def qkv_grads(core, dq, dkv, pieces, small):
    count, width = pieces[0].shape
    group, full = dq.shape
    blocks, extra = small.shape[1:3]
    unit = width // (2 * blocks)
    once = pl.Buffered(1)
    whole = pl.BlockSpec((count, width), lambda t, core: (0, 0), pipeline_mode=once)
    return pl.pallas_call(
        qkv_grads_kernel,
        grid_spec=pltpu.PrefetchScalarGridSpec(
            num_scalar_prefetch=1,
            grid=(3,),
            in_specs=[
                pl.BlockSpec((group, full), lambda t, core: (0, 0), pipeline_mode=once),
                pl.BlockSpec((2, 1, group, full), lambda t, core: (0, jnp.maximum(t - 1, 0), 0, 0)),
                whole,
                whole,
                whole,
                whole,
                pl.BlockSpec((2, blocks, extra, group), lambda t, core: (0, 0, 0, t)),
            ],
            out_specs=pl.BlockSpec((2, blocks, unit + extra, group), lambda t, core: (0, 0, 0, t)),
        ),
        out_shape=jax.ShapeDtypeStruct((2, blocks, unit + extra, 3 * group), BF16),
        compiler_params=pltpu.CompilerParams(vmem_limit_bytes=VMEM_BYTES),
        cost_estimate=pl.CostEstimate(
            flops=10 * full * width * group, bytes_accessed=16 * full * width, transcendentals=0
        ),
        name="qkv_grads",
    )(core, dq, dkv, *pieces, small)


GATE = 4
ORDER = 0


def unpacked(blocks, parts):
    devices, size, width = blocks.shape
    rows = size // (2 * parts + 1)
    back = blocks[:, : parts * rows].reshape(devices * parts * rows, width)
    into = blocks[:, parts * rows : 2 * parts * rows].reshape(devices, parts, rows, width)
    into = into.transpose(0, 2, 1, 3).reshape(devices * rows, parts * width)
    return back, into, blocks[:, 2 * parts * rows :].reshape(devices * rows, width)


def packed(back, into, out, devices):
    rows, width = out.shape[0] // devices, out.shape[1]
    parts = back.shape[0] // out.shape[0]
    into = into.reshape(devices, rows, parts, width).transpose(0, 2, 1, 3)
    return jnp.concatenate(
        [a.reshape(devices, -1, width) for a in (back, into, out)], axis=1
    )


def dot_tn(a, b):
    return lax.dot_general(a, b, (((0,), (0,)), ((), ())), preferred_element_type=F32)


def per_device(
    tokens,
    lengths,
    pair_flip,
    w_qkv,
    q_bias,
    v_bias,
    w_out,
    out_bias,
    norm1_gain,
    norm1_shift,
    w_in,
    in_bias,
    w_back,
    back_bias,
    norm2_gain,
    norm2_shift,
    cotangent,
):
    both = ("head", "blk")
    cores = lax.axis_size("head")
    blocks = lax.axis_size("blk")
    core = lax.axis_index("head")
    block = lax.axis_index("blk")
    local, width = tokens.shape[1:]
    half = local * cores
    heads = HEADS // cores
    group = heads * HD
    ff = w_in.shape[1]
    parts = ff // width
    rows = w_qkv.shape[0]
    x = tokens[0]

    x_sib = swap(x, "head", 1)
    x_far = swap(x, "blk", 1)
    vectors = jnp.stack(
        [q_bias, v_bias, out_bias, back_bias, norm1_gain, norm1_shift, norm2_gain, norm2_shift], axis=0
    )
    extra = jnp.concatenate(
        [
            jnp.pad(vectors, ((0, 0), (0, LANES - rows))),
            jnp.pad(in_bias[None], ((0, 7), (0, 3 * group - LANES - parts * rows))),
        ],
        axis=1,
    )
    columns = w_qkv.reshape(rows, 3, cores, group)
    kept = lax.dynamic_index_in_dim(columns, core, 2, keepdims=False).reshape(rows, 3 * group)
    given = lax.dynamic_index_in_dim(columns, 1 - core, 2, keepdims=False).reshape(rows, 3 * group)
    mine = jnp.concatenate([kept, extra], axis=0)
    theirs = swap(jnp.concatenate([given, extra], axis=0), "head", 1)
    first, second, x_far = gather_blk(place(mine, theirs, core == 1, 0), x_far)
    small = jnp.concatenate([first[:, rows:, : 2 * LANES], second[:, rows:, : 2 * LANES]], axis=0)

    def vector(slot):
        if slot == 8:
            return small[:, 0, LANES : LANES + parts * rows].reshape(-1).astype(F32)
        return small[:, slot, :rows].reshape(-1).astype(F32)

    bias = jnp.concatenate(
        [
            lax.dynamic_slice_in_dim(vector(0), core * group, group),
            jnp.zeros((group,), F32),
            lax.dynamic_slice_in_dim(vector(1), core * group, group),
        ]
    )
    vec = jnp.concatenate(
        [
            vector(8)[None],
            jnp.pad(jnp.concatenate([vector(2), vector(3), vector(4), vector(5)]), (0, ff - 4 * width))[None],
            jnp.pad(jnp.concatenate([vector(6), vector(7)]), (0, ff - 2 * width))[None],
            jnp.zeros((5, ff), F32),
        ],
        axis=0,
    )

    shard = jnp.concatenate(
        [w_back, w_in.reshape(rows, parts, width).transpose(1, 0, 2).reshape(parts * rows, width), w_out], axis=0
    )
    if GATE in (1, 4):
        shard, x_far = lax.optimization_barrier((shard, x_far))
    elif GATE in (2, 6):
        shard, first = lax.optimization_barrier((shard, first))
    elif GATE == 3:
        shard, first, x_far = lax.optimization_barrier((shard, first, x_far))
    gathered = lax.all_gather(shard, both, axis=0, tiled=True).reshape(cores * blocks, -1, width)
    direct = rows % 8 == 0 and blocks % 4 == 0 and (2 * blocks) % (4 * parts) == 0
    if direct:
        inner, outer = 4, blocks // 4
    else:
        inner, outer = 4, 4
        gathered = packed(*unpacked(gathered, parts), cores * inner * outer)

    pieces = (x, x_sib, x_far, swap(x_far, "head", 1))
    bias = jnp.pad(bias[None], ((0, 7), (0, 0)))
    if direct:
        qkv, weight = project(pieces, first, second, bias)
    else:
        shape = (16, width // 32, 3 * group)
        qkv, weight = project(
            pieces, first[:, :rows].reshape(shape), second[:, :rows].reshape(shape), bias
        )

    sequence = block // 2
    own_half = block % 2
    length = lax.dynamic_index_in_dim(lengths, sequence, 0, keepdims=False)
    flags = lax.dynamic_index_in_dim(pair_flip, sequence, 0, keepdims=False)
    flags = lax.dynamic_slice_in_dim(flags, core * heads, heads)
    bounds = [jnp.clip(length - h * half, 0, half) for h in (own_half, 1 - own_half)]
    sc = jnp.concatenate([flags, jnp.stack(bounds + [jnp.int32(local), core])]).astype(jnp.int32)

    context, lse = attend(sc, qkv, group)
    other = swap(context[local:], "head", 1)
    at_core = core.reshape(1).astype(jnp.int32)
    out, grad_resid1, gc_own, gc_other, low, act, gh, gb, attn, sums = middle(
        at_core, x, context[:local], other, cotangent[0], gathered, vec
    )
    grad_context = jnp.concatenate([gc_own, swap(gc_other, "head", 1)], axis=0)

    keep, send = weight_grads(at_core, act, gb, low, gh, context[:local], other, attn, inner, outer)
    chip = (keep.astype(F32) + swap(send, "head", 1).astype(F32)).astype(BF16)
    if direct:
        chip = chip.reshape(inner * outer * (2 * parts + 1) * rows, width)
        near = [[o * inner + i for i in range(inner)] for o in range(outer)]
        far = [[o * inner + i for o in range(outer)] for i in range(inner)]
        for groups in (near, far):
            chip = lax.psum_scatter(chip, "blk", scatter_dimension=0, axis_index_groups=groups, tiled=True)
    else:
        chip = chip.transpose(1, 0, 2, 3, 4).reshape(inner * outer, -1, width)
        chip = packed(*unpacked(chip, parts), blocks)
        chip = lax.psum_scatter(chip, "blk", scatter_dimension=0, tiled=True)[0]
    sum_wback = chip[: parts * rows].astype(F32)
    sum_win = chip[parts * rows : 2 * parts * rows].astype(F32)
    sum_win = sum_win.reshape(parts, rows, width).transpose(1, 0, 2).reshape(rows, ff)
    sum_wout = chip[2 * parts * rows :].astype(F32)

    dq, dkv, dq_sum = attend_back(sc, qkv, context, lse, grad_context, group)
    joint = dkv.reshape(2, 2 * group, half)

    at_group = lambda v: lax.dynamic_update_slice_in_dim(jnp.zeros((width,), F32), v, core * group, 0)
    grad_small = [
        at_group(jnp.sum(dq_sum, axis=1)),
        place(sums[2, 2 * width : 2 * width + group], sums[2, 2 * width + group : 3 * width], core == 1, 0).reshape(-1),
        sums[1, :width],
        sums[1, width : 2 * width],
        sums[1, 2 * width : 3 * width],
        sums[1, 3 * width : 4 * width],
        sums[2, :width],
        sums[2, width : 2 * width],
    ]
    grad_small = jnp.concatenate(
        [jnp.stack(grad_small, 0).reshape(8, cores, blocks, rows).transpose(1, 2, 0, 3).reshape(cores, blocks, -1)]
        + [sums[0].reshape(cores, blocks, parts * rows)],
        axis=2,
    )
    small_size = grad_small.shape[2]
    grad_small = jnp.pad(grad_small, ((0, 0), (0, 0), (0, 3 * group - small_size)))
    high = grad_small.astype(BF16)
    low_part = (grad_small - high.astype(F32)).astype(BF16)
    small_rows = jnp.pad(jnp.stack([high, low_part], axis=2), ((0, 0), (0, 0), (0, 6), (0, 0)))
    small_rows = jnp.where(core == 0, small_rows, small_rows[::-1])
    if direct:
        outgoing = qkv_grads(at_core, dq, dkv, pieces, small_rows)
    else:
        none = jnp.zeros((2, 16, 8, 3 * group), BF16)
        outgoing = qkv_grads(at_core, dq, dkv, pieces, none)[:, :, : width // 32]
        outgoing = jnp.concatenate([outgoing.reshape(2, blocks, rows, 3 * group), small_rows], axis=2)
    keep, came = outgoing[0], swap(outgoing[1], "head", 1)
    exchanged = lax.all_to_all(jnp.stack([keep, came], axis=1), "blk", 0, 0, tiled=True).astype(F32)
    keep_far, send_far = far_rows(joint, weight)
    far_sib = swap(send_far, "head", 1)
    far_in = swap((keep_far.astype(F32) + far_sib.astype(F32)).astype(BF16), "blk", 1)
    keep_near, send_near = near_rows(dq, joint, weight, grad_resid1)
    near_sib = swap(send_near, "head", 1)
    grad_tokens = keep_near + near_sib.astype(F32) + far_in.astype(F32)

    total = jnp.sum(exchanged, axis=0)
    own_w, other_w = (total[s, :rows].reshape(rows, 3, group) for s in (0, 1))
    sum_wqkv = place(own_w, other_w, core == 1, 2).reshape(rows, 3 * width)
    vectors = total[0, rows] + total[0, rows + 1] + total[1, rows] + total[1, rows + 1]

    def summed(slot, size=rows):
        return vectors[slot * rows : slot * rows + size]

    return (
        out[None],
        grad_tokens[None],
        sum_wqkv,
        summed(0),
        summed(1),
        sum_wout,
        summed(2),
        summed(4),
        summed(5),
        sum_win,
        summed(8, parts * rows),
        sum_wback,
        summed(3),
        summed(6),
        summed(7),
    )


def solution(mesh):
    split = P(("head", "blk"))
    matrix = P(("head", "blk"), None)
    rows = P("blk", "head", None)
    return jax.shard_map(
        per_device,
        mesh=mesh,
        in_specs=(
            rows,
            P(),
            P(),
            matrix,
            split,
            split,
            matrix,
            split,
            split,
            split,
            matrix,
            split,
            matrix,
            split,
            split,
            split,
            rows,
        ),
        out_specs=(
            rows,
            rows,
            matrix,
            split,
            split,
            matrix,
            split,
            split,
            split,
            matrix,
            split,
            matrix,
            split,
            split,
            split,
        ),
        check_vma=False,
    )
```

```python
import functools

import jax
import jax.numpy as jnp
from jax import lax
from jax.experimental import pallas as pl
from jax.experimental.pallas import tpu as pltpu
from jax.sharding import PartitionSpec as P

HEADS = 12
HD = 64
LANES = 128
NEG = -1e30
EPS = 1e-06
SAFE_LOGIT = 60.0
BF16 = jnp.bfloat16
F32 = jnp.float32
NT = (((1,), (1,)), ((), ()))
VMEM_BYTES = 58 << 20


def dot(a, b):
    return jnp.dot(a, b, preferred_element_type=F32)


def dot_nt(a, b):
    return lax.dot_general(a, b, NT, preferred_element_type=F32)


def swap(value, axis, apart):
    pairs = [(source, source ^ apart) for source in range(lax.axis_size(axis))]
    return lax.ppermute(value, axis, pairs)


def place(mine, theirs, upper, axis):
    return jnp.stack([jnp.where(upper, theirs, mine), jnp.where(upper, mine, theirs)], axis=axis)


def gather_blk(pair, also):
    count = lax.axis_size("blk")
    index = lax.axis_index("blk")
    bits = [1 << b for b in range(count.bit_length() - 1)][::-1]
    held = pair
    depth = 1
    for bit in bits[:-2]:
        held = place(held, swap(held, "blk", bit), (index & bit) != 0, depth)
        depth += 1
    if GATE >= 4:
        held, also = lax.optimization_barrier((held, also))
    first, second = held[0], held[1]
    depth -= 1
    high, low = bits[-2], bits[-1]
    first_in = swap(first, "blk", high)
    second_in = swap(second, "blk", low)
    first = place(first, first_in, (index & high) != 0, depth)
    second = place(second, second_in, (index & low) != 0, depth)
    first_in = swap(first, "blk", low)
    second_in = swap(second, "blk", high)
    first = place(first, first_in, (index & low) != 0, depth + 1)
    second = place(second, second_in, (index & high) != 0, depth)
    return tuple(a.reshape((count,) + pair.shape[1:]) for a in (first, second)) + (also,)


def first_head(rows):
    lane = lax.broadcasted_iota(jnp.int32, (rows, LANES), 1)
    return lane < HD, lane % HD


def key_rows(own, sub, keys, row, sc, source, heads):
    at = lax.broadcasted_iota(jnp.int32, keys.shape, 0) + row
    bound, local, core = sc[heads + source], sc[heads + 2], sc[heads + 3]
    position = jnp.where(at < local, at + core * local, at - core * local)
    bias = jnp.where(position < bound, 0.0, NEG)
    extra = jnp.where(sub < 3, -1.0, jnp.where(sub == 3, bias, 0.0))
    return jnp.where(own, keys.astype(F32), extra).astype(BF16)


def three_parts(value):
    first = value.astype(BF16).astype(F32)
    rest = value - first
    second = rest.astype(BF16).astype(F32)
    return first, second, rest - second


def attend_kernel(
    sc, q_ref, ka_ref, kb_ref, va_ref, vb_ref, o_ref, lse_ref, keys, values, key_norm, *, heads, step
):
    pair = pl.program_id(0)
    count = keys.shape[1]
    rows = q_ref.shape[1]
    scale = HD ** (-0.5)

    @pl.when(pl.program_id(1) == 0)
    def _():
        piece = min(512, count)
        own0, sub = first_head(piece)
        for h, (k_ref, v_ref) in enumerate(((ka_ref, va_ref), (kb_ref, vb_ref))):
            source = sc[2 * pair + h]
            own = own0 if h == 0 else jnp.logical_not(own0)
            largest = jnp.float32(0.0)
            for r in range(0, count, piece):
                k = k_ref[0, r : r + piece, :]
                keys[h, r : r + piece, :] = key_rows(own, sub, k, r, sc, source, heads)
                values[h, :HD, r : r + piece] = v_ref[0, r : r + piece, :].T[h * HD : (h + 1) * HD, :]
                values[h, HD:, r : r + piece] = jnp.ones((16, piece), BF16)
                k = jnp.where(own, k.astype(F32), 0.0)
                largest = jnp.maximum(largest, jnp.max(jnp.sum(k * k, axis=1, keepdims=True)))
            key_norm[h] = largest

    q = q_ref[0].astype(F32) * scale
    own0, sub = first_head(rows)
    one = jnp.where(sub == 3, 1.0, 0.0)
    square = q * q
    norm_a = jnp.max(jnp.sum(jnp.where(own0, square, 0.0), axis=1, keepdims=True))
    norm_b = jnp.max(jnp.sum(jnp.where(own0, 0.0, square), axis=1, keepdims=True))
    largest = jnp.maximum(norm_a * key_norm[0], norm_b * key_norm[1])
    small = largest < SAFE_LOGIT * SAFE_LOGIT

    def queries(h):
        return (jnp.where(own0, q, one) if h == 0 else jnp.where(own0, one, q)).astype(BF16)

    def finish(outs, peaks):
        totals = [jnp.broadcast_to(o[HD : HD + 1, :], (HD, rows)) for o in outs]
        o_ref[...] = (
            jnp.concatenate([o[:HD, :] / t for o, t in zip(outs, totals)], axis=0).T.astype(BF16)
        )
        lse = jnp.concatenate([jnp.log(totals[1]), jnp.log(totals[0])], axis=0).T
        if peaks is not None:
            lse = lse + jnp.where(own0, peaks[1], peaks[0])
        lse_ref[...] = lse

    @pl.when(small)
    def _():
        outs = []
        for h in (0, 1):
            qa = queries(h)
            out = None
            for c in range(0, count, step):
                p = jnp.exp(dot_nt(qa, keys[h, c : c + step, :])).astype(BF16)
                part = dot_nt(values[h, :, c : c + step], p)
                out = part if out is None else out + part
            outs.append(out)
        finish(outs, None)

    @pl.when(jnp.logical_not(small))
    def _():
        outs, peaks = [], []
        for h in (0, 1):
            s = dot_nt(queries(h), keys[h])
            peak = jnp.max(s, axis=1, keepdims=True)
            outs.append(dot_nt(values[h], jnp.exp(s - peak).astype(BF16)))
            peaks.append(peak)
        finish(outs, peaks)


def pair_specs(count, width, skip=0):
    pairs = width // LANES

    def key_value(h, base):
        return pl.BlockSpec((1, count, LANES), lambda p, i, sc: (sc[2 * (p + skip) + h], 0, base * pairs + p + skip))

    return [key_value(0, 1), key_value(1, 1), key_value(0, 2), key_value(1, 2)]


def attend(sc, qkv, width):
    count = qkv.shape[1]
    rows = min(1024, count)
    row_spec = pl.BlockSpec((rows, LANES), lambda p, i, sc: (i, p))
    q_spec = pl.BlockSpec((1, rows, LANES), lambda p, i, sc: (0, i, p))
    heads = width // HD
    return pl.pallas_call(
        functools.partial(attend_kernel, heads=heads, step=min(512, count)),
        grid_spec=pltpu.PrefetchScalarGridSpec(
            num_scalar_prefetch=1,
            grid=(width // LANES, count // rows),
            in_specs=[q_spec] + pair_specs(count, width),
            out_specs=[row_spec, row_spec],
            scratch_shapes=[
                pltpu.VMEM((2, count, LANES), BF16),
                pltpu.VMEM((2, HD + 16, count), BF16),
                pltpu.SMEM((2,), F32),
            ],
        ),
        out_shape=[
            jax.ShapeDtypeStruct((count, width), BF16),
            jax.ShapeDtypeStruct((count, width), F32),
        ],
        compiler_params=pltpu.CompilerParams(vmem_limit_bytes=VMEM_BYTES),
        cost_estimate=pl.CostEstimate(
            flops=4 * 4 * count * count * width, bytes_accessed=2 * 6 * count * width, transcendentals=0
        ),
        name="attend",
    )(sc, qkv, qkv, qkv, qkv, qkv)


def attend_back_kernel(
    sc,
    q_ref,
    ka_ref,
    kb_ref,
    va_ref,
    vb_ref,
    o_ref,
    lse_ref,
    do_ref,
    dq_ref,
    dkv_ref,
    sum_ref,
    keys,
    keys_t,
    values,
    dk_sum,
    dv_sum,
    *,
    heads,
    step,
    skip,
):
    pair = pl.program_id(0) + skip
    block = pl.program_id(1)
    count = keys.shape[1]
    rows = q_ref.shape[1]
    scale = HD ** (-0.5)

    @pl.when(block == 0)
    def _():
        piece = min(512, count)
        own0, sub = first_head(piece)
        for h, (k_ref, v_ref) in enumerate(((ka_ref, va_ref), (kb_ref, vb_ref))):
            source = sc[2 * pair + h]
            own = own0 if h == 0 else jnp.logical_not(own0)
            for r in range(0, count, piece):
                k = k_ref[0, r : r + piece, :]
                keys[h, r : r + piece, :] = key_rows(own, sub, k, r, sc, source, heads)
                keys_t[h, :, r : r + piece] = k.T[h * HD : (h + 1) * HD, :]
                v = v_ref[0, r : r + piece, :].astype(F32)
                values[h, r : r + piece, :] = jnp.where(own, v, 1.0).astype(BF16)
        sum_ref[...] = jnp.zeros_like(sum_ref)
        dk_sum[...] = jnp.zeros_like(dk_sum)
        dv_sum[...] = jnp.zeros_like(dv_sum)

    q = q_ref[0]
    do = do_ref[...]
    own0, sub = first_head(rows)
    qf = q.astype(F32) * scale
    first, second, third = three_parts(lse_ref[...])
    q_extra = jnp.where(
        sub == 0, first, jnp.where(sub == 1, second, jnp.where(sub == 2, third, jnp.where(sub == 3, 1.0, 0.0)))
    )
    dof = do.astype(F32)
    product = dof * o_ref[...].astype(F32)
    inner_a = jnp.sum(jnp.where(own0, product, 0.0), axis=1, keepdims=True)
    inner_b = jnp.sum(jnp.where(own0, 0.0, product), axis=1, keepdims=True)
    first, second, third = three_parts(jnp.where(own0, -inner_b, -inner_a))
    do_extra = jnp.where(sub == 0, first, jnp.where(sub == 1, second, jnp.where(sub == 2, third, 0.0)))
    q_t = q.T
    do_t = do.T
    grads = []
    for h in (0, 1):
        qa = (jnp.where(own0, qf, q_extra) if h == 0 else jnp.where(own0, q_extra, qf)).astype(BF16)
        da = (jnp.where(own0, dof, do_extra) if h == 0 else jnp.where(own0, do_extra, dof)).astype(BF16)
        own_rows = slice(h * HD, (h + 1) * HD)
        dq = None
        for c in range(0, count, step):
            part = slice(c, c + step)
            p = jnp.exp(dot_nt(qa, keys[h, part, :]))
            ds = (p * dot_nt(da, values[h, part, :])).astype(BF16)
            p = p.astype(BF16)
            t = dot_nt(keys_t[h, :, part], ds)
            dq = t if dq is None else dq + t
            dk_sum[own_rows, part] += dot(q_t[own_rows, :], ds)
            dv_sum[own_rows, part] += dot(do_t[own_rows, :], p)
        grads.append(dq)
    dq = (jnp.concatenate(grads, axis=0) * scale).astype(BF16)
    dq_ref[...] = dq
    for c in range(0, rows, LANES):
        sum_ref[...] += dq[:, c : c + LANES].astype(F32)

    @pl.when(block == pl.num_programs(1) - 1)
    def _():
        for h in (0, 1):
            source = sc[2 * pair + h]
            own_rows = slice(h * HD, (h + 1) * HD)
            dk = dk_sum[own_rows, :] * scale
            dv = dv_sum[own_rows, :]
            for half in (0, 1):
                here = source == half
                dkv_ref[half, 0, own_rows, :] = jnp.where(here, dk, 0.0).astype(BF16)
                dkv_ref[half, 1, own_rows, :] = jnp.where(here, dv, 0.0).astype(BF16)


def attend_back(sc, qkv, context, lse, grad_context, width, skip, pairs):
    count = qkv.shape[1]
    rows = min(1024, count)
    row_spec = pl.BlockSpec((rows, LANES), lambda p, i, sc: (i, p + skip))
    q_spec = pl.BlockSpec((1, rows, LANES), lambda p, i, sc: (0, i, p + skip))
    dq_spec = pl.BlockSpec((LANES, rows), lambda p, i, sc: (p, i))
    dkv_spec = pl.BlockSpec((2, 2, LANES, count), lambda p, i, sc: (0, 0, p, 0))
    heads = width // HD
    return pl.pallas_call(
        functools.partial(attend_back_kernel, heads=heads, step=min(512, count), skip=skip),
        grid_spec=pltpu.PrefetchScalarGridSpec(
            num_scalar_prefetch=1,
            grid=(pairs, count // rows),
            in_specs=[q_spec] + pair_specs(count, width, skip) + [row_spec, row_spec, row_spec],
            out_specs=[dq_spec, dkv_spec, pl.BlockSpec((LANES, LANES), lambda p, i, sc: (p, 0))],
            scratch_shapes=[
                pltpu.VMEM((2, count, LANES), BF16),
                pltpu.VMEM((2, HD, count), BF16),
                pltpu.VMEM((2, count, LANES), BF16),
                pltpu.VMEM((LANES, count), F32),
                pltpu.VMEM((LANES, count), F32),
            ],
        ),
        out_shape=[
            jax.ShapeDtypeStruct((pairs * LANES, count), BF16),
            jax.ShapeDtypeStruct((2, 2, pairs * LANES, count), BF16),
            jax.ShapeDtypeStruct((pairs * LANES, LANES), F32),
        ],
        compiler_params=pltpu.CompilerParams(vmem_limit_bytes=VMEM_BYTES),
        cost_estimate=pl.CostEstimate(
            flops=10 * 4 * count * count * pairs * LANES, bytes_accessed=2 * 12 * count * pairs * LANES, transcendentals=0
        ),
        name="attend_back",
    )(sc, qkv, qkv, qkv, qkv, qkv, context, lse, grad_context)


def mean_of(value):
    return jnp.mean(value, axis=-1, keepdims=True)


def norm_of(value):
    center = value - mean_of(value)
    inverse = lax.rsqrt(mean_of(center * center) + EPS)
    return center * inverse, inverse


def norm_back(grad, normed, inverse, gain):
    dn = grad * gain
    return inverse * (dn - mean_of(dn) - normed * mean_of(dn * normed))


def sum_rows(value):
    return jnp.sum(value, axis=0, keepdims=True)


def middle_kernel(
    core,
    x_ref,
    own_ref,
    other_ref,
    cot_ref,
    wo_own_ref,
    wo_other_ref,
    *refs,
    width,
    ff,
):
    chunk = width
    parts = ff // width
    w_in_refs = refs[:parts]
    (
        w_back_ref,
        vec,
        out_ref,
        resid_ref,
        gc_own,
        gc_other,
        low_ref,
        act_ref,
        gh_ref,
        gb_ref,
        attn_ref,
        sums,
        slope,
        wo_own,
        wo_other,
        w_in,
        w_back,
    ) = refs[parts:]
    in_bias = lambda c: vec[0:1, c : c + chunk]
    row = lambda r, s: vec[r : r + 1, s * width : (s + 1) * width]
    out_bias, back_bias, gain1, shift1 = (row(1, s) for s in range(4))
    gain2, shift2 = row(2, 0), row(2, 1)

    @pl.when(pl.program_id(0) == 0)
    def _():
        sums[...] = jnp.zeros_like(sums)
        wo_own[...] = wo_own_ref[...].reshape(wo_own.shape)
        wo_other[...] = wo_other_ref[...].reshape(wo_other.shape)
        for j in range(parts):
            w_in[j] = w_in_refs[j][...].reshape(w_in.shape[1:])
        devices, rows = w_back_ref.shape[:2]
        some = devices // parts
        for j in range(parts):
            w_back[j] = w_back_ref[j * some : (j + 1) * some].reshape(some * rows, width)

    attended = dot(own_ref[...], wo_own[...]) + dot(other_ref[...], wo_other[...]) + out_bias
    hat1, inverse1 = norm_of(x_ref[...].astype(F32) + attended)
    normed = hat1 * gain1 + shift1
    low = normed.astype(BF16)
    low_ref[...] = low
    branch = None
    for c in range(0, ff, chunk):
        hidden = dot(low, w_in[c // chunk]) + in_bias(c)
        cumulative = 0.5 * (1.0 + lax.erf(hidden * 0.7071067811865476))
        density = 0.3989422804014327 * jnp.exp(-0.5 * hidden * hidden)
        slope[:, c : c + chunk] = cumulative + hidden * density
        act = (hidden * cumulative).astype(BF16)
        act_ref[:, c : c + chunk] = act
        part = dot(act, w_back[c // chunk])
        branch = part if branch is None else branch + part
    hat2, inverse2 = norm_of(normed + (branch + back_bias))
    out_ref[...] = (hat2 * gain2 + shift2).astype(BF16)
    cot = cot_ref[...].astype(F32)
    grad2 = norm_back(cot, hat2, inverse2, gain2)
    gb = grad2.astype(BF16)
    gb_ref[...] = gb
    grad_normed = grad2
    for c in range(0, ff, chunk):
        gh = (dot_nt(gb, w_back[c // chunk]) * slope[:, c : c + chunk]).astype(BF16)
        gh_ref[:, c : c + chunk] = gh
        sums[0:1, c : c + chunk] += sum_rows(gh.astype(F32))
        grad_normed = grad_normed + dot_nt(gh, w_in[c // chunk])
    grad1 = norm_back(grad_normed, hat1, inverse1, gain1)
    resid_ref[...] = grad1
    attn = grad1.astype(BF16)
    attn_ref[...] = attn
    gc_own[...] = dot_nt(attn, wo_own[...]).astype(BF16)
    gc_other[...] = dot_nt(attn, wo_other[...]).astype(BF16)
    at = lambda r, s, v: sums.__setitem__(
        (slice(r, r + 1), slice(s * width, (s + 1) * width)),
        sums[r : r + 1, s * width : (s + 1) * width] + sum_rows(v),
    )
    at(1, 0, attn.astype(F32))
    at(1, 1, gb.astype(F32))
    at(1, 2, grad_normed * hat1)
    at(1, 3, grad_normed)
    at(2, 0, cot * hat2)
    at(2, 1, cot)
    for s, ref in enumerate((gc_own, gc_other)):
        half = ref.shape[1]
        lane = slice(2 * width + s * half, 2 * width + (s + 1) * half)
        sums[2:3, lane] += sum_rows(ref[...].astype(F32))


def middle(core, x, own, other, cot, weights, vec):
    count, width = x.shape
    ff = vec.shape[1]
    parts = ff // width
    devices = weights.shape[0]
    unit = width // devices
    once = pl.Buffered(1)
    half_spec = lambda at: pl.BlockSpec(
        (devices // 2, unit, width), lambda i, core: (at(core[0]), 2 * parts, 0), pipeline_mode=once
    )
    in_spec = lambda j: pl.BlockSpec(
        (devices, unit, width), lambda i, core: (0, parts + j, 0), pipeline_mode=once
    )
    half = own.shape[1]
    rows = min(256, count)
    tile = lambda w: pl.BlockSpec((rows, w), lambda i, core: (i, 0))
    whole = lambda a: pl.BlockSpec(a.shape, lambda i, core: (0, 0), pipeline_mode=once)
    return pl.pallas_call(
        functools.partial(middle_kernel, width=width, ff=ff),
        grid_spec=pltpu.PrefetchScalarGridSpec(
            num_scalar_prefetch=1,
            grid=(count // rows,),
            in_specs=[
                tile(width),
                tile(half),
                tile(half),
                tile(width),
                half_spec(lambda c: c),
                half_spec(lambda c: 1 - c),
                *[in_spec(j) for j in range(parts)],
                pl.BlockSpec((devices, parts * unit, width), lambda i, core: (0, 0, 0), pipeline_mode=once),
                whole(vec),
            ],
            out_specs=[
                tile(width),
                tile(width),
                tile(half),
                tile(half),
                tile(width),
                tile(ff),
                tile(ff),
                tile(width),
                tile(width),
                pl.BlockSpec((8, ff), lambda i, core: (0, 0)),
            ],
            scratch_shapes=[
                pltpu.VMEM((rows, ff), F32),
                pltpu.VMEM((half, width), BF16),
                pltpu.VMEM((half, width), BF16),
                pltpu.VMEM((parts, width, width), BF16),
                pltpu.VMEM((parts, width, width), BF16),
            ],
        ),
        out_shape=[
            jax.ShapeDtypeStruct((count, width), BF16),
            jax.ShapeDtypeStruct((count, width), F32),
            jax.ShapeDtypeStruct((count, half), BF16),
            jax.ShapeDtypeStruct((count, half), BF16),
            jax.ShapeDtypeStruct((count, width), BF16),
            jax.ShapeDtypeStruct((count, ff), BF16),
            jax.ShapeDtypeStruct((count, ff), BF16),
            jax.ShapeDtypeStruct((count, width), BF16),
            jax.ShapeDtypeStruct((count, width), BF16),
            jax.ShapeDtypeStruct((8, ff), F32),
        ],
        compiler_params=pltpu.CompilerParams(vmem_limit_bytes=VMEM_BYTES),
        cost_estimate=pl.CostEstimate(
            flops=2 * count * width * (4 * ff + 2 * width), bytes_accessed=2 * (4 * width * ff + 2 * count * ff + 8 * count * width), transcendentals=0
        ),
        name="middle",
    )(core, x, own, other, cot, *([weights] * (3 + parts)), vec)


def weight_grads_kernel(
    core, act, gb, low, gh, own, other, attn, keep_ref, send_ref, stage_a, stage_b, sems, *, parts
):
    step = pl.program_id(0)
    inner, outer, _, unit, width = keep_ref.shape
    last = 2 * parts

    def tn(a, b):
        return lax.dot_general(a, b, (((0,), (0,)), ((), ())), preferred_element_type=F32).astype(BF16)

    def copies(t):
        slot = t % 2
        runs = 2 * outer // parts if t < parts else 2 * outer
        found = []
        for r in range(runs):
            g = t * runs + r if t < parts else r
            take = slice(r * inner, (r + 1) * inner)
            at = (slice(None), g % outer, slice(0, parts) if t < parts else t)
            source = (stage_a if t < parts else stage_b).at[slot, take]
            found.append(
                (g // outer,)
                + tuple(
                    functools.partial(pltpu.make_async_copy, source, ref.at[at], sems.at[slot])
                    for ref in (keep_ref, send_ref)
                )
            )
        return found

    def finish(t):
        for _, keep, _ in copies(t):
            keep().wait()

    for t in range(2, last + 1):

        @pl.when(step == t)
        def _():
            finish(t - 2)

    slot = lax.rem(step, 2)

    @pl.when(step < parts)
    def _():
        stage_a[slot] = tn(act[...], gb[...]).reshape(stage_a.shape[1:])

    @pl.when(jnp.logical_and(step >= parts, step < last))
    def _():
        stage_b[slot] = tn(low[...], gh[...]).reshape(stage_b.shape[1:])

    @pl.when(step == last)
    def _():
        half = stage_b.shape[1] // 2
        stage_b[slot, :half] = tn(own[...], attn[...]).reshape((half,) + stage_b.shape[2:])
        stage_b[slot, half:] = tn(other[...], attn[...]).reshape((half,) + stage_b.shape[2:])

    for t in range(last + 1):

        @pl.when(step == t)
        def _():
            for c, keep, send in copies(t):
                if t == last:
                    (keep if c == 0 else send)().start()
                    continue

                @pl.when(core[0] == c)
                def _():
                    keep().start()

                @pl.when(core[0] != c)
                def _():
                    send().start()

    @pl.when(step == last)
    def _():
        finish(last - 1)
        finish(last)


def weight_grads(core, act, gb, low, gh, own, other, attn, inner, outer):
    count, width = low.shape
    parts = act.shape[1] // width
    unit = width // (2 * inner * outer)
    once = pl.Buffered(1)
    whole = lambda a: pl.BlockSpec(a.shape, lambda t, core: (0, 0), pipeline_mode=once)
    shape = jax.ShapeDtypeStruct((inner, outer, 2 * parts + 1, unit, width), BF16)
    return pl.pallas_call(
        functools.partial(weight_grads_kernel, parts=parts),
        grid_spec=pltpu.PrefetchScalarGridSpec(
            num_scalar_prefetch=1,
            grid=(2 * parts + 1,),
            in_specs=[
                pl.BlockSpec((count, width), lambda t, core: (0, jnp.minimum(t, parts - 1))),
                whole(gb),
                whole(low),
                pl.BlockSpec((count, width), lambda t, core: (0, jnp.clip(t - parts, 0, parts - 1))),
                whole(own),
                whole(other),
                whole(attn),
            ],
            out_specs=[pl.BlockSpec(memory_space=pl.ANY)] * 2,
            scratch_shapes=[
                pltpu.VMEM((2, 2 * inner * outer // parts, parts, unit, width), BF16),
                pltpu.VMEM((2, 2 * inner * outer, unit, width), BF16),
                pltpu.SemaphoreType.DMA((2,)),
            ],
        ),
        out_shape=[shape, shape],
        compiler_params=pltpu.CompilerParams(vmem_limit_bytes=VMEM_BYTES),
        cost_estimate=pl.CostEstimate(
            flops=2 * count * width * width * (2 * parts + 1), bytes_accessed=2 * width * (2 * parts + 4) * (count + width), transcendentals=0
        ),
        name="weight_grads",
    )(core, act, gb, low, gh, own, other, attn)


def project_kernel(x0, x1, x2, x3, first, second, bias, out_ref, weight_ref, *, group):
    step = pl.program_id(0)
    blocks, width = pl.num_programs(0) // 4, x0.shape[1]
    rows = first.shape[0] * (weight_ref.shape[0] // first.shape[0] // 2)

    @pl.when(step == 0)
    def _():
        unit = weight_ref.shape[0] // (2 * first.shape[0])
        weight_ref[:rows, :] = first[:, :unit, :].reshape(rows, 3 * group)
        weight_ref[rows:, :] = second[:, :unit, :].reshape(rows, 3 * group)

    for p, ref in enumerate((x0, x1, x2, x3)):

        @pl.when(step // blocks == p)
        def _():
            start = 0 if p < 2 else group
            got = dot(ref[...], weight_ref[:, start:]) + bias[0:1, start:]
            out_ref[0, :, start:] = got.astype(BF16)


def project(pieces, first, second, bias):
    count, width = pieces[0].shape
    wide = first.shape[2]
    rows = min(512, count)
    blocks = count // rows
    once = pl.Buffered(1)
    piece = lambda p: pl.BlockSpec((rows, width), lambda i: (jnp.clip(i - p * blocks, 0, blocks - 1), 0))
    whole = lambda a: pl.BlockSpec(a.shape, lambda i: (0,) * a.ndim, pipeline_mode=once)
    return pl.pallas_call(
        functools.partial(project_kernel, group=wide // 3),
        grid=(4 * blocks,),
        in_specs=[piece(p) for p in range(4)] + [whole(first), whole(second), whole(bias)],
        out_specs=[
            pl.BlockSpec((1, rows, wide), lambda i: (i // (2 * blocks), i % (2 * blocks), 0)),
            pl.BlockSpec((width, wide), lambda i: (0, 0)),
        ],
        out_shape=[
            jax.ShapeDtypeStruct((2, 2 * count, wide), BF16),
            jax.ShapeDtypeStruct((width, wide), BF16),
        ],
        compiler_params=pltpu.CompilerParams(vmem_limit_bytes=VMEM_BYTES),
        cost_estimate=pl.CostEstimate(
            flops=2 * 4 * count * width * wide, bytes_accessed=8 * count * (width + wide), transcendentals=0
        ),
        name="project",
    )(*pieces, first, second, bias)


def stacked(refs, which):
    return jnp.concatenate([ref[0, kind] for kind in which for ref in refs], axis=0).T


def far_rows_kernel(*refs, group):
    *dkv, weight, keep_ref, send_ref = refs
    step = pl.program_id(0)
    got = dot_nt(stacked(dkv, (0, 1)), weight[:, group:]).astype(BF16)

    @pl.when(step < pl.num_programs(0) // 2)
    def _():
        keep_ref[...] = got

    @pl.when(step >= pl.num_programs(0) // 2)
    def _():
        send_ref[...] = got


def dkv_spec(part, rows, source):
    return pl.BlockSpec((1, 2, part.shape[2], rows), lambda i: (source, 0, 0, i))


def far_rows(dkv, weight):
    count, (width, wide) = dkv[0].shape[3], weight.shape
    rows = min(512, count // 2)
    blocks = count // rows
    return pl.pallas_call(
        functools.partial(far_rows_kernel, group=wide // 3),
        grid=(blocks,),
        in_specs=[dkv_spec(part, rows, 1) for part in dkv]
        + [pl.BlockSpec((width, wide), lambda i: (0, 0), pipeline_mode=pl.Buffered(1))],
        out_specs=[
            pl.BlockSpec((rows, width), lambda i: (jnp.minimum(i, blocks // 2 - 1), 0)),
            pl.BlockSpec((rows, width), lambda i: (jnp.maximum(i - blocks // 2, 0), 0)),
        ],
        out_shape=[jax.ShapeDtypeStruct((count // 2, width), BF16)] * 2,
        compiler_params=pltpu.CompilerParams(vmem_limit_bytes=VMEM_BYTES),
        cost_estimate=pl.CostEstimate(
            flops=2 * count * width * wide * 2 // 3, bytes_accessed=8 * count * width, transcendentals=0
        ),
        name="far_rows",
    )(*dkv, weight)


def near_rows_kernel(*refs, parts, group):
    dq, dkv = refs[:parts], refs[parts : 2 * parts]
    weight, resid, keep_ref, send_ref = refs[2 * parts :]
    step = pl.program_id(0)
    queries = jnp.concatenate([ref[...] for ref in dq], axis=0).T
    got = dot_nt(queries, weight[:, :group]) + dot_nt(stacked(dkv, (0, 1)), weight[:, group:])

    @pl.when(step < pl.num_programs(0) // 2)
    def _():
        keep_ref[...] = got + resid[...]

    @pl.when(step >= pl.num_programs(0) // 2)
    def _():
        send_ref[...] = got.astype(BF16)


def near_rows(dq, dkv, weight, resid):
    count, (width, wide) = dkv[0].shape[3], weight.shape
    rows = min(512, count // 2)
    blocks = count // rows
    return pl.pallas_call(
        functools.partial(near_rows_kernel, parts=len(dq), group=wide // 3),
        grid=(blocks,),
        in_specs=[pl.BlockSpec((part.shape[0], rows), lambda i: (0, i)) for part in dq]
        + [dkv_spec(part, rows, 0) for part in dkv]
        + [
            pl.BlockSpec((width, wide), lambda i: (0, 0), pipeline_mode=pl.Buffered(1)),
            pl.BlockSpec((rows, width), lambda i: (jnp.minimum(i, blocks // 2 - 1), 0)),
        ],
        out_specs=[
            pl.BlockSpec((rows, width), lambda i: (jnp.minimum(i, blocks // 2 - 1), 0)),
            pl.BlockSpec((rows, width), lambda i: (jnp.maximum(i - blocks // 2, 0), 0)),
        ],
        out_shape=[
            jax.ShapeDtypeStruct((count // 2, width), F32),
            jax.ShapeDtypeStruct((count // 2, width), BF16),
        ],
        compiler_params=pltpu.CompilerParams(vmem_limit_bytes=VMEM_BYTES),
        cost_estimate=pl.CostEstimate(
            flops=2 * count * width * wide, bytes_accessed=12 * count * width, transcendentals=0
        ),
        name="near_rows",
    )(*dq, *dkv, weight, resid)


def qkv_grads_kernel(core, dq, dkv, x0, x1, x2, x3, *refs):
    *small, keep_ref, send_ref = refs
    step = pl.program_id(0)
    inner, outer = keep_ref.shape[:2]
    unit = x0.shape[1] // (2 * inner * outer)
    local = x0.shape[0]

    def put(value):
        value = value.T.astype(BF16)
        half = value.shape[0] // 2
        for h in (0, 1):
            part = value[h * half : (h + 1) * half].reshape(outer, inner, unit, -1)

            @pl.when(core[0] == h)
            def _():
                for o in range(outer):
                    keep_ref[:, o, :unit, :] = part[o]

            @pl.when(core[0] != h)
            def _():
                for o in range(outer):
                    send_ref[:, o, :unit, :] = part[o]

    @pl.when(step == 0)
    def _():
        put(dot(dq[:, :local], x0[...]) + dot(dq[:, local:], x1[...]))

    @pl.when(step > 0)
    def _():
        near, far = dkv[0, 0], dkv[1, 0]
        put(
            dot(near[:, :local], x0[...])
            + dot(near[:, local:], x1[...])
            + dot(far[:, :local], x2[...])
            + dot(far[:, local:], x3[...])
        )

    for extra in small:
        keep_ref[:, :, unit:, :] = extra[0]
        send_ref[:, :, unit:, :] = extra[1]


def qkv_grads(core, dq, dkv, pieces, inner, outer, *small):
    count, width = pieces[0].shape
    group, full = dq.shape
    extra = sum(part.shape[3] for part in small)
    unit = width // (2 * inner * outer)
    once = pl.Buffered(1)
    whole = pl.BlockSpec((count, width), lambda t, core: (0, 0), pipeline_mode=once)
    out_spec = pl.BlockSpec((inner, outer, unit + extra, group), lambda t, core: (0, 0, 0, t))
    return pl.pallas_call(
        qkv_grads_kernel,
        grid_spec=pltpu.PrefetchScalarGridSpec(
            num_scalar_prefetch=1,
            grid=(3,),
            in_specs=[
                pl.BlockSpec((group, full), lambda t, core: (0, 0), pipeline_mode=once),
                pl.BlockSpec((2, 1, group, full), lambda t, core: (0, jnp.maximum(t - 1, 0), 0, 0)),
                whole,
                whole,
                whole,
                whole,
                *[pl.BlockSpec((2, inner, outer, extra, group), lambda t, core: (0, 0, 0, 0, t)) for _ in small],
            ],
            out_specs=[out_spec, out_spec],
        ),
        out_shape=[jax.ShapeDtypeStruct((inner, outer, unit + extra, 3 * group), BF16)] * 2,
        compiler_params=pltpu.CompilerParams(vmem_limit_bytes=VMEM_BYTES),
        cost_estimate=pl.CostEstimate(
            flops=10 * full * width * group, bytes_accessed=8 * full * width + 20 * full * group, transcendentals=0
        ),
        name="qkv_grads",
    )(core, dq, dkv, *pieces, *small)


def unpack_kernel(core, chip, moved, back_ref, in_ref, out_ref, qkv_ref, vec_ref, *, rows, parts):
    width = chip.shape[1]
    at = lambda slot, count=1: chip[slot * rows : (slot + count) * rows, :].astype(F32)
    back_ref[...] = at(0, parts)
    for j in range(parts):
        in_ref[:, j * width : (j + 1) * width] = at(parts + j)
    out_ref[...] = at(2 * parts)
    total = jnp.sum(moved[...].astype(F32), axis=0)
    vec_ref[...] = total[rows : rows + 8]
    half = total.shape[1] // 2
    firsts = at(2 * parts + 1), at(2 * parts + 2)
    seconds = total[:rows, :half], total[:rows, half:]
    wide, narrow = width // 3, half // 3
    for h in (0, 1):
        own = core[0] == h
        first = jnp.where(own, *firsts)
        second = jnp.where(own, *seconds)
        for t in range(3):
            start = (2 * t + h) * (wide + narrow)
            qkv_ref[:, start : start + wide] = first[:, t * wide : (t + 1) * wide]
            qkv_ref[:, start + wide : start + wide + narrow] = second[:, t * narrow : (t + 1) * narrow]


def unpack(core, chip, moved, rows, parts):
    width = chip.shape[1]
    whole = lambda a: pl.BlockSpec(a.shape, lambda i, core: (0,) * len(a.shape))
    outs = [
        jax.ShapeDtypeStruct(shape, F32)
        for shape in (
            (parts * rows, width),
            (rows, parts * width),
            (rows, width),
            (rows, 3 * width),
            (8, moved.shape[2]),
        )
    ]
    return pl.pallas_call(
        functools.partial(unpack_kernel, rows=rows, parts=parts),
        grid_spec=pltpu.PrefetchScalarGridSpec(
            num_scalar_prefetch=1,
            grid=(1,),
            in_specs=[whole(chip), whole(moved)],
            out_specs=[whole(a) for a in outs],
        ),
        out_shape=outs,
        name="unpack",
    )(core, chip, moved)


GATE = 4
SHARES = (20,)


def unpacked(blocks, parts):
    devices, size, width = blocks.shape
    rows = size // (2 * parts + 1)
    back = blocks[:, : parts * rows].reshape(devices * parts * rows, width)
    into = blocks[:, parts * rows : 2 * parts * rows].reshape(devices, parts, rows, width)
    into = into.transpose(0, 2, 1, 3).reshape(devices * rows, parts * width)
    return back, into, blocks[:, 2 * parts * rows :].reshape(devices * rows, width)


def packed(back, into, out, devices):
    rows, width = out.shape[0] // devices, out.shape[1]
    parts = back.shape[0] // out.shape[0]
    into = into.reshape(devices, rows, parts, width).transpose(0, 2, 1, 3)
    return jnp.concatenate(
        [a.reshape(devices, -1, width) for a in (back, into, out)], axis=1
    )


def dot_tn(a, b):
    return lax.dot_general(a, b, (((0,), (0,)), ((), ())), preferred_element_type=F32)


def per_device(
    tokens,
    lengths,
    pair_flip,
    w_qkv,
    q_bias,
    v_bias,
    w_out,
    out_bias,
    norm1_gain,
    norm1_shift,
    w_in,
    in_bias,
    w_back,
    back_bias,
    norm2_gain,
    norm2_shift,
    cotangent,
):
    both = ("head", "blk")
    cores = lax.axis_size("head")
    blocks = lax.axis_size("blk")
    core = lax.axis_index("head")
    block = lax.axis_index("blk")
    local, width = tokens.shape[1:]
    half = local * cores
    heads = HEADS // cores
    group = heads * HD
    ff = w_in.shape[1]
    parts = ff // width
    rows = w_qkv.shape[0]
    x = tokens[0]

    x_sib = swap(x, "head", 1)
    x_far = swap(x, "blk", 1)
    vectors = jnp.stack(
        [q_bias, v_bias, out_bias, back_bias, norm1_gain, norm1_shift, norm2_gain, norm2_shift], axis=0
    )
    extra = jnp.concatenate(
        [
            jnp.pad(vectors, ((0, 0), (0, LANES - rows))),
            jnp.pad(in_bias[None], ((0, 7), (0, 3 * group - LANES - parts * rows))),
        ],
        axis=1,
    )
    columns = w_qkv.reshape(rows, 3, cores, group)
    kept = lax.dynamic_index_in_dim(columns, core, 2, keepdims=False).reshape(rows, 3 * group)
    given = lax.dynamic_index_in_dim(columns, 1 - core, 2, keepdims=False).reshape(rows, 3 * group)
    mine = jnp.concatenate([kept, extra], axis=0)
    theirs = swap(jnp.concatenate([given, extra], axis=0), "head", 1)
    first, second, x_far = gather_blk(place(mine, theirs, core == 1, 0), x_far)
    small = jnp.concatenate([first[:, rows:, : 2 * LANES], second[:, rows:, : 2 * LANES]], axis=0)

    def vector(slot):
        if slot == 8:
            return small[:, 0, LANES : LANES + parts * rows].reshape(-1).astype(F32)
        return small[:, slot, :rows].reshape(-1).astype(F32)

    bias = jnp.concatenate(
        [
            lax.dynamic_slice_in_dim(vector(0), core * group, group),
            jnp.zeros((group,), F32),
            lax.dynamic_slice_in_dim(vector(1), core * group, group),
        ]
    )
    vec = jnp.concatenate(
        [
            vector(8)[None],
            jnp.pad(jnp.concatenate([vector(2), vector(3), vector(4), vector(5)]), (0, ff - 4 * width))[None],
            jnp.pad(jnp.concatenate([vector(6), vector(7)]), (0, ff - 2 * width))[None],
            jnp.zeros((5, ff), F32),
        ],
        axis=0,
    )

    shard = jnp.concatenate(
        [w_back, w_in.reshape(rows, parts, width).transpose(1, 0, 2).reshape(parts * rows, width), w_out], axis=0
    )
    if GATE in (1, 4):
        shard, x_far = lax.optimization_barrier((shard, x_far))
    elif GATE in (2, 6):
        shard, first = lax.optimization_barrier((shard, first))
    elif GATE == 3:
        shard, first, x_far = lax.optimization_barrier((shard, first, x_far))
    gathered = lax.all_gather(shard, both, axis=0, tiled=True).reshape(cores * blocks, -1, width)
    direct = rows % 8 == 0 and blocks % 4 == 0 and (2 * blocks) % (4 * parts) == 0
    if direct:
        inner, outer = 4, blocks // 4
    else:
        inner, outer = 4, 4
        gathered = packed(*unpacked(gathered, parts), cores * inner * outer)

    pieces = (x, x_sib, x_far, swap(x_far, "head", 1))
    bias = jnp.pad(bias[None], ((0, 7), (0, 0)))
    if direct:
        qkv, weight = project(pieces, first, second, bias)
    else:
        shape = (16, width // 32, 3 * group)
        qkv, weight = project(
            pieces, first[:, :rows].reshape(shape), second[:, :rows].reshape(shape), bias
        )

    sequence = block // 2
    own_half = block % 2
    length = lax.dynamic_index_in_dim(lengths, sequence, 0, keepdims=False)
    flags = lax.dynamic_index_in_dim(pair_flip, sequence, 0, keepdims=False)
    flags = lax.dynamic_slice_in_dim(flags, core * heads, heads)
    bounds = [jnp.clip(length - h * half, 0, half) for h in (own_half, 1 - own_half)]
    sc = jnp.concatenate([flags, jnp.stack(bounds + [jnp.int32(local), core])]).astype(jnp.int32)

    context, lse = attend(sc, qkv, group)
    other = swap(context[local:], "head", 1)
    at_core = core.reshape(1).astype(jnp.int32)
    out, grad_resid1, gc_own, gc_other, low, act, gh, gb, attn, sums = middle(
        at_core, x, context[:local], other, cotangent[0], gathered, vec
    )
    grad_context = jnp.concatenate([gc_own, swap(gc_other, "head", 1)], axis=0)

    keep, send = weight_grads(at_core, act, gb, low, gh, context[:local], other, attn, inner, outer)
    chip = (keep.astype(F32) + swap(send, "head", 1).astype(F32)).astype(BF16)
    grad_context, chip = lax.optimization_barrier((grad_context, chip))
    near_groups = [[o * inner + i for i in range(inner)] for o in range(outer)]
    far_groups = [[o * inner + i for o in range(outer)] for i in range(inner)]

    def over_plane(value):
        flat = value.reshape(-1, value.shape[3])
        flat = lax.psum_scatter(flat, "blk", scatter_dimension=0, axis_index_groups=near_groups, tiled=True)
        return flat.reshape(value.shape[1:])

    def over_column(value):
        flat = value.reshape(-1, value.shape[2])
        return lax.psum_scatter(flat, "blk", scatter_dimension=0, axis_index_groups=far_groups, tiled=True)

    if direct:
        chip = over_plane(chip.reshape(inner, outer, (2 * parts + 1) * rows, width))
    else:
        chip = chip.transpose(1, 0, 2, 3, 4).reshape(inner * outer, -1, width)
        chip = packed(*unpacked(chip, parts), blocks)
        chip = lax.psum_scatter(chip, "blk", scatter_dimension=0, tiled=True)[0]

    v_sums = place(
        sums[2, 2 * width : 2 * width + group], sums[2, 2 * width + group : 3 * width], core == 1, 0
    ).reshape(-1)
    by_rows = [v_sums] + [sums[1, s * width : (s + 1) * width] for s in range(4)]
    by_rows = jnp.stack(by_rows + [sums[2, s * width : (s + 1) * width] for s in range(2)], axis=0)
    by_rows = by_rows.reshape(7, cores, blocks, rows).transpose(1, 2, 0, 3).reshape(cores, blocks, -1)
    early_small = jnp.concatenate([by_rows, sums[0].reshape(cores, blocks, parts * rows)], axis=2)
    early_small, grad_context = lax.optimization_barrier((early_small, grad_context))

    def part_rows(dq, dkv, *small_rows):
        columns = 3 * dq.shape[0]
        keep, send = qkv_grads(at_core, dq, dkv, pieces, inner, outer, *(small_rows if direct else ()))
        if not direct:
            keep, send = (
                jnp.concatenate(
                    [a.transpose(1, 0, 2, 3).reshape(blocks, rows, columns)]
                    + [b[i].transpose(1, 0, 2, 3).reshape(blocks, -1, columns) for b in small_rows],
                    axis=1,
                )
                for i, a in enumerate((keep, send))
            )
        return keep, swap(send, "head", 1)

    def finish_part(keep, came):
        both_cores = jnp.concatenate([keep, came], axis=-1)
        if direct:
            both_cores = both_cores.transpose(1, 0, 2, 3).reshape((blocks,) + both_cores.shape[2:])
        return lax.all_to_all(both_cores, "blk", 0, 0, tiled=True)

    def total_of(moved):
        return jnp.sum(moved.astype(F32), axis=0).reshape(moved.shape[1], 2, -1)

    pairs = group // LANES
    first_pairs = pairs - pairs // 3
    dq_a, dkv_a, sum_a = attend_back(sc, qkv, context, lse, grad_context, group, 0, first_pairs)
    keep_a, came_a = part_rows(dq_a, dkv_a)
    if direct:
        part_a = jnp.concatenate([keep_a, came_a], axis=2)
        grad_context, part_a, chip = lax.optimization_barrier((grad_context, part_a, chip))
        chip = over_column(jnp.concatenate([chip, over_plane(part_a)], axis=1))
    else:
        total_a = total_of(finish_part(keep_a, came_a))
    dq_b, dkv_b, sum_b = attend_back(
        sc, qkv, context, lse, grad_context, group, first_pairs, pairs - first_pairs
    )

    q_sums = jnp.sum(jnp.concatenate([sum_a, sum_b], axis=0), axis=1)
    q_sums = lax.dynamic_update_slice_in_dim(jnp.zeros((width,), F32), q_sums, core * group, 0)
    grad_small = jnp.concatenate([q_sums.reshape(cores, blocks, rows), early_small], axis=2)
    room = 3 * (pairs - first_pairs) * LANES
    grad_small = jnp.pad(grad_small, ((0, 0), (0, 0), (0, room - grad_small.shape[2])))
    high = grad_small.astype(BF16)
    low_part = (grad_small - high.astype(F32)).astype(BF16)
    small_rows = jnp.pad(jnp.stack([high, low_part], axis=2), ((0, 0), (0, 0), (0, 6), (0, 0)))
    small_rows = jnp.where(core == 0, small_rows, small_rows[::-1])
    small_rows = small_rows.reshape(2, blocks // inner, inner, 8, room).transpose(0, 2, 1, 3, 4)

    dkv = (dkv_a, dkv_b)
    keep_far, send_far = far_rows(dkv, weight)
    far_sib = swap(send_far, "head", 1)
    cuts = [0, *(local * share // 32 for share in SHARES), local]
    far_sums = [
        (keep_far[lo:hi].astype(F32) + far_sib[lo:hi].astype(F32)).astype(BF16)
        for lo, hi in zip(cuts, cuts[1:])
    ]
    far_sums, dq_b = lax.optimization_barrier((far_sums, dq_b))
    far_in = [swap(part, "blk", 1) for part in far_sums]
    keep_b, came_b = part_rows(dq_b, dkv_b, small_rows)
    far_in[0], came_b = lax.optimization_barrier((far_in[0], came_b))
    moved_b = finish_part(keep_b, came_b)
    came_b, dq_a = lax.optimization_barrier((came_b, dq_a))
    keep_near, send_near = near_rows((dq_a, dq_b), dkv, weight, grad_resid1)
    chip, send_near = lax.optimization_barrier((chip, send_near))
    near_sib = swap(send_near, "head", 1)
    grad_tokens = keep_near + near_sib.astype(F32) + jnp.concatenate(far_in, axis=0).astype(F32)

    if direct:
        sum_wback, sum_win, sum_wout, sum_wqkv, vectors = unpack(at_core, chip, moved_b, rows, parts)
        vectors = vectors[0] + vectors[1]
        vectors = vectors[: vectors.shape[0] // 2] + vectors[vectors.shape[0] // 2 :]
    else:
        total_b = total_of(moved_b)
        sum_wback = chip[: parts * rows].astype(F32)
        sum_win = chip[parts * rows : 2 * parts * rows].astype(F32)
        sum_win = sum_win.reshape(parts, rows, width).transpose(1, 0, 2).reshape(rows, ff)
        sum_wout = chip[2 * parts * rows : (2 * parts + 1) * rows].astype(F32)

        def columns_of(total):
            own_w, other_w = (total[:rows, s].reshape(rows, 3, -1) for s in (0, 1))
            return place(own_w, other_w, core == 1, 2)

        sum_wqkv = jnp.concatenate([columns_of(total_a), columns_of(total_b)], axis=3).reshape(rows, 3 * width)
        vectors = jnp.sum(total_b[rows : rows + 2], axis=(0, 1))

    def summed(slot, size=rows):
        return vectors[slot * rows : slot * rows + size]

    return (
        out[None],
        grad_tokens[None],
        sum_wqkv,
        summed(0),
        summed(1),
        sum_wout,
        summed(2),
        summed(4),
        summed(5),
        sum_win,
        summed(8, parts * rows),
        sum_wback,
        summed(3),
        summed(6),
        summed(7),
    )


def solution(mesh):
    split = P(("head", "blk"))
    matrix = P(("head", "blk"), None)
    rows = P("blk", "head", None)
    return jax.shard_map(
        per_device,
        mesh=mesh,
        in_specs=(
            rows,
            P(),
            P(),
            matrix,
            split,
            split,
            matrix,
            split,
            split,
            split,
            matrix,
            split,
            matrix,
            split,
            split,
            split,
            rows,
        ),
        out_specs=(
            rows,
            rows,
            matrix,
            split,
            split,
            matrix,
            split,
            split,
            split,
            matrix,
            split,
            matrix,
            split,
            split,
            split,
        ),
        check_vma=False,
    )
```

```python
import functools

import jax
import jax.numpy as jnp
from jax import lax
from jax.experimental import pallas as pl
from jax.experimental.pallas import tpu as pltpu
from jax.sharding import PartitionSpec as P

HEADS = 12
HD = 64
LANES = 128
NEG = -1e30
EPS = 1e-06
SAFE_LOGIT = 60.0
BF16 = jnp.bfloat16
F32 = jnp.float32
NT = (((1,), (1,)), ((), ()))
VMEM_BYTES = 58 << 20


def dot(a, b):
    return jnp.dot(a, b, preferred_element_type=F32)


def dot_nt(a, b):
    return lax.dot_general(a, b, NT, preferred_element_type=F32)


def swap(value, axis, apart):
    pairs = [(source, source ^ apart) for source in range(lax.axis_size(axis))]
    return lax.ppermute(value, axis, pairs)


def place(mine, theirs, upper, axis):
    return jnp.stack([jnp.where(upper, theirs, mine), jnp.where(upper, mine, theirs)], axis=axis)


def gather_blk(pair, also):
    count = lax.axis_size("blk")
    index = lax.axis_index("blk")
    bits = [1 << b for b in range(count.bit_length() - 1)][::-1]
    held = pair
    depth = 1
    for bit in bits[:-2]:
        held = place(held, swap(held, "blk", bit), (index & bit) != 0, depth)
        depth += 1
    if GATE >= 4:
        held, also = lax.optimization_barrier((held, also))
    first, second = held[0], held[1]
    depth -= 1
    high, low = bits[-2], bits[-1]
    first_in = swap(first, "blk", high)
    second_in = swap(second, "blk", low)
    first = place(first, first_in, (index & high) != 0, depth)
    second = place(second, second_in, (index & low) != 0, depth)
    first_in = swap(first, "blk", low)
    second_in = swap(second, "blk", high)
    first = place(first, first_in, (index & low) != 0, depth + 1)
    second = place(second, second_in, (index & high) != 0, depth)
    return tuple(a.reshape((count,) + pair.shape[1:]) for a in (first, second)) + (also,)


def first_head(rows):
    lane = lax.broadcasted_iota(jnp.int32, (rows, LANES), 1)
    return lane < HD, lane % HD


def key_rows(own, sub, keys, row, sc, source, heads):
    at = lax.broadcasted_iota(jnp.int32, keys.shape, 0) + row
    bound, local, core = sc[heads + source], sc[heads + 2], sc[heads + 3]
    position = jnp.where(at < local, at + core * local, at - core * local)
    bias = jnp.where(position < bound, 0.0, NEG)
    extra = jnp.where(sub < 3, -1.0, jnp.where(sub == 3, bias, 0.0))
    return jnp.where(own, keys.astype(F32), extra).astype(BF16)


def three_parts(value):
    first = value.astype(BF16).astype(F32)
    rest = value - first
    second = rest.astype(BF16).astype(F32)
    return first, second, rest - second


def attend_kernel(
    sc, q_ref, ka_ref, kb_ref, va_ref, vb_ref, own_ref, sib_ref, lse_ref, keys, values, key_norm, *, heads, step
):
    pair = pl.program_id(0)
    count = keys.shape[1]
    rows = q_ref.shape[1]
    scale = HD ** (-0.5)

    @pl.when(pl.program_id(1) == 0)
    def _():
        piece = min(512, count)
        own0, sub = first_head(piece)
        for h, (k_ref, v_ref) in enumerate(((ka_ref, va_ref), (kb_ref, vb_ref))):
            source = sc[2 * pair + h]
            own = own0 if h == 0 else jnp.logical_not(own0)
            largest = jnp.float32(0.0)
            for r in range(0, count, piece):
                k = k_ref[0, r : r + piece, :]
                keys[h, r : r + piece, :] = key_rows(own, sub, k, r, sc, source, heads)
                values[h, :HD, r : r + piece] = v_ref[0, r : r + piece, :].T[h * HD : (h + 1) * HD, :]
                values[h, HD:, r : r + piece] = jnp.ones((16, piece), BF16)
                k = jnp.where(own, k.astype(F32), 0.0)
                largest = jnp.maximum(largest, jnp.max(jnp.sum(k * k, axis=1, keepdims=True)))
            key_norm[h] = largest

    q = q_ref[0].astype(F32) * scale
    own0, sub = first_head(rows)
    one = jnp.where(sub == 3, 1.0, 0.0)
    square = q * q
    norm_a = jnp.max(jnp.sum(jnp.where(own0, square, 0.0), axis=1, keepdims=True))
    norm_b = jnp.max(jnp.sum(jnp.where(own0, 0.0, square), axis=1, keepdims=True))
    largest = jnp.maximum(norm_a * key_norm[0], norm_b * key_norm[1])
    small = largest < SAFE_LOGIT * SAFE_LOGIT

    def queries(h):
        return (jnp.where(own0, q, one) if h == 0 else jnp.where(own0, one, q)).astype(BF16)

    def finish(outs, peaks):
        totals = [jnp.broadcast_to(o[HD : HD + 1, :], (HD, rows)) for o in outs]
        out = jnp.concatenate([o[:HD, :] / t for o, t in zip(outs, totals)], axis=0).T.astype(BF16)
        mine = pl.program_id(1) < pl.num_programs(1) // 2

        @pl.when(mine)
        def _():
            own_ref[...] = out

        @pl.when(jnp.logical_not(mine))
        def _():
            sib_ref[...] = out

        lse = jnp.concatenate([jnp.log(totals[1]), jnp.log(totals[0])], axis=0).T
        if peaks is not None:
            lse = lse + jnp.where(own0, peaks[1], peaks[0])
        lse_ref[...] = lse

    @pl.when(small)
    def _():
        outs = []
        for h in (0, 1):
            qa = queries(h)
            out = None
            for c in range(0, count, step):
                p = jnp.exp(dot_nt(qa, keys[h, c : c + step, :])).astype(BF16)
                part = dot_nt(values[h, :, c : c + step], p)
                out = part if out is None else out + part
            outs.append(out)
        finish(outs, None)

    @pl.when(jnp.logical_not(small))
    def _():
        outs, peaks = [], []
        for h in (0, 1):
            s = dot_nt(queries(h), keys[h])
            peak = jnp.max(s, axis=1, keepdims=True)
            outs.append(dot_nt(values[h], jnp.exp(s - peak).astype(BF16)))
            peaks.append(peak)
        finish(outs, peaks)


def pair_specs(count, width, skip=0):
    pairs = width // LANES

    def key_value(h, base):
        return pl.BlockSpec((1, count, LANES), lambda p, i, sc: (sc[2 * (p + skip) + h], 0, base * pairs + p + skip))

    return [key_value(0, 1), key_value(1, 1), key_value(0, 2), key_value(1, 2)]


def halves_specs(rows, blocks, skip=0):
    first = pl.BlockSpec((rows, LANES), lambda p, i, sc: (jnp.minimum(i, blocks // 2 - 1), p + skip))
    return [first, pl.BlockSpec((rows, LANES), lambda p, i, sc: (jnp.maximum(i - blocks // 2, 0), p + skip))]


def attend(sc, qkv, width):
    count = qkv.shape[1]
    rows = min(1024, count // 2)
    row_spec = pl.BlockSpec((rows, LANES), lambda p, i, sc: (i, p))
    q_spec = pl.BlockSpec((1, rows, LANES), lambda p, i, sc: (0, i, p))
    heads = width // HD
    return pl.pallas_call(
        functools.partial(attend_kernel, heads=heads, step=min(512, count)),
        grid_spec=pltpu.PrefetchScalarGridSpec(
            num_scalar_prefetch=1,
            grid=(width // LANES, count // rows),
            in_specs=[q_spec] + pair_specs(count, width),
            out_specs=halves_specs(rows, count // rows) + [row_spec],
            scratch_shapes=[
                pltpu.VMEM((2, count, LANES), BF16),
                pltpu.VMEM((2, HD + 16, count), BF16),
                pltpu.SMEM((2,), F32),
            ],
        ),
        out_shape=[
            jax.ShapeDtypeStruct((count // 2, width), BF16),
            jax.ShapeDtypeStruct((count // 2, width), BF16),
            jax.ShapeDtypeStruct((count, width), F32),
        ],
        compiler_params=pltpu.CompilerParams(vmem_limit_bytes=VMEM_BYTES),
        cost_estimate=pl.CostEstimate(
            flops=4 * 4 * count * count * width, bytes_accessed=2 * 6 * count * width, transcendentals=0
        ),
        name="attend",
    )(sc, qkv, qkv, qkv, qkv, qkv)


def attend_back_kernel(
    sc,
    q_ref,
    ka_ref,
    kb_ref,
    va_ref,
    vb_ref,
    o_own,
    o_sib,
    do_own,
    do_sib,
    lse_ref,
    x0,
    x1,
    x2,
    x3,
    dq_ref,
    dkv_ref,
    sum_ref,
    keep_ref,
    send_ref,
    keys,
    keys_t,
    values,
    dk_sum,
    dv_sum,
    dq_all,
    *,
    heads,
    step,
    skip,
):
    pair = pl.program_id(0) + skip
    block = pl.program_id(1)
    count = keys.shape[1]
    rows = q_ref.shape[1]
    scale = HD ** (-0.5)

    @pl.when(block == 0)
    def _():
        piece = min(512, count)
        own0, sub = first_head(piece)
        for h, (k_ref, v_ref) in enumerate(((ka_ref, va_ref), (kb_ref, vb_ref))):
            source = sc[2 * pair + h]
            own = own0 if h == 0 else jnp.logical_not(own0)
            for r in range(0, count, piece):
                k = k_ref[0, r : r + piece, :]
                keys[h, r : r + piece, :] = key_rows(own, sub, k, r, sc, source, heads)
                keys_t[h, :, r : r + piece] = k.T[h * HD : (h + 1) * HD, :]
                v = v_ref[0, r : r + piece, :].astype(F32)
                values[h, r : r + piece, :] = jnp.where(own, v, 1.0).astype(BF16)
        sum_ref[...] = jnp.zeros_like(sum_ref)
        dk_sum[...] = jnp.zeros_like(dk_sum)
        dv_sum[...] = jnp.zeros_like(dv_sum)

    q = q_ref[0]
    mine = block < pl.num_programs(1) // 2
    do = jnp.where(mine, do_own[...], do_sib[...])
    out = jnp.where(mine, o_own[...], o_sib[...])
    own0, sub = first_head(rows)
    qf = q.astype(F32) * scale
    first, second, third = three_parts(lse_ref[...])
    q_extra = jnp.where(
        sub == 0, first, jnp.where(sub == 1, second, jnp.where(sub == 2, third, jnp.where(sub == 3, 1.0, 0.0)))
    )
    dof = do.astype(F32)
    product = dof * out.astype(F32)
    inner_a = jnp.sum(jnp.where(own0, product, 0.0), axis=1, keepdims=True)
    inner_b = jnp.sum(jnp.where(own0, 0.0, product), axis=1, keepdims=True)
    first, second, third = three_parts(jnp.where(own0, -inner_b, -inner_a))
    do_extra = jnp.where(sub == 0, first, jnp.where(sub == 1, second, jnp.where(sub == 2, third, 0.0)))
    q_t = q.T
    do_t = do.T
    grads = []
    for h in (0, 1):
        qa = (jnp.where(own0, qf, q_extra) if h == 0 else jnp.where(own0, q_extra, qf)).astype(BF16)
        da = (jnp.where(own0, dof, do_extra) if h == 0 else jnp.where(own0, do_extra, dof)).astype(BF16)
        own_rows = slice(h * HD, (h + 1) * HD)
        dq = None
        for c in range(0, count, step):
            part = slice(c, c + step)
            p = jnp.exp(dot_nt(qa, keys[h, part, :]))
            ds = (p * dot_nt(da, values[h, part, :])).astype(BF16)
            p = p.astype(BF16)
            t = dot_nt(keys_t[h, :, part], ds)
            dq = t if dq is None else dq + t
            dk_sum[own_rows, part] += dot(q_t[own_rows, :], ds)
            dv_sum[own_rows, part] += dot(do_t[own_rows, :], p)
        grads.append(dq)
    dq = (jnp.concatenate(grads, axis=0) * scale).astype(BF16)
    dq_ref[...] = dq
    for i in range(count // rows):

        @pl.when(block == i)
        def _():
            dq_all[:, i * rows : (i + 1) * rows] = dq

    for c in range(0, rows, LANES):
        sum_ref[...] += dq[:, c : c + LANES].astype(F32)

    @pl.when(block == pl.num_programs(1) - 1)
    def _():
        for h in (0, 1):
            source = sc[2 * pair + h]
            own_rows = slice(h * HD, (h + 1) * HD)
            dk = dk_sum[own_rows, :] * scale
            dv = dv_sum[own_rows, :]
            for half in (0, 1):
                here = source == half
                dkv_ref[half, 0, own_rows, :] = jnp.where(here, dk, 0.0).astype(BF16)
                dkv_ref[half, 1, own_rows, :] = jnp.where(here, dv, 0.0).astype(BF16)

        local = x0.shape[0]
        near = jnp.concatenate([dq_all[...], dkv_ref[0, 0], dkv_ref[0, 1]], axis=0)
        far = jnp.concatenate([dkv_ref[1, 0], dkv_ref[1, 1]], axis=0)
        near = dot(near[:, :local], x0[...]) + dot(near[:, local:], x1[...])
        far = dot(far[:, :local], x2[...]) + dot(far[:, local:], x3[...])
        grad = jnp.concatenate([near[:LANES], near[LANES:] + far], axis=0).T.astype(BF16)
        inner, outer, unit, _ = keep_ref.shape
        half_rows = grad.shape[0] // 2
        for c in (0, 1):
            part = grad[c * half_rows : (c + 1) * half_rows].reshape(outer, inner, unit, 3 * LANES)
            core = sc[heads + 3]

            @pl.when(core == c)
            def _():
                for o in range(outer):
                    keep_ref[:, o] = part[o]

            @pl.when(core != c)
            def _():
                for o in range(outer):
                    send_ref[:, o] = part[o]


def attend_back(sc, qkv, contexts, lse, grads, pieces, width, skip, pairs, inner, outer):
    model = pieces[0].shape[1]
    unit = model // (2 * inner * outer)
    piece = pl.BlockSpec(pieces[0].shape, lambda p, i, sc: (0, 0), pipeline_mode=pl.Buffered(1))
    grad_spec = pl.BlockSpec((inner, outer, unit, 3 * LANES), lambda p, i, sc: (0, 0, 0, p))
    grad_shape = jax.ShapeDtypeStruct((inner, outer, unit, 3 * pairs * LANES), BF16)
    count = qkv.shape[1]
    rows = min(1024, count // 2)
    row_spec = pl.BlockSpec((rows, LANES), lambda p, i, sc: (i, p + skip))
    q_spec = pl.BlockSpec((1, rows, LANES), lambda p, i, sc: (0, i, p + skip))
    dq_spec = pl.BlockSpec((LANES, rows), lambda p, i, sc: (p, i))
    dkv_spec = pl.BlockSpec((2, 2, LANES, count), lambda p, i, sc: (0, 0, p, 0))
    heads = width // HD
    return pl.pallas_call(
        functools.partial(attend_back_kernel, heads=heads, step=min(512, count), skip=skip),
        grid_spec=pltpu.PrefetchScalarGridSpec(
            num_scalar_prefetch=1,
            grid=(pairs, count // rows),
            in_specs=[q_spec] + pair_specs(count, width, skip) + halves_specs(rows, count // rows, skip) * 2
            + [row_spec]
            + [piece] * 4,
            out_specs=[
                dq_spec,
                dkv_spec,
                pl.BlockSpec((LANES, LANES), lambda p, i, sc: (p, 0)),
                grad_spec,
                grad_spec,
            ],
            scratch_shapes=[
                pltpu.VMEM((2, count, LANES), BF16),
                pltpu.VMEM((2, HD, count), BF16),
                pltpu.VMEM((2, count, LANES), BF16),
                pltpu.VMEM((LANES, count), F32),
                pltpu.VMEM((LANES, count), F32),
                pltpu.VMEM((LANES, count), BF16),
            ],
        ),
        out_shape=[
            jax.ShapeDtypeStruct((pairs * LANES, count), BF16),
            jax.ShapeDtypeStruct((2, 2, pairs * LANES, count), BF16),
            jax.ShapeDtypeStruct((pairs * LANES, LANES), F32),
            grad_shape,
            grad_shape,
        ],
        compiler_params=pltpu.CompilerParams(vmem_limit_bytes=VMEM_BYTES),
        cost_estimate=pl.CostEstimate(
            flops=10 * 4 * count * count * pairs * LANES, bytes_accessed=2 * 12 * count * pairs * LANES, transcendentals=0
        ),
        name="attend_back",
    )(sc, qkv, qkv, qkv, qkv, qkv, *contexts, *grads, lse, *pieces)


def mean_of(value):
    return jnp.mean(value, axis=-1, keepdims=True)


def norm_of(value):
    center = value - mean_of(value)
    inverse = lax.rsqrt(mean_of(center * center) + EPS)
    return center * inverse, inverse


def norm_back(grad, normed, inverse, gain):
    dn = grad * gain
    return inverse * (dn - mean_of(dn) - normed * mean_of(dn * normed))


def sum_rows(value):
    return jnp.sum(value, axis=0, keepdims=True)


def middle_kernel(
    core,
    x_ref,
    own_ref,
    other_ref,
    cot_ref,
    wo_own_ref,
    wo_other_ref,
    *refs,
    width,
    ff,
):
    chunk = width
    parts = ff // width
    w_in_refs = refs[:parts]
    (
        w_back_ref,
        vec,
        out_ref,
        resid_ref,
        gc_own,
        gc_other,
        low_ref,
        act_ref,
        gh_ref,
        gb_ref,
        attn_ref,
        sums,
        slope,
        wo_own,
        wo_other,
        w_in,
        w_back,
    ) = refs[parts:]
    in_bias = lambda c: vec[0:1, c : c + chunk]
    row = lambda r, s: vec[r : r + 1, s * width : (s + 1) * width]
    out_bias, back_bias, gain1, shift1 = (row(1, s) for s in range(4))
    gain2, shift2 = row(2, 0), row(2, 1)

    @pl.when(pl.program_id(0) == 0)
    def _():
        sums[...] = jnp.zeros_like(sums)
        wo_own[...] = wo_own_ref[...].reshape(wo_own.shape)
        wo_other[...] = wo_other_ref[...].reshape(wo_other.shape)
        for j in range(parts):
            w_in[j] = w_in_refs[j][...].reshape(w_in.shape[1:])
        devices, rows = w_back_ref.shape[:2]
        some = devices // parts
        for j in range(parts):
            w_back[j] = w_back_ref[j * some : (j + 1) * some].reshape(some * rows, width)

    attended = dot(own_ref[...], wo_own[...]) + dot(other_ref[...], wo_other[...]) + out_bias
    hat1, inverse1 = norm_of(x_ref[...].astype(F32) + attended)
    normed = hat1 * gain1 + shift1
    low = normed.astype(BF16)
    low_ref[...] = low
    branch = None
    for c in range(0, ff, chunk):
        hidden = dot(low, w_in[c // chunk]) + in_bias(c)
        cumulative = 0.5 * (1.0 + lax.erf(hidden * 0.7071067811865476))
        density = 0.3989422804014327 * jnp.exp(-0.5 * hidden * hidden)
        slope[:, c : c + chunk] = cumulative + hidden * density
        act = (hidden * cumulative).astype(BF16)
        act_ref[:, c : c + chunk] = act
        part = dot(act, w_back[c // chunk])
        branch = part if branch is None else branch + part
    hat2, inverse2 = norm_of(normed + (branch + back_bias))
    out_ref[...] = (hat2 * gain2 + shift2).astype(BF16)
    cot = cot_ref[...].astype(F32)
    grad2 = norm_back(cot, hat2, inverse2, gain2)
    gb = grad2.astype(BF16)
    gb_ref[...] = gb
    grad_normed = grad2
    for c in range(0, ff, chunk):
        gh = (dot_nt(gb, w_back[c // chunk]) * slope[:, c : c + chunk]).astype(BF16)
        gh_ref[:, c : c + chunk] = gh
        sums[0:1, c : c + chunk] += sum_rows(gh.astype(F32))
        grad_normed = grad_normed + dot_nt(gh, w_in[c // chunk])
    grad1 = norm_back(grad_normed, hat1, inverse1, gain1)
    resid_ref[...] = grad1
    attn = grad1.astype(BF16)
    attn_ref[...] = attn
    gc_own[...] = dot_nt(attn, wo_own[...]).astype(BF16)
    gc_other[...] = dot_nt(attn, wo_other[...]).astype(BF16)
    at = lambda r, s, v: sums.__setitem__(
        (slice(r, r + 1), slice(s * width, (s + 1) * width)),
        sums[r : r + 1, s * width : (s + 1) * width] + sum_rows(v),
    )
    at(1, 0, attn.astype(F32))
    at(1, 1, gb.astype(F32))
    at(1, 2, grad_normed * hat1)
    at(1, 3, grad_normed)
    at(2, 0, cot * hat2)
    at(2, 1, cot)
    for s, ref in enumerate((gc_own, gc_other)):
        half = ref.shape[1]
        lane = slice(2 * width + s * half, 2 * width + (s + 1) * half)
        sums[2:3, lane] += sum_rows(ref[...].astype(F32))


def middle(core, x, own, other, cot, weights, vec):
    count, width = x.shape
    ff = vec.shape[1]
    parts = ff // width
    devices = weights.shape[0]
    unit = width // devices
    once = pl.Buffered(1)
    half_spec = lambda at: pl.BlockSpec(
        (devices // 2, unit, width), lambda i, core: (at(core[0]), 2 * parts, 0), pipeline_mode=once
    )
    in_spec = lambda j: pl.BlockSpec(
        (devices, unit, width), lambda i, core: (0, parts + j, 0), pipeline_mode=once
    )
    half = own.shape[1]
    rows = min(256, count)
    tile = lambda w: pl.BlockSpec((rows, w), lambda i, core: (i, 0))
    whole = lambda a: pl.BlockSpec(a.shape, lambda i, core: (0, 0), pipeline_mode=once)
    return pl.pallas_call(
        functools.partial(middle_kernel, width=width, ff=ff),
        grid_spec=pltpu.PrefetchScalarGridSpec(
            num_scalar_prefetch=1,
            grid=(count // rows,),
            in_specs=[
                tile(width),
                tile(half),
                tile(half),
                tile(width),
                half_spec(lambda c: c),
                half_spec(lambda c: 1 - c),
                *[in_spec(j) for j in range(parts)],
                pl.BlockSpec((devices, parts * unit, width), lambda i, core: (0, 0, 0), pipeline_mode=once),
                whole(vec),
            ],
            out_specs=[
                tile(width),
                tile(width),
                tile(half),
                tile(half),
                tile(width),
                tile(ff),
                tile(ff),
                tile(width),
                tile(width),
                pl.BlockSpec((8, ff), lambda i, core: (0, 0)),
            ],
            scratch_shapes=[
                pltpu.VMEM((rows, ff), F32),
                pltpu.VMEM((half, width), BF16),
                pltpu.VMEM((half, width), BF16),
                pltpu.VMEM((parts, width, width), BF16),
                pltpu.VMEM((parts, width, width), BF16),
            ],
        ),
        out_shape=[
            jax.ShapeDtypeStruct((count, width), BF16),
            jax.ShapeDtypeStruct((count, width), F32),
            jax.ShapeDtypeStruct((count, half), BF16),
            jax.ShapeDtypeStruct((count, half), BF16),
            jax.ShapeDtypeStruct((count, width), BF16),
            jax.ShapeDtypeStruct((count, ff), BF16),
            jax.ShapeDtypeStruct((count, ff), BF16),
            jax.ShapeDtypeStruct((count, width), BF16),
            jax.ShapeDtypeStruct((count, width), BF16),
            jax.ShapeDtypeStruct((8, ff), F32),
        ],
        compiler_params=pltpu.CompilerParams(vmem_limit_bytes=VMEM_BYTES),
        cost_estimate=pl.CostEstimate(
            flops=2 * count * width * (4 * ff + 2 * width), bytes_accessed=2 * (4 * width * ff + 2 * count * ff + 8 * count * width), transcendentals=0
        ),
        name="middle",
    )(core, x, own, other, cot, *([weights] * (3 + parts)), vec)


def dot_tn(a, b):
    return lax.dot_general(a, b, (((0,), (0,)), ((), ())), preferred_element_type=F32)


def back_grads_kernel(core, act, gb, *refs):
    *came, out_ref = refs
    inner, span, parts, unit, width = out_ref.shape
    got = dot_tn(act[...], gb[...]).reshape(span, inner, parts, unit, width)
    for o in range(span):
        mine = got[o]
        for ref in came:
            mine = mine + ref[:, o].astype(F32)
        out_ref[:, o] = mine.astype(BF16)


def in_grads_kernel(core, low, gh, context, attn, *refs, parts):
    *came, out_ref = refs
    came = came[:1]
    inner, outer, _, unit, width = out_ref.shape

    def put(value):
        value = value.reshape(outer, inner, unit, width)
        for o in range(outer):
            mine = value[o]
            for ref in came:
                mine = mine + ref[:, o, 0].astype(F32)
            out_ref[:, o, 0] = mine.astype(BF16)

    @pl.when(pl.program_id(0) < parts)
    def _():
        put(dot_tn(low[...], gh[...]))

    @pl.when(pl.program_id(0) == parts)
    def _():
        put(dot_tn(context[...], attn[...]))


def weight_grads(core, act, gb, low, gh, own, other, attn, inner, outer):
    count, width = low.shape
    parts = act.shape[1] // width
    unit = width // (2 * inner * outer)
    tiles = parts // 2
    span = outer // tiles
    once = pl.Buffered(1)
    whole = pl.BlockSpec((count, width), lambda t, core: (0, 0), pipeline_mode=once)
    anywhere = pl.BlockSpec(memory_space=pl.ANY)

    def call(kernel, tiles, in_specs, out_spec, slots, args, came, aliases, flops):
        return pl.pallas_call(
            kernel,
            grid_spec=pltpu.PrefetchScalarGridSpec(
                num_scalar_prefetch=1, grid=(tiles,), in_specs=in_specs, out_specs=out_spec
            ),
            out_shape=jax.ShapeDtypeStruct((inner, outer, slots, unit, width), BF16),
            input_output_aliases=aliases,
            compiler_params=pltpu.CompilerParams(vmem_limit_bytes=VMEM_BYTES),
            cost_estimate=pl.CostEstimate(flops=flops, bytes_accessed=3 * flops // width, transcendentals=0),
            name="weight_grads",
        )(core, *args, *came)

    def back(pick, slots, came):
        spec = pl.BlockSpec((inner, span, parts, unit, width), lambda t, core: (0, t, 0, 0, 0))
        tile = pl.BlockSpec((count, width), lambda t, core: (0, tiles * pick(core[0]) + t))
        return call(
            back_grads_kernel,
            tiles,
            [tile, whole] + [spec] * len(came),
            spec,
            slots,
            (act, gb),
            came,
            {},
            count * width * width * parts,
        )

    def into(pick, context, skip, came, base):
        spec = lambda skip: pl.BlockSpec((inner, outer, 1, unit, width), lambda t, core: (0, 0, t + skip, 0, 0))
        half = context.shape[1]
        return call(
            functools.partial(in_grads_kernel, parts=parts),
            parts + 1,
            [
                pl.BlockSpec((count, half), lambda t, core: (0, pick(core[0])), pipeline_mode=once),
                pl.BlockSpec((count, width), lambda t, core: (0, jnp.minimum(t, parts - 1))),
                pl.BlockSpec((count, half), lambda t, core: (0, 0), pipeline_mode=once),
                whole,
            ]
            + [spec(0)] * len(came)
            + [anywhere] * len(base),
            spec(skip),
            skip + parts + 1,
            (low, gh, context, attn),
            came + base,
            {6: 0} if base else {},
            count * width * width * (parts + 1),
        )

    mine, theirs = (lambda c: c), (lambda c: 1 - c)
    sent = back(theirs, parts, ())
    sent, low, act = lax.optimization_barrier((sent, low, act))
    back_came = swap(sent, "head", 1)
    in_sent = into(theirs, other, 0, (), ())
    back_came, in_sent, act = lax.optimization_barrier((back_came, in_sent, act))
    in_came = swap(in_sent, "head", 1)
    kept = back(mine, 2 * parts + 1, (back_came,))
    return into(mine, own, parts, (in_came,), (kept,))


def project_kernel(x0, x1, x2, x3, first, second, bias, out_ref, weight_ref, *, group):
    step = pl.program_id(0)
    blocks, width = pl.num_programs(0) // 4, x0.shape[1]
    rows = first.shape[0] * (weight_ref.shape[0] // first.shape[0] // 2)

    @pl.when(step == 0)
    def _():
        unit = weight_ref.shape[0] // (2 * first.shape[0])
        weight_ref[:rows, :] = first[:, :unit, :].reshape(rows, 3 * group)
        weight_ref[rows:, :] = second[:, :unit, :].reshape(rows, 3 * group)

    for p, ref in enumerate((x0, x1, x2, x3)):

        @pl.when(step // blocks == p)
        def _():
            start = 0 if p < 2 else group
            got = dot(ref[...], weight_ref[:, start:]) + bias[0:1, start:]
            out_ref[0, :, start:] = got.astype(BF16)


def project(pieces, first, second, bias):
    count, width = pieces[0].shape
    wide = first.shape[2]
    rows = min(512, count)
    blocks = count // rows
    once = pl.Buffered(1)
    piece = lambda p: pl.BlockSpec((rows, width), lambda i: (jnp.clip(i - p * blocks, 0, blocks - 1), 0))
    whole = lambda a: pl.BlockSpec(a.shape, lambda i: (0,) * a.ndim, pipeline_mode=once)
    return pl.pallas_call(
        functools.partial(project_kernel, group=wide // 3),
        grid=(4 * blocks,),
        in_specs=[piece(p) for p in range(4)] + [whole(first), whole(second), whole(bias)],
        out_specs=[
            pl.BlockSpec((1, rows, wide), lambda i: (i // (2 * blocks), i % (2 * blocks), 0)),
            pl.BlockSpec((width, wide), lambda i: (0, 0)),
        ],
        out_shape=[
            jax.ShapeDtypeStruct((2, 2 * count, wide), BF16),
            jax.ShapeDtypeStruct((width, wide), BF16),
        ],
        compiler_params=pltpu.CompilerParams(vmem_limit_bytes=VMEM_BYTES),
        cost_estimate=pl.CostEstimate(
            flops=2 * 4 * count * width * wide, bytes_accessed=8 * count * (width + wide), transcendentals=0
        ),
        name="project",
    )(*pieces, first, second, bias)


def stacked(refs, which):
    return jnp.concatenate([ref[0, kind] for kind in which for ref in refs], axis=0).T


def far_rows_kernel(*refs, group):
    *dkv, weight, keep_ref, send_ref = refs
    step = pl.program_id(0)
    got = dot_nt(stacked(dkv, (0, 1)), weight[:, group:]).astype(BF16)

    @pl.when(step < pl.num_programs(0) // 2)
    def _():
        keep_ref[...] = got

    @pl.when(step >= pl.num_programs(0) // 2)
    def _():
        send_ref[...] = got


def dkv_spec(part, rows, source):
    return pl.BlockSpec((1, 2, part.shape[2], rows), lambda i: (source, 0, 0, i))


def far_rows(dkv, weight):
    count, (width, wide) = dkv[0].shape[3], weight.shape
    rows = min(512, count // 2)
    blocks = count // rows
    return pl.pallas_call(
        functools.partial(far_rows_kernel, group=wide // 3),
        grid=(blocks,),
        in_specs=[dkv_spec(part, rows, 1) for part in dkv]
        + [pl.BlockSpec((width, wide), lambda i: (0, 0), pipeline_mode=pl.Buffered(1))],
        out_specs=[
            pl.BlockSpec((rows, width), lambda i: (jnp.minimum(i, blocks // 2 - 1), 0)),
            pl.BlockSpec((rows, width), lambda i: (jnp.maximum(i - blocks // 2, 0), 0)),
        ],
        out_shape=[jax.ShapeDtypeStruct((count // 2, width), BF16)] * 2,
        compiler_params=pltpu.CompilerParams(vmem_limit_bytes=VMEM_BYTES),
        cost_estimate=pl.CostEstimate(
            flops=2 * count * width * wide * 2 // 3, bytes_accessed=8 * count * width, transcendentals=0
        ),
        name="far_rows",
    )(*dkv, weight)


def near_rows_kernel(*refs, parts, group):
    dq, dkv = refs[:parts], refs[parts : 2 * parts]
    weight, resid, keep_ref, send_ref = refs[2 * parts :]
    step = pl.program_id(0)
    queries = jnp.concatenate([ref[...] for ref in dq], axis=0).T
    got = dot_nt(queries, weight[:, :group]) + dot_nt(stacked(dkv, (0, 1)), weight[:, group:])

    @pl.when(step < pl.num_programs(0) // 2)
    def _():
        keep_ref[...] = got + resid[...]

    @pl.when(step >= pl.num_programs(0) // 2)
    def _():
        send_ref[...] = got.astype(BF16)


def near_rows(dq, dkv, weight, resid):
    count, (width, wide) = dkv[0].shape[3], weight.shape
    rows = min(512, count // 2)
    blocks = count // rows
    return pl.pallas_call(
        functools.partial(near_rows_kernel, parts=len(dq), group=wide // 3),
        grid=(blocks,),
        in_specs=[pl.BlockSpec((part.shape[0], rows), lambda i: (0, i)) for part in dq]
        + [dkv_spec(part, rows, 0) for part in dkv]
        + [
            pl.BlockSpec((width, wide), lambda i: (0, 0), pipeline_mode=pl.Buffered(1)),
            pl.BlockSpec((rows, width), lambda i: (jnp.minimum(i, blocks // 2 - 1), 0)),
        ],
        out_specs=[
            pl.BlockSpec((rows, width), lambda i: (jnp.minimum(i, blocks // 2 - 1), 0)),
            pl.BlockSpec((rows, width), lambda i: (jnp.maximum(i - blocks // 2, 0), 0)),
        ],
        out_shape=[
            jax.ShapeDtypeStruct((count // 2, width), F32),
            jax.ShapeDtypeStruct((count // 2, width), BF16),
        ],
        compiler_params=pltpu.CompilerParams(vmem_limit_bytes=VMEM_BYTES),
        cost_estimate=pl.CostEstimate(
            flops=2 * count * width * wide, bytes_accessed=12 * count * width, transcendentals=0
        ),
        name="near_rows",
    )(*dq, *dkv, weight, resid)


def unpack_kernel(core, chip, moved, back_ref, in_ref, out_ref, qkv_ref, vec_ref, *, rows, parts):
    width = chip.shape[1]
    at = lambda slot, count=1: chip[slot * rows : (slot + count) * rows, :].astype(F32)
    back_ref[...] = at(0, parts)
    for j in range(parts):
        in_ref[:, j * width : (j + 1) * width] = at(parts + j)
    out_ref[...] = at(2 * parts)
    total = jnp.sum(moved[...].astype(F32), axis=0)
    vec_ref[...] = total[rows : rows + 8]
    half = total.shape[1] // 2
    firsts = at(2 * parts + 1), at(2 * parts + 2)
    seconds = total[:rows, :half], total[:rows, half:]
    block = half // 3
    for h in (0, 1):
        own = core[0] == h
        first = jnp.where(own, *firsts)
        second = jnp.where(own, *seconds)
        early = width // half
        for t in range(3):
            for p in range(early + 1):
                start = ((2 * t + h) * (early + 1) + p) * block
                source, at_pair = (first, p) if p < early else (second, 0)
                lane = (3 * at_pair + t) * block
                qkv_ref[:, start : start + block] = source[:, lane : lane + block]


def unpack(core, chip, moved, rows, parts):
    width = chip.shape[1]
    whole = lambda a: pl.BlockSpec(a.shape, lambda i, core: (0,) * len(a.shape))
    outs = [
        jax.ShapeDtypeStruct(shape, F32)
        for shape in (
            (parts * rows, width),
            (rows, parts * width),
            (rows, width),
            (rows, 3 * width),
            (8, moved.shape[2]),
        )
    ]
    return pl.pallas_call(
        functools.partial(unpack_kernel, rows=rows, parts=parts),
        grid_spec=pltpu.PrefetchScalarGridSpec(
            num_scalar_prefetch=1,
            grid=(1,),
            in_specs=[whole(chip), whole(moved)],
            out_specs=[whole(a) for a in outs],
        ),
        out_shape=outs,
        name="unpack",
    )(core, chip, moved)


GATE = 4
SHARES = (21,)
ORDER = 0


def unpacked(blocks, parts):
    devices, size, width = blocks.shape
    rows = size // (2 * parts + 1)
    back = blocks[:, : parts * rows].reshape(devices * parts * rows, width)
    into = blocks[:, parts * rows : 2 * parts * rows].reshape(devices, parts, rows, width)
    into = into.transpose(0, 2, 1, 3).reshape(devices * rows, parts * width)
    return back, into, blocks[:, 2 * parts * rows :].reshape(devices * rows, width)


def packed(back, into, out, devices):
    rows, width = out.shape[0] // devices, out.shape[1]
    parts = back.shape[0] // out.shape[0]
    into = into.reshape(devices, rows, parts, width).transpose(0, 2, 1, 3)
    return jnp.concatenate(
        [a.reshape(devices, -1, width) for a in (back, into, out)], axis=1
    )


def per_device(
    tokens,
    lengths,
    pair_flip,
    w_qkv,
    q_bias,
    v_bias,
    w_out,
    out_bias,
    norm1_gain,
    norm1_shift,
    w_in,
    in_bias,
    w_back,
    back_bias,
    norm2_gain,
    norm2_shift,
    cotangent,
):
    both = ("head", "blk")
    cores = lax.axis_size("head")
    blocks = lax.axis_size("blk")
    core = lax.axis_index("head")
    block = lax.axis_index("blk")
    local, width = tokens.shape[1:]
    half = local * cores
    heads = HEADS // cores
    group = heads * HD
    ff = w_in.shape[1]
    parts = ff // width
    rows = w_qkv.shape[0]
    x = tokens[0]

    x_sib = swap(x, "head", 1)
    x_far = swap(x, "blk", 1)
    vectors = jnp.stack(
        [q_bias, v_bias, out_bias, back_bias, norm1_gain, norm1_shift, norm2_gain, norm2_shift], axis=0
    )
    extra = jnp.concatenate(
        [
            jnp.pad(vectors, ((0, 0), (0, LANES - rows))),
            jnp.pad(in_bias[None], ((0, 7), (0, 3 * group - LANES - parts * rows))),
        ],
        axis=1,
    )
    columns = w_qkv.reshape(rows, 3, cores, group)
    kept = lax.dynamic_index_in_dim(columns, core, 2, keepdims=False).reshape(rows, 3 * group)
    given = lax.dynamic_index_in_dim(columns, 1 - core, 2, keepdims=False).reshape(rows, 3 * group)
    mine = jnp.concatenate([kept, extra], axis=0)
    theirs = swap(jnp.concatenate([given, extra], axis=0), "head", 1)
    first, second, x_far = gather_blk(place(mine, theirs, core == 1, 0), x_far)
    small = jnp.concatenate([first[:, rows:, : 2 * LANES], second[:, rows:, : 2 * LANES]], axis=0)

    def vector(slot):
        if slot == 8:
            return small[:, 0, LANES : LANES + parts * rows].reshape(-1).astype(F32)
        return small[:, slot, :rows].reshape(-1).astype(F32)

    bias = jnp.concatenate(
        [
            lax.dynamic_slice_in_dim(vector(0), core * group, group),
            jnp.zeros((group,), F32),
            lax.dynamic_slice_in_dim(vector(1), core * group, group),
        ]
    )
    vec = jnp.concatenate(
        [
            vector(8)[None],
            jnp.pad(jnp.concatenate([vector(2), vector(3), vector(4), vector(5)]), (0, ff - 4 * width))[None],
            jnp.pad(jnp.concatenate([vector(6), vector(7)]), (0, ff - 2 * width))[None],
            jnp.zeros((5, ff), F32),
        ],
        axis=0,
    )

    shard = jnp.concatenate(
        [w_back, w_in.reshape(rows, parts, width).transpose(1, 0, 2).reshape(parts * rows, width), w_out], axis=0
    )
    if GATE in (1, 4):
        shard, x_far = lax.optimization_barrier((shard, x_far))
    elif GATE in (2, 6):
        shard, first = lax.optimization_barrier((shard, first))
    elif GATE == 3:
        shard, first, x_far = lax.optimization_barrier((shard, first, x_far))
    gathered = lax.all_gather(shard, both, axis=0, tiled=True).reshape(cores * blocks, -1, width)
    direct = rows % 8 == 0 and blocks % 4 == 0 and (2 * blocks) % (4 * parts) == 0
    if direct:
        inner, outer = 4, blocks // 4
    else:
        inner, outer = 4, 4
        gathered = packed(*unpacked(gathered, parts), cores * inner * outer)

    pieces = (x, x_sib, x_far, swap(x_far, "head", 1))
    bias = jnp.pad(bias[None], ((0, 7), (0, 0)))
    if direct:
        qkv, weight = project(pieces, first, second, bias)
    else:
        shape = (16, width // 32, 3 * group)
        qkv, weight = project(
            pieces, first[:, :rows].reshape(shape), second[:, :rows].reshape(shape), bias
        )

    sequence = block // 2
    own_half = block % 2
    length = lax.dynamic_index_in_dim(lengths, sequence, 0, keepdims=False)
    flags = lax.dynamic_index_in_dim(pair_flip, sequence, 0, keepdims=False)
    flags = lax.dynamic_slice_in_dim(flags, core * heads, heads)
    bounds = [jnp.clip(length - h * half, 0, half) for h in (own_half, 1 - own_half)]
    sc = jnp.concatenate([flags, jnp.stack(bounds + [jnp.int32(local), core])]).astype(jnp.int32)

    context_own, context_sib, lse = attend(sc, qkv, group)
    other = swap(context_sib, "head", 1)
    at_core = core.reshape(1).astype(jnp.int32)
    out, grad_resid1, gc_own, gc_other, low, act, gh, gb, attn, sums = middle(
        at_core, x, context_own, other, cotangent[0], gathered, vec
    )
    grad_context = (gc_own, swap(gc_other, "head", 1))
    contexts = (context_own, context_sib)

    chip = weight_grads(at_core, act, gb, low, gh, context_own, other, attn, inner, outer)
    grad_context, chip = lax.optimization_barrier((grad_context, chip))
    near_groups = [[o * inner + i for i in range(inner)] for o in range(outer)]
    far_groups = [[o * inner + i for o in range(outer)] for i in range(inner)]

    def over_plane(value):
        flat = value.reshape(-1, value.shape[3])
        flat = lax.psum_scatter(flat, "blk", scatter_dimension=0, axis_index_groups=near_groups, tiled=True)
        return flat.reshape(value.shape[1:])

    def over_column(value):
        flat = value.reshape(-1, value.shape[2])
        return lax.psum_scatter(flat, "blk", scatter_dimension=0, axis_index_groups=far_groups, tiled=True)

    if direct:
        chip = over_plane(chip.reshape(inner, outer, (2 * parts + 1) * rows, width))
    else:
        chip = chip.transpose(1, 0, 2, 3, 4).reshape(inner * outer, -1, width)
        chip = packed(*unpacked(chip, parts), blocks)
        chip = lax.psum_scatter(chip, "blk", scatter_dimension=0, tiled=True)[0]

    v_sums = place(
        sums[2, 2 * width : 2 * width + group], sums[2, 2 * width + group : 3 * width], core == 1, 0
    ).reshape(-1)
    by_rows = [v_sums] + [sums[1, s * width : (s + 1) * width] for s in range(4)]
    by_rows = jnp.stack(by_rows + [sums[2, s * width : (s + 1) * width] for s in range(2)], axis=0)
    by_rows = by_rows.reshape(7, cores, blocks, rows).transpose(1, 2, 0, 3).reshape(cores, blocks, -1)
    early_small = jnp.concatenate([by_rows, sums[0].reshape(cores, blocks, parts * rows)], axis=2)
    early_small, grad_context = lax.optimization_barrier((early_small, grad_context))

    def part_rows(keep, send, *small_rows):
        if not direct:
            keep, send = (a.transpose(1, 0, 2, 3).reshape(blocks, rows, -1) for a in (keep, send))
        for extra in small_rows:
            if not direct:
                extra = extra.transpose(0, 2, 1, 3, 4).reshape(2, blocks, 8, -1)
            keep, send = (jnp.concatenate([a, b], axis=-2) for a, b in zip((keep, send), extra))
        return keep, swap(send, "head", 1)

    def finish_part(keep, came):
        both_cores = jnp.concatenate([keep, came], axis=-1)
        if direct:
            both_cores = both_cores.transpose(1, 0, 2, 3).reshape((blocks,) + both_cores.shape[2:])
        return lax.all_to_all(both_cores, "blk", 0, 0, tiled=True)

    def total_of(moved):
        return jnp.sum(moved.astype(F32), axis=0).reshape(moved.shape[1], 2, -1)

    pairs = group // LANES
    first_pairs = pairs - pairs // 3
    dq_a, dkv_a, sum_a, *grad_a = attend_back(
        sc, qkv, contexts, lse, grad_context, pieces, group, 0, first_pairs, inner, outer
    )
    keep_a, came_a = part_rows(*grad_a)
    if direct:
        part_a = jnp.concatenate([keep_a, came_a], axis=2)
        grad_context, part_a, chip = lax.optimization_barrier((grad_context, part_a, chip))
        chip = over_column(jnp.concatenate([chip, over_plane(part_a)], axis=1))
    else:
        total_a = total_of(finish_part(keep_a, came_a))
    dq_b, dkv_b, sum_b, *grad_b = attend_back(
        sc, qkv, contexts, lse, grad_context, pieces, group, first_pairs, pairs - first_pairs, inner, outer
    )

    q_sums = jnp.sum(jnp.concatenate([sum_a, sum_b], axis=0), axis=1)
    q_sums = lax.dynamic_update_slice_in_dim(jnp.zeros((width,), F32), q_sums, core * group, 0)
    grad_small = jnp.concatenate([q_sums.reshape(cores, blocks, rows), early_small], axis=2)
    room = 3 * (pairs - first_pairs) * LANES
    grad_small = jnp.pad(grad_small, ((0, 0), (0, 0), (0, room - grad_small.shape[2])))
    high = grad_small.astype(BF16)
    low_part = (grad_small - high.astype(F32)).astype(BF16)
    small_rows = jnp.pad(jnp.stack([high, low_part], axis=2), ((0, 0), (0, 0), (0, 6), (0, 0)))
    small_rows = jnp.where(core == 0, small_rows, small_rows[::-1])
    small_rows = small_rows.reshape(2, blocks // inner, inner, 8, room).transpose(0, 2, 1, 3, 4)

    dkv = (dkv_a, dkv_b)
    keep_b, came_b = part_rows(*grad_b, small_rows)
    keep_far, send_far = far_rows(dkv, weight)
    far_sib = swap(send_far, "head", 1)
    cuts = [0, *(local * share // 32 for share in SHARES), local]
    far_sums = [
        (keep_far[lo:hi].astype(F32) + far_sib[lo:hi].astype(F32)).astype(BF16)
        for lo, hi in zip(cuts, cuts[1:])
    ]
    far_sums, dq_a, dq_b = lax.optimization_barrier((far_sums, dq_a, dq_b))
    far_in = [swap(part, "blk", 1) for part in far_sums]
    keep_near, send_near = near_rows((dq_a, dq_b), dkv, weight, grad_resid1)
    if ORDER == 0:
        far_in[0], came_b, send_near = lax.optimization_barrier((far_in[0], came_b, send_near))
    moved_b = finish_part(keep_b, came_b)
    chip, send_near = lax.optimization_barrier((chip, send_near))
    near_sib = swap(send_near, "head", 1)
    grad_tokens = keep_near + near_sib.astype(F32) + jnp.concatenate(far_in, axis=0).astype(F32)

    if direct:
        sum_wback, sum_win, sum_wout, sum_wqkv, vectors = unpack(at_core, chip, moved_b, rows, parts)
        vectors = vectors[0] + vectors[1]
        vectors = vectors[: vectors.shape[0] // 2] + vectors[vectors.shape[0] // 2 :]
    else:
        total_b = total_of(moved_b)
        sum_wback = chip[: parts * rows].astype(F32)
        sum_win = chip[parts * rows : 2 * parts * rows].astype(F32)
        sum_win = sum_win.reshape(parts, rows, width).transpose(1, 0, 2).reshape(rows, ff)
        sum_wout = chip[2 * parts * rows : (2 * parts + 1) * rows].astype(F32)

        def columns_of(total):
            parts_of = lambda a: a.reshape(rows, -1, 3, LANES).transpose(0, 2, 1, 3).reshape(rows, 3, -1)
            return place(*(parts_of(total[:rows, s]) for s in (0, 1)), core == 1, 2)

        sum_wqkv = jnp.concatenate([columns_of(total_a), columns_of(total_b)], axis=3).reshape(rows, 3 * width)
        vectors = jnp.sum(total_b[rows : rows + 2], axis=(0, 1))

    def summed(slot, size=rows):
        return vectors[slot * rows : slot * rows + size]

    return (
        out[None],
        grad_tokens[None],
        sum_wqkv,
        summed(0),
        summed(1),
        sum_wout,
        summed(2),
        summed(4),
        summed(5),
        sum_win,
        summed(8, parts * rows),
        sum_wback,
        summed(3),
        summed(6),
        summed(7),
    )


def solution(mesh):
    split = P(("head", "blk"))
    matrix = P(("head", "blk"), None)
    rows = P("blk", "head", None)
    return jax.shard_map(
        per_device,
        mesh=mesh,
        in_specs=(
            rows,
            P(),
            P(),
            matrix,
            split,
            split,
            matrix,
            split,
            split,
            split,
            matrix,
            split,
            matrix,
            split,
            split,
            split,
            rows,
        ),
        out_specs=(
            rows,
            rows,
            matrix,
            split,
            split,
            matrix,
            split,
            split,
            split,
            matrix,
            split,
            matrix,
            split,
            split,
            split,
        ),
        check_vma=False,
    )
```

```python
import functools

import jax
import jax.numpy as jnp
from jax import lax
from jax.experimental import pallas as pl
from jax.experimental.pallas import tpu as pltpu
from jax.sharding import PartitionSpec as P

HEADS = 12
HD = 64
LANES = 128
NEG = -1e30
EPS = 1e-06
SAFE_LOGIT = 60.0
BF16 = jnp.bfloat16
F32 = jnp.float32
NT = (((1,), (1,)), ((), ()))
VMEM_BYTES = 58 << 20


def dot(a, b):
    return jnp.dot(a, b, preferred_element_type=F32)


def dot_nt(a, b):
    return lax.dot_general(a, b, NT, preferred_element_type=F32)


def swap(value, axis, apart):
    pairs = [(source, source ^ apart) for source in range(lax.axis_size(axis))]
    return lax.ppermute(value, axis, pairs)


def place(mine, theirs, upper, axis):
    return jnp.stack([jnp.where(upper, theirs, mine), jnp.where(upper, mine, theirs)], axis=axis)


def gather_blk(pair, also):
    count = lax.axis_size("blk")
    index = lax.axis_index("blk")
    bits = [1 << b for b in range(count.bit_length() - 1)][::-1]
    held = pair
    depth = 1
    for bit in bits[:-2]:
        held = place(held, swap(held, "blk", bit), (index & bit) != 0, depth)
        depth += 1
    held, also = lax.optimization_barrier((held, also))
    first, second = held[0], held[1]
    depth -= 1
    high, low = bits[-2], bits[-1]
    first_in = swap(first, "blk", high)
    second_in = swap(second, "blk", low)
    first = place(first, first_in, (index & high) != 0, depth)
    second = place(second, second_in, (index & low) != 0, depth)
    first_in = swap(first, "blk", low)
    second_in = swap(second, "blk", high)
    first = place(first, first_in, (index & low) != 0, depth + 1)
    second = place(second, second_in, (index & high) != 0, depth)
    return tuple(a.reshape((count,) + pair.shape[1:]) for a in (first, second)) + (also,)


def first_head(rows):
    lane = lax.broadcasted_iota(jnp.int32, (rows, LANES), 1)
    return lane < HD, lane % HD


def key_rows(own, sub, keys, row, sc, source, heads):
    at = lax.broadcasted_iota(jnp.int32, keys.shape, 0) + row
    bound, local, core = sc[heads + source], sc[heads + 2], sc[heads + 3]
    position = jnp.where(at < local, at + core * local, at - core * local)
    bias = jnp.where(position < bound, 0.0, NEG)
    extra = jnp.where(sub < 3, -1.0, jnp.where(sub == 3, bias, 0.0))
    return jnp.where(own, keys.astype(F32), extra).astype(BF16)


def three_parts(value):
    first = value.astype(BF16).astype(F32)
    rest = value - first
    second = rest.astype(BF16).astype(F32)
    return first, second, rest - second


def attend_kernel(
    sc, q_ref, ka_ref, kb_ref, va_ref, vb_ref, own_ref, sib_ref, lse_ref, keys, values, key_norm, *, heads, step
):
    pair = pl.program_id(0)
    count = keys.shape[1]
    rows = q_ref.shape[1]
    scale = HD ** (-0.5)

    @pl.when(pl.program_id(1) == 0)
    def _():
        piece = min(512, count)
        own0, sub = first_head(piece)
        for h, (k_ref, v_ref) in enumerate(((ka_ref, va_ref), (kb_ref, vb_ref))):
            source = sc[2 * pair + h]
            own = own0 if h == 0 else jnp.logical_not(own0)
            largest = jnp.float32(0.0)
            for r in range(0, count, piece):
                k = k_ref[0, r : r + piece, :]
                keys[h, r : r + piece, :] = key_rows(own, sub, k, r, sc, source, heads)
                values[h, :HD, r : r + piece] = v_ref[0, r : r + piece, :].T[h * HD : (h + 1) * HD, :]
                values[h, HD:, r : r + piece] = jnp.ones((16, piece), BF16)
                k = jnp.where(own, k.astype(F32), 0.0)
                largest = jnp.maximum(largest, jnp.max(jnp.sum(k * k, axis=1, keepdims=True)))
            key_norm[h] = largest

    q = q_ref[0].astype(F32) * scale
    own0, sub = first_head(rows)
    one = jnp.where(sub == 3, 1.0, 0.0)
    square = q * q
    norm_a = jnp.max(jnp.sum(jnp.where(own0, square, 0.0), axis=1, keepdims=True))
    norm_b = jnp.max(jnp.sum(jnp.where(own0, 0.0, square), axis=1, keepdims=True))
    largest = jnp.maximum(norm_a * key_norm[0], norm_b * key_norm[1])
    small = largest < SAFE_LOGIT * SAFE_LOGIT

    def queries(h):
        return (jnp.where(own0, q, one) if h == 0 else jnp.where(own0, one, q)).astype(BF16)

    def finish(outs, peaks):
        totals = [jnp.broadcast_to(o[HD : HD + 1, :], (HD, rows)) for o in outs]
        out = jnp.concatenate([o[:HD, :] / t for o, t in zip(outs, totals)], axis=0).astype(BF16).T
        mine = pl.program_id(1) < pl.num_programs(1) // 2

        @pl.when(mine)
        def _():
            own_ref[...] = out

        @pl.when(jnp.logical_not(mine))
        def _():
            sib_ref[...] = out

        for h in (0, 1):
            lse = jnp.log(outs[h][HD : HD + 1, :])
            if peaks is not None:
                lse = lse + jnp.broadcast_to(peaks[h], (rows, LANES)).T[:1, :]
            lse_ref[h : h + 1, :] = lse

    @pl.when(small)
    def _():
        outs = []
        for h in (0, 1):
            qa = queries(h)
            out = None
            for c in range(0, count, step):
                p = jnp.exp(dot_nt(qa, keys[h, c : c + step, :])).astype(BF16)
                part = dot_nt(values[h, :, c : c + step], p)
                out = part if out is None else out + part
            outs.append(out)
        finish(outs, None)

    @pl.when(jnp.logical_not(small))
    def _():
        outs, peaks = [], []
        for h in (0, 1):
            s = dot_nt(queries(h), keys[h])
            peak = jnp.max(s, axis=1, keepdims=True)
            outs.append(dot_nt(values[h], jnp.exp(s - peak).astype(BF16)))
            peaks.append(peak)
        finish(outs, peaks)


def pair_specs(count, width, skip=0):
    pairs = width // LANES

    def key_value(h, base):
        return pl.BlockSpec((1, count, LANES), lambda p, i, sc: (sc[2 * (p + skip) + h], 0, base * pairs + p + skip))

    return [key_value(0, 1), key_value(1, 1), key_value(0, 2), key_value(1, 2)]


def halves_specs(rows, blocks, skip=0):
    first = pl.BlockSpec((rows, LANES), lambda p, i, sc: (jnp.minimum(i, blocks // 2 - 1), p + skip))
    return [first, pl.BlockSpec((rows, LANES), lambda p, i, sc: (jnp.maximum(i - blocks // 2, 0), p + skip))]


def attend(sc, qkv, width):
    count = qkv.shape[1]
    rows = min(1024, count // 2)
    q_spec = pl.BlockSpec((1, rows, LANES), lambda p, i, sc: (0, i, p))
    heads = width // HD
    return pl.pallas_call(
        functools.partial(attend_kernel, heads=heads, step=min(512, count)),
        grid_spec=pltpu.PrefetchScalarGridSpec(
            num_scalar_prefetch=1,
            grid=(width // LANES, count // rows),
            in_specs=[q_spec] + pair_specs(count, width),
            out_specs=halves_specs(rows, count // rows) + [pl.BlockSpec((8, rows), lambda p, i, sc: (p, i))],
            scratch_shapes=[
                pltpu.VMEM((2, count, LANES), BF16),
                pltpu.VMEM((2, HD + 16, count), BF16),
                pltpu.SMEM((2,), F32),
            ],
        ),
        out_shape=[
            jax.ShapeDtypeStruct((count // 2, width), BF16),
            jax.ShapeDtypeStruct((count // 2, width), BF16),
            jax.ShapeDtypeStruct((8 * width // LANES, count), F32),
        ],
        compiler_params=pltpu.CompilerParams(vmem_limit_bytes=VMEM_BYTES),
        cost_estimate=pl.CostEstimate(
            flops=4 * 4 * count * count * width, bytes_accessed=2 * 6 * count * width, transcendentals=0
        ),
        name="attend",
    )(sc, qkv, qkv, qkv, qkv, qkv)


def attend_back_kernel(
    sc,
    q_ref,
    ka_ref,
    kb_ref,
    va_ref,
    vb_ref,
    o_own,
    o_sib,
    do_own,
    do_sib,
    lse_ref,
    x0,
    x1,
    x2,
    x3,
    dq_ref,
    dkv_ref,
    sum_ref,
    keep_ref,
    send_ref,
    keys,
    keys_t,
    values,
    dk_sum,
    dv_sum,
    dq_all,
    tokens,
    sem,
    *,
    heads,
    step,
    skip,
):
    pair = pl.program_id(0) + skip
    block = pl.program_id(1)
    count = keys.shape[1]
    rows = q_ref.shape[1]
    scale = HD ** (-0.5)

    copies = [pltpu.make_async_copy(ref, tokens.at[i], sem.at[i]) for i, ref in enumerate((x0, x1, x2, x3))]

    @pl.when(jnp.logical_and(pl.program_id(0) == 0, block == 0))
    def _():
        for copy in copies:
            copy.start()

    @pl.when(jnp.logical_and(pl.program_id(0) == 0, block == pl.num_programs(1) - 1))
    def _():
        for copy in copies:
            copy.wait()

    @pl.when(block == 0)
    def _():
        piece = min(512, count)
        own0, sub = first_head(piece)
        for h, (k_ref, v_ref) in enumerate(((ka_ref, va_ref), (kb_ref, vb_ref))):
            source = sc[2 * pair + h]
            own = own0 if h == 0 else jnp.logical_not(own0)
            for r in range(0, count, piece):
                k = k_ref[0, r : r + piece, :]
                keys[h, r : r + piece, :] = key_rows(own, sub, k, r, sc, source, heads)
                keys_t[h, :, r : r + piece] = k.T[h * HD : (h + 1) * HD, :]
                v = v_ref[0, r : r + piece, :].astype(F32)
                values[h, r : r + piece, :] = jnp.where(own, v, 1.0).astype(BF16)
        sum_ref[...] = jnp.zeros_like(sum_ref)
        dk_sum[...] = jnp.zeros_like(dk_sum)
        dv_sum[...] = jnp.zeros_like(dv_sum)

    q = q_ref[0]
    mine = block < pl.num_programs(1) // 2
    do = jnp.where(mine, do_own[...], do_sib[...])
    out = jnp.where(mine, o_own[...], o_sib[...])
    own0, sub = first_head(rows)
    qf = q.astype(F32) * scale
    lse = lse_ref[...].T
    first, second, third = three_parts(jnp.where(own0, lse[:, 1:2], lse[:, 0:1]))
    q_extra = jnp.where(
        sub == 0, first, jnp.where(sub == 1, second, jnp.where(sub == 2, third, jnp.where(sub == 3, 1.0, 0.0)))
    )
    dof = do.astype(F32)
    product = dof * out.astype(F32)
    inner_a = jnp.sum(jnp.where(own0, product, 0.0), axis=1, keepdims=True)
    inner_b = jnp.sum(jnp.where(own0, 0.0, product), axis=1, keepdims=True)
    first, second, third = three_parts(jnp.where(own0, -inner_b, -inner_a))
    do_extra = jnp.where(sub == 0, first, jnp.where(sub == 1, second, jnp.where(sub == 2, third, 0.0)))
    q_t = q.T
    do_t = do.T
    grads = []
    for h in (0, 1):
        qa = (jnp.where(own0, qf, q_extra) if h == 0 else jnp.where(own0, q_extra, qf)).astype(BF16)
        da = (jnp.where(own0, dof, do_extra) if h == 0 else jnp.where(own0, do_extra, dof)).astype(BF16)
        own_rows = slice(h * HD, (h + 1) * HD)
        dq = None
        for c in range(0, count, step):
            part = slice(c, c + step)
            p = jnp.exp(dot_nt(qa, keys[h, part, :]))
            ds = (p * dot_nt(da, values[h, part, :])).astype(BF16)
            p = p.astype(BF16)
            t = dot_nt(keys_t[h, :, part], ds)
            dq = t if dq is None else dq + t
            dk_sum[own_rows, part] += dot(q_t[own_rows, :], ds)
            dv_sum[own_rows, part] += dot(do_t[own_rows, :], p)
        grads.append(dq)
    dq = (jnp.concatenate(grads, axis=0) * scale).astype(BF16)
    dq_ref[...] = dq
    for i in range(count // rows):

        @pl.when(block == i)
        def _():
            dq_all[:, i * rows : (i + 1) * rows] = dq

    for c in range(0, rows, LANES):
        sum_ref[...] += dq[:, c : c + LANES].astype(F32)

    @pl.when(block == pl.num_programs(1) - 1)
    def _():
        for h in (0, 1):
            source = sc[2 * pair + h]
            own_rows = slice(h * HD, (h + 1) * HD)
            dk = dk_sum[own_rows, :] * scale
            dv = dv_sum[own_rows, :]
            for half in (0, 1):
                here = source == half
                dkv_ref[half, 0, own_rows, :] = jnp.where(here, dk, 0.0).astype(BF16)
                dkv_ref[half, 1, own_rows, :] = jnp.where(here, dv, 0.0).astype(BF16)

        local = tokens.shape[1]
        near = jnp.concatenate([dq_all[...], dkv_ref[0, 0], dkv_ref[0, 1]], axis=0)
        far = jnp.concatenate([dkv_ref[1, 0], dkv_ref[1, 1]], axis=0)
        near = dot(near[:, :local], tokens[0]) + dot(near[:, local:], tokens[1])
        far = dot(far[:, :local], tokens[2]) + dot(far[:, local:], tokens[3])
        grad = jnp.concatenate([near[:LANES], near[LANES:] + far], axis=0).T.astype(BF16)
        inner, outer, unit, _ = keep_ref.shape
        half_rows = grad.shape[0] // 2
        for c in (0, 1):
            part = grad[c * half_rows : (c + 1) * half_rows].reshape(outer, inner, unit, 3 * LANES)
            core = sc[heads + 3]

            @pl.when(core == c)
            def _():
                for o in range(outer):
                    keep_ref[:, o] = part[o]

            @pl.when(core != c)
            def _():
                for o in range(outer):
                    send_ref[:, o] = part[o]


def attend_back(sc, qkv, contexts, lse, grads, pieces, width, skip, pairs, inner, outer):
    model = pieces[0].shape[1]
    unit = model // (2 * inner * outer)
    piece = pl.BlockSpec(memory_space=pl.ANY)
    grad_spec = pl.BlockSpec((inner, outer, unit, 3 * LANES), lambda p, i, sc: (0, 0, 0, p))
    grad_shape = jax.ShapeDtypeStruct((inner, outer, unit, 3 * pairs * LANES), BF16)
    count = qkv.shape[1]
    rows = min(1024, count // 2)
    lse_spec = pl.BlockSpec((8, rows), lambda p, i, sc: (p + skip, i))
    q_spec = pl.BlockSpec((1, rows, LANES), lambda p, i, sc: (0, i, p + skip))
    dq_spec = pl.BlockSpec((LANES, rows), lambda p, i, sc: (p, i))
    dkv_spec = pl.BlockSpec((2, 2, LANES, count), lambda p, i, sc: (0, 0, p, 0))
    heads = width // HD
    return pl.pallas_call(
        functools.partial(attend_back_kernel, heads=heads, step=min(512, count), skip=skip),
        grid_spec=pltpu.PrefetchScalarGridSpec(
            num_scalar_prefetch=1,
            grid=(pairs, count // rows),
            in_specs=[q_spec] + pair_specs(count, width, skip) + halves_specs(rows, count // rows, skip) * 2
            + [lse_spec]
            + [piece] * 4,
            out_specs=[
                dq_spec,
                dkv_spec,
                pl.BlockSpec((LANES, LANES), lambda p, i, sc: (p, 0)),
                grad_spec,
                grad_spec,
            ],
            scratch_shapes=[
                pltpu.VMEM((2, count, LANES), BF16),
                pltpu.VMEM((2, HD, count), BF16),
                pltpu.VMEM((2, count, LANES), BF16),
                pltpu.VMEM((LANES, count), F32),
                pltpu.VMEM((LANES, count), F32),
                pltpu.VMEM((LANES, count), BF16),
                pltpu.VMEM((4,) + pieces[0].shape, BF16),
                pltpu.SemaphoreType.DMA((4,)),
            ],
        ),
        out_shape=[
            jax.ShapeDtypeStruct((pairs * LANES, count), BF16),
            jax.ShapeDtypeStruct((2, 2, pairs * LANES, count), BF16),
            jax.ShapeDtypeStruct((pairs * LANES, LANES), F32),
            grad_shape,
            grad_shape,
        ],
        compiler_params=pltpu.CompilerParams(vmem_limit_bytes=VMEM_BYTES),
        cost_estimate=pl.CostEstimate(
            flops=10 * 4 * count * count * pairs * LANES, bytes_accessed=2 * 12 * count * pairs * LANES, transcendentals=0
        ),
        name="attend_back",
    )(sc, qkv, qkv, qkv, qkv, qkv, *contexts, *grads, lse, *pieces)


def mean_of(value):
    return jnp.mean(value, axis=-1, keepdims=True)


def norm_of(value):
    center = value - mean_of(value)
    inverse = lax.rsqrt(mean_of(center * center) + EPS)
    return center * inverse, inverse


def norm_back(grad, normed, inverse, gain):
    dn = grad * gain
    return inverse * (dn - mean_of(dn) - normed * mean_of(dn * normed))


def sum_rows(value):
    return jnp.sum(value, axis=0, keepdims=True)


def middle_kernel(
    core,
    x_ref,
    own_ref,
    other_ref,
    cot_ref,
    wo_own_ref,
    wo_other_ref,
    *refs,
    width,
    ff,
):
    chunk = width
    parts = ff // width
    w_in_refs = refs[:parts]
    (
        w_back_ref,
        vec,
        out_ref,
        resid_ref,
        gc_own,
        gc_other,
        low_ref,
        act_ref,
        gh_ref,
        gb_ref,
        attn_ref,
        sums,
        slope,
        wo_own,
        wo_other,
        w_in,
        w_back,
    ) = refs[parts:]
    in_bias = lambda c: vec[0:1, c : c + chunk]
    row = lambda r, s: vec[r : r + 1, s * width : (s + 1) * width]
    out_bias, back_bias, gain1, shift1 = (row(1, s) for s in range(4))
    gain2, shift2 = row(2, 0), row(2, 1)

    @pl.when(pl.program_id(0) == 0)
    def _():
        sums[...] = jnp.zeros_like(sums)
        wo_own[...] = wo_own_ref[...].reshape(wo_own.shape)
        wo_other[...] = wo_other_ref[...].reshape(wo_other.shape)
        for j in range(parts):
            w_in[j] = w_in_refs[j][...].reshape(w_in.shape[1:])
        devices, rows = w_back_ref.shape[:2]
        some = devices // parts
        for j in range(parts):
            w_back[j] = w_back_ref[j * some : (j + 1) * some].reshape(some * rows, width)

    attended = dot(own_ref[...], wo_own[...]) + dot(other_ref[...], wo_other[...]) + out_bias
    hat1, inverse1 = norm_of(x_ref[...].astype(F32) + attended)
    normed = hat1 * gain1 + shift1
    low = normed.astype(BF16)
    low_ref[...] = low
    branch = None
    for c in range(0, ff, chunk):
        hidden = dot(low, w_in[c // chunk]) + in_bias(c)
        cumulative = 0.5 * (1.0 + lax.erf(hidden * 0.7071067811865476))
        density = 0.3989422804014327 * jnp.exp(-0.5 * hidden * hidden)
        slope[:, c : c + chunk] = cumulative + hidden * density
        act = (hidden * cumulative).astype(BF16)
        act_ref[:, c : c + chunk] = act
        part = dot(act, w_back[c // chunk])
        branch = part if branch is None else branch + part
    hat2, inverse2 = norm_of(normed + (branch + back_bias))
    out_ref[...] = (hat2 * gain2 + shift2).astype(BF16)
    cot = cot_ref[...].astype(F32)
    grad2 = norm_back(cot, hat2, inverse2, gain2)
    gb = grad2.astype(BF16)
    gb_ref[...] = gb
    grad_normed = grad2
    for c in range(0, ff, chunk):
        gh = (dot_nt(gb, w_back[c // chunk]) * slope[:, c : c + chunk]).astype(BF16)
        gh_ref[:, c : c + chunk] = gh
        sums[0:1, c : c + chunk] += sum_rows(gh.astype(F32))
        grad_normed = grad_normed + dot_nt(gh, w_in[c // chunk])
    grad1 = norm_back(grad_normed, hat1, inverse1, gain1)
    resid_ref[...] = grad1
    attn = grad1.astype(BF16)
    attn_ref[...] = attn
    gc_own[...] = dot_nt(attn, wo_own[...]).astype(BF16)
    gc_other[...] = dot_nt(attn, wo_other[...]).astype(BF16)
    at = lambda r, s, v: sums.__setitem__(
        (slice(r, r + 1), slice(s * width, (s + 1) * width)),
        sums[r : r + 1, s * width : (s + 1) * width] + sum_rows(v),
    )
    at(1, 0, attn.astype(F32))
    at(1, 1, gb.astype(F32))
    at(1, 2, grad_normed * hat1)
    at(1, 3, grad_normed)
    at(2, 0, cot * hat2)
    at(2, 1, cot)
    for s, ref in enumerate((gc_own, gc_other)):
        half = ref.shape[1]
        lane = slice(2 * width + s * half, 2 * width + (s + 1) * half)
        sums[2:3, lane] += sum_rows(ref[...].astype(F32))


def middle(core, x, own, other, cot, weights, vec):
    count, width = x.shape
    ff = vec.shape[1]
    parts = ff // width
    devices = weights.shape[0]
    unit = width // devices
    once = pl.Buffered(1)
    half_spec = lambda at: pl.BlockSpec(
        (devices // 2, unit, width), lambda i, core: (at(core[0]), 2 * parts, 0), pipeline_mode=once
    )
    in_spec = lambda j: pl.BlockSpec(
        (devices, unit, width), lambda i, core: (0, parts + j, 0), pipeline_mode=once
    )
    half = own.shape[1]
    rows = min(256, count)
    tile = lambda w: pl.BlockSpec((rows, w), lambda i, core: (i, 0))
    whole = lambda a: pl.BlockSpec(a.shape, lambda i, core: (0, 0), pipeline_mode=once)
    return pl.pallas_call(
        functools.partial(middle_kernel, width=width, ff=ff),
        grid_spec=pltpu.PrefetchScalarGridSpec(
            num_scalar_prefetch=1,
            grid=(count // rows,),
            in_specs=[
                tile(width),
                tile(half),
                tile(half),
                tile(width),
                half_spec(lambda c: c),
                half_spec(lambda c: 1 - c),
                *[in_spec(j) for j in range(parts)],
                pl.BlockSpec((devices, parts * unit, width), lambda i, core: (0, 0, 0), pipeline_mode=once),
                whole(vec),
            ],
            out_specs=[
                tile(width),
                tile(width),
                tile(half),
                tile(half),
                tile(width),
                tile(ff),
                tile(ff),
                tile(width),
                tile(width),
                pl.BlockSpec((8, ff), lambda i, core: (0, 0)),
            ],
            scratch_shapes=[
                pltpu.VMEM((rows, ff), F32),
                pltpu.VMEM((half, width), BF16),
                pltpu.VMEM((half, width), BF16),
                pltpu.VMEM((parts, width, width), BF16),
                pltpu.VMEM((parts, width, width), BF16),
            ],
        ),
        out_shape=[
            jax.ShapeDtypeStruct((count, width), BF16),
            jax.ShapeDtypeStruct((count, width), F32),
            jax.ShapeDtypeStruct((count, half), BF16),
            jax.ShapeDtypeStruct((count, half), BF16),
            jax.ShapeDtypeStruct((count, width), BF16),
            jax.ShapeDtypeStruct((count, ff), BF16),
            jax.ShapeDtypeStruct((count, ff), BF16),
            jax.ShapeDtypeStruct((count, width), BF16),
            jax.ShapeDtypeStruct((count, width), BF16),
            jax.ShapeDtypeStruct((8, ff), F32),
        ],
        compiler_params=pltpu.CompilerParams(vmem_limit_bytes=VMEM_BYTES),
        cost_estimate=pl.CostEstimate(
            flops=2 * count * width * (4 * ff + 2 * width), bytes_accessed=2 * (4 * width * ff + 2 * count * ff + 8 * count * width), transcendentals=0
        ),
        name="middle",
    )(core, x, own, other, cot, *([weights] * (3 + parts)), vec)


def dot_tn(a, b):
    return lax.dot_general(a, b, (((0,), (0,)), ((), ())), preferred_element_type=F32)


def back_grads_kernel(core, act, gb, *refs):
    *came, out_ref = refs
    inner, span, parts, unit, width = out_ref.shape
    got = dot_tn(act[...], gb[...]).reshape(span, inner, parts, unit, width)
    for o in range(span):
        mine = got[o]
        for ref in came:
            mine = mine + ref[:, o].astype(F32)
        out_ref[:, o] = mine.astype(BF16)


def in_grads_kernel(core, low, gh, context, attn, *refs, parts):
    *came, out_ref = refs
    came = came[:1]
    inner, outer, _, unit, width = out_ref.shape

    def put(value):
        value = value.reshape(outer, inner, unit, width)
        for o in range(outer):
            mine = value[o]
            for ref in came:
                mine = mine + ref[:, o, 0].astype(F32)
            out_ref[:, o, 0] = mine.astype(BF16)

    @pl.when(pl.program_id(0) < parts)
    def _():
        put(dot_tn(low[...], gh[...]))

    @pl.when(pl.program_id(0) == parts)
    def _():
        put(dot_tn(context[...], attn[...]))


def weight_grads(core, act, gb, low, gh, own, other, attn, inner, outer):
    count, width = low.shape
    parts = act.shape[1] // width
    unit = width // (2 * inner * outer)
    tiles = parts // 2
    span = outer // tiles
    once = pl.Buffered(1)
    whole = pl.BlockSpec((count, width), lambda t, core: (0, 0), pipeline_mode=once)
    anywhere = pl.BlockSpec(memory_space=pl.ANY)

    def call(kernel, tiles, in_specs, out_spec, slots, args, came, aliases, flops):
        return pl.pallas_call(
            kernel,
            grid_spec=pltpu.PrefetchScalarGridSpec(
                num_scalar_prefetch=1, grid=(tiles,), in_specs=in_specs, out_specs=out_spec
            ),
            out_shape=jax.ShapeDtypeStruct((inner, outer, slots, unit, width), BF16),
            input_output_aliases=aliases,
            compiler_params=pltpu.CompilerParams(vmem_limit_bytes=26 << 20),
            cost_estimate=pl.CostEstimate(flops=flops, bytes_accessed=3 * flops // width, transcendentals=0),
            name="weight_grads",
        )(core, *args, *came)

    def back(pick, slots, came):
        spec = pl.BlockSpec((inner, span, parts, unit, width), lambda t, core: (0, t, 0, 0, 0))
        tile = pl.BlockSpec((count, width), lambda t, core: (0, tiles * pick(core[0]) + t))
        return call(
            back_grads_kernel,
            tiles,
            [tile, whole] + [spec] * len(came),
            spec,
            slots,
            (act, gb),
            came,
            {},
            count * width * width * parts,
        )

    def into(pick, context, skip, came, base):
        spec = lambda skip: pl.BlockSpec((inner, outer, 1, unit, width), lambda t, core: (0, 0, t + skip, 0, 0))
        half = context.shape[1]
        return call(
            functools.partial(in_grads_kernel, parts=parts),
            parts + 1,
            [
                pl.BlockSpec((count, half), lambda t, core: (0, pick(core[0])), pipeline_mode=once),
                pl.BlockSpec((count, width), lambda t, core: (0, jnp.minimum(t, parts - 1))),
                pl.BlockSpec((count, half), lambda t, core: (0, 0), pipeline_mode=once),
                whole,
            ]
            + [spec(0)] * len(came)
            + [anywhere] * len(base),
            spec(skip),
            skip + parts + 1,
            (low, gh, context, attn),
            came + base,
            {6: 0} if base else {},
            count * width * width * (parts + 1),
        )

    mine, theirs = (lambda c: c), (lambda c: 1 - c)
    sent = back(theirs, parts, ())
    sent, low, act = lax.optimization_barrier((sent, low, act))
    back_came = swap(sent, "head", 1)
    in_sent = into(theirs, other, 0, (), ())
    back_came, in_sent, act = lax.optimization_barrier((back_came, in_sent, act))
    in_came = swap(in_sent, "head", 1)
    kept = back(mine, 2 * parts + 1, (back_came,))
    return into(mine, own, parts, (in_came,), (kept,))


def project_kernel(x0, x1, x2, x3, first, second, bias, out_ref, weight_ref, *, group):
    step = pl.program_id(0)
    blocks, width = pl.num_programs(0) // 4, x0.shape[1]
    rows = first.shape[0] * (weight_ref.shape[0] // first.shape[0] // 2)

    @pl.when(step == 0)
    def _():
        unit = weight_ref.shape[0] // (2 * first.shape[0])
        weight_ref[:rows, :] = first[:, :unit, :].reshape(rows, 3 * group)
        weight_ref[rows:, :] = second[:, :unit, :].reshape(rows, 3 * group)

    for p, ref in enumerate((x0, x1, x2, x3)):

        @pl.when(step // blocks == p)
        def _():
            start = 0 if p < 2 else group
            got = dot(ref[...], weight_ref[:, start:]) + bias[0:1, start:]
            out_ref[0, :, start:] = got.astype(BF16)


def project(pieces, first, second, bias):
    count, width = pieces[0].shape
    wide = first.shape[2]
    rows = min(512, count)
    blocks = count // rows
    once = pl.Buffered(1)
    piece = lambda p: pl.BlockSpec((rows, width), lambda i: (jnp.clip(i - p * blocks, 0, blocks - 1), 0))
    whole = lambda a: pl.BlockSpec(a.shape, lambda i: (0,) * a.ndim, pipeline_mode=once)
    return pl.pallas_call(
        functools.partial(project_kernel, group=wide // 3),
        grid=(4 * blocks,),
        in_specs=[piece(p) for p in range(4)] + [whole(first), whole(second), whole(bias)],
        out_specs=[
            pl.BlockSpec((1, rows, wide), lambda i: (i // (2 * blocks), i % (2 * blocks), 0)),
            pl.BlockSpec((width, wide), lambda i: (0, 0)),
        ],
        out_shape=[
            jax.ShapeDtypeStruct((2, 2 * count, wide), BF16),
            jax.ShapeDtypeStruct((width, wide), BF16),
        ],
        compiler_params=pltpu.CompilerParams(vmem_limit_bytes=VMEM_BYTES),
        cost_estimate=pl.CostEstimate(
            flops=2 * 4 * count * width * wide, bytes_accessed=8 * count * (width + wide), transcendentals=0
        ),
        name="project",
    )(*pieces, first, second, bias)


def stacked(refs, which):
    return jnp.concatenate([ref[0, kind] for kind in which for ref in refs], axis=0).T


def far_rows_kernel(*refs, group):
    *dkv, weight, keep_ref, send_ref = refs
    step = pl.program_id(0)
    got = dot_nt(stacked(dkv, (0, 1)), weight[:, group:]).astype(BF16)

    @pl.when(step < pl.num_programs(0) // 2)
    def _():
        keep_ref[...] = got

    @pl.when(step >= pl.num_programs(0) // 2)
    def _():
        send_ref[...] = got


def dkv_spec(part, rows, source):
    return pl.BlockSpec((1, 2, part.shape[2], rows), lambda i: (source, 0, 0, i))


def far_rows(dkv, weight):
    count, (width, wide) = dkv[0].shape[3], weight.shape
    rows = min(512, count // 2)
    blocks = count // rows
    return pl.pallas_call(
        functools.partial(far_rows_kernel, group=wide // 3),
        grid=(blocks,),
        in_specs=[dkv_spec(part, rows, 1) for part in dkv]
        + [pl.BlockSpec((width, wide), lambda i: (0, 0), pipeline_mode=pl.Buffered(1))],
        out_specs=[
            pl.BlockSpec((rows, width), lambda i: (jnp.minimum(i, blocks // 2 - 1), 0)),
            pl.BlockSpec((rows, width), lambda i: (jnp.maximum(i - blocks // 2, 0), 0)),
        ],
        out_shape=[jax.ShapeDtypeStruct((count // 2, width), BF16)] * 2,
        compiler_params=pltpu.CompilerParams(vmem_limit_bytes=VMEM_BYTES),
        cost_estimate=pl.CostEstimate(
            flops=2 * count * width * wide * 2 // 3, bytes_accessed=8 * count * width, transcendentals=0
        ),
        name="far_rows",
    )(*dkv, weight)


def near_rows_kernel(*refs, parts, group):
    dq, dkv = refs[:parts], refs[parts : 2 * parts]
    weight, resid, keep_ref, send_ref = refs[2 * parts :]
    step = pl.program_id(0)
    queries = jnp.concatenate([ref[...] for ref in dq], axis=0).T
    got = dot_nt(queries, weight[:, :group]) + dot_nt(stacked(dkv, (0, 1)), weight[:, group:])

    @pl.when(step < pl.num_programs(0) // 2)
    def _():
        keep_ref[...] = got + resid[...]

    @pl.when(step >= pl.num_programs(0) // 2)
    def _():
        send_ref[...] = got.astype(BF16)


def near_rows(dq, dkv, weight, resid):
    count, (width, wide) = dkv[0].shape[3], weight.shape
    rows = min(512, count // 2)
    blocks = count // rows
    return pl.pallas_call(
        functools.partial(near_rows_kernel, parts=len(dq), group=wide // 3),
        grid=(blocks,),
        in_specs=[pl.BlockSpec((part.shape[0], rows), lambda i: (0, i)) for part in dq]
        + [dkv_spec(part, rows, 0) for part in dkv]
        + [
            pl.BlockSpec((width, wide), lambda i: (0, 0), pipeline_mode=pl.Buffered(1)),
            pl.BlockSpec((rows, width), lambda i: (jnp.minimum(i, blocks // 2 - 1), 0)),
        ],
        out_specs=[
            pl.BlockSpec((rows, width), lambda i: (jnp.minimum(i, blocks // 2 - 1), 0)),
            pl.BlockSpec((rows, width), lambda i: (jnp.maximum(i - blocks // 2, 0), 0)),
        ],
        out_shape=[
            jax.ShapeDtypeStruct((count // 2, width), F32),
            jax.ShapeDtypeStruct((count // 2, width), BF16),
        ],
        compiler_params=pltpu.CompilerParams(vmem_limit_bytes=VMEM_BYTES),
        cost_estimate=pl.CostEstimate(
            flops=2 * count * width * wide, bytes_accessed=12 * count * width, transcendentals=0
        ),
        name="near_rows",
    )(*dq, *dkv, weight, resid)


def unpack_kernel(core, chip, moved, back_ref, in_ref, out_ref, qkv_ref, vec_ref, *, rows, parts):
    width = chip.shape[1]
    at = lambda slot, count=1: chip[slot * rows : (slot + count) * rows, :].astype(F32)
    back_ref[...] = at(0, parts)
    for j in range(parts):
        in_ref[:, j * width : (j + 1) * width] = at(parts + j)
    out_ref[...] = at(2 * parts)
    total = jnp.sum(moved[...].astype(F32), axis=0)
    vec_ref[...] = total[rows : rows + 8]
    half = total.shape[1] // 2
    firsts = at(2 * parts + 1), at(2 * parts + 2)
    seconds = total[:rows, :half], total[:rows, half:]
    block = half // 3
    for h in (0, 1):
        own = core[0] == h
        first = jnp.where(own, *firsts)
        second = jnp.where(own, *seconds)
        early = width // half
        for t in range(3):
            for p in range(early + 1):
                start = ((2 * t + h) * (early + 1) + p) * block
                source, at_pair = (first, p) if p < early else (second, 0)
                lane = (3 * at_pair + t) * block
                qkv_ref[:, start : start + block] = source[:, lane : lane + block]


def unpack(core, chip, moved, rows, parts):
    width = chip.shape[1]
    whole = lambda a: pl.BlockSpec(a.shape, lambda i, core: (0,) * len(a.shape))
    outs = [
        jax.ShapeDtypeStruct(shape, F32)
        for shape in (
            (parts * rows, width),
            (rows, parts * width),
            (rows, width),
            (rows, 3 * width),
            (8, moved.shape[2]),
        )
    ]
    return pl.pallas_call(
        functools.partial(unpack_kernel, rows=rows, parts=parts),
        grid_spec=pltpu.PrefetchScalarGridSpec(
            num_scalar_prefetch=1,
            grid=(1,),
            in_specs=[whole(chip), whole(moved)],
            out_specs=[whole(a) for a in outs],
        ),
        out_shape=outs,
        name="unpack",
    )(core, chip, moved)


def unpacked(blocks, parts):
    devices, size, width = blocks.shape
    rows = size // (2 * parts + 1)
    back = blocks[:, : parts * rows].reshape(devices * parts * rows, width)
    into = blocks[:, parts * rows : 2 * parts * rows].reshape(devices, parts, rows, width)
    into = into.transpose(0, 2, 1, 3).reshape(devices * rows, parts * width)
    return back, into, blocks[:, 2 * parts * rows :].reshape(devices * rows, width)


def packed(back, into, out, devices):
    rows, width = out.shape[0] // devices, out.shape[1]
    parts = back.shape[0] // out.shape[0]
    into = into.reshape(devices, rows, parts, width).transpose(0, 2, 1, 3)
    return jnp.concatenate(
        [a.reshape(devices, -1, width) for a in (back, into, out)], axis=1
    )


def per_device(
    tokens,
    lengths,
    pair_flip,
    w_qkv,
    q_bias,
    v_bias,
    w_out,
    out_bias,
    norm1_gain,
    norm1_shift,
    w_in,
    in_bias,
    w_back,
    back_bias,
    norm2_gain,
    norm2_shift,
    cotangent,
):
    both = ("head", "blk")
    cores = lax.axis_size("head")
    blocks = lax.axis_size("blk")
    core = lax.axis_index("head")
    block = lax.axis_index("blk")
    local, width = tokens.shape[1:]
    half = local * cores
    heads = HEADS // cores
    group = heads * HD
    ff = w_in.shape[1]
    parts = ff // width
    rows = w_qkv.shape[0]
    x = tokens[0]

    x_sib = swap(x, "head", 1)
    x_far = swap(x, "blk", 1)
    vectors = jnp.stack(
        [q_bias, v_bias, out_bias, back_bias, norm1_gain, norm1_shift, norm2_gain, norm2_shift], axis=0
    )
    extra = jnp.concatenate(
        [
            jnp.pad(vectors, ((0, 0), (0, LANES - rows))),
            jnp.pad(in_bias[None], ((0, 7), (0, 3 * group - LANES - parts * rows))),
        ],
        axis=1,
    )
    columns = w_qkv.reshape(rows, 3, cores, group)
    kept = lax.dynamic_index_in_dim(columns, core, 2, keepdims=False).reshape(rows, 3 * group)
    given = lax.dynamic_index_in_dim(columns, 1 - core, 2, keepdims=False).reshape(rows, 3 * group)
    mine = jnp.concatenate([kept, extra], axis=0)
    theirs = swap(jnp.concatenate([given, extra], axis=0), "head", 1)
    first, second, x_far = gather_blk(place(mine, theirs, core == 1, 0), x_far)
    small = jnp.concatenate([first[:, rows:, : 2 * LANES], second[:, rows:, : 2 * LANES]], axis=0)

    def vector(slot):
        if slot == 8:
            return small[:, 0, LANES : LANES + parts * rows].reshape(-1).astype(F32)
        return small[:, slot, :rows].reshape(-1).astype(F32)

    bias = jnp.concatenate(
        [
            lax.dynamic_slice_in_dim(vector(0), core * group, group),
            jnp.zeros((group,), F32),
            lax.dynamic_slice_in_dim(vector(1), core * group, group),
        ]
    )
    vec = jnp.concatenate(
        [
            vector(8)[None],
            jnp.pad(jnp.concatenate([vector(2), vector(3), vector(4), vector(5)]), (0, ff - 4 * width))[None],
            jnp.pad(jnp.concatenate([vector(6), vector(7)]), (0, ff - 2 * width))[None],
            jnp.zeros((5, ff), F32),
        ],
        axis=0,
    )

    shard = jnp.concatenate(
        [w_back, w_in.reshape(rows, parts, width).transpose(1, 0, 2).reshape(parts * rows, width), w_out], axis=0
    )
    shard, x_far = lax.optimization_barrier((shard, x_far))
    gathered = lax.all_gather(shard, both, axis=0, tiled=True).reshape(cores * blocks, -1, width)
    direct = rows % 8 == 0 and blocks % 4 == 0 and (2 * blocks) % (4 * parts) == 0
    if direct:
        inner, outer = 4, blocks // 4
    else:
        inner, outer = 4, 4
        gathered = packed(*unpacked(gathered, parts), cores * inner * outer)

    pieces = (x, x_sib, x_far, swap(x_far, "head", 1))
    bias = jnp.pad(bias[None], ((0, 7), (0, 0)))
    if direct:
        qkv, weight = project(pieces, first, second, bias)
    else:
        shape = (16, width // 32, 3 * group)
        qkv, weight = project(
            pieces, first[:, :rows].reshape(shape), second[:, :rows].reshape(shape), bias
        )

    sequence = block // 2
    own_half = block % 2
    length = lax.dynamic_index_in_dim(lengths, sequence, 0, keepdims=False)
    flags = lax.dynamic_index_in_dim(pair_flip, sequence, 0, keepdims=False)
    flags = lax.dynamic_slice_in_dim(flags, core * heads, heads)
    bounds = [jnp.clip(length - h * half, 0, half) for h in (own_half, 1 - own_half)]
    sc = jnp.concatenate([flags, jnp.stack(bounds + [jnp.int32(local), core])]).astype(jnp.int32)

    context_own, context_sib, lse = attend(sc, qkv, group)
    other = swap(context_sib, "head", 1)
    at_core = core.reshape(1).astype(jnp.int32)
    out, grad_resid1, gc_own, gc_other, low, act, gh, gb, attn, sums = middle(
        at_core, x, context_own, other, cotangent[0], gathered, vec
    )
    grad_context = (gc_own, swap(gc_other, "head", 1))
    contexts = (context_own, context_sib)

    chip = weight_grads(at_core, act, gb, low, gh, context_own, other, attn, inner, outer)
    grad_context, chip = lax.optimization_barrier((grad_context, chip))
    near_groups = [[o * inner + i for i in range(inner)] for o in range(outer)]
    far_groups = [[o * inner + i for o in range(outer)] for i in range(inner)]

    def over_plane(value):
        flat = value.reshape(-1, value.shape[3])
        flat = lax.psum_scatter(flat, "blk", scatter_dimension=0, axis_index_groups=near_groups, tiled=True)
        return flat.reshape(value.shape[1:])

    def over_column(value):
        flat = value.reshape(-1, value.shape[2])
        return lax.psum_scatter(flat, "blk", scatter_dimension=0, axis_index_groups=far_groups, tiled=True)

    if direct:
        chip = over_plane(chip.reshape(inner, outer, (2 * parts + 1) * rows, width))
    else:
        chip = chip.transpose(1, 0, 2, 3, 4).reshape(inner * outer, -1, width)
        chip = packed(*unpacked(chip, parts), blocks)
        chip = lax.psum_scatter(chip, "blk", scatter_dimension=0, tiled=True)[0]

    v_sums = place(
        sums[2, 2 * width : 2 * width + group], sums[2, 2 * width + group : 3 * width], core == 1, 0
    ).reshape(-1)
    by_rows = [v_sums] + [sums[1, s * width : (s + 1) * width] for s in range(4)]
    by_rows = jnp.stack(by_rows + [sums[2, s * width : (s + 1) * width] for s in range(2)], axis=0)
    by_rows = by_rows.reshape(7, cores, blocks, rows).transpose(1, 2, 0, 3).reshape(cores, blocks, -1)
    early_small = jnp.concatenate([by_rows, sums[0].reshape(cores, blocks, parts * rows)], axis=2)
    early_small, grad_context = lax.optimization_barrier((early_small, grad_context))

    def part_rows(keep, send, *small_rows):
        if not direct:
            keep, send = (a.transpose(1, 0, 2, 3).reshape(blocks, rows, -1) for a in (keep, send))
        for extra in small_rows:
            if not direct:
                extra = extra.transpose(0, 2, 1, 3, 4).reshape(2, blocks, 8, -1)
            keep, send = (jnp.concatenate([a, b], axis=-2) for a, b in zip((keep, send), extra))
        return keep, swap(send, "head", 1)

    def finish_part(keep, came):
        both_cores = jnp.concatenate([keep, came], axis=-1)
        if direct:
            both_cores = both_cores.transpose(1, 0, 2, 3).reshape((blocks,) + both_cores.shape[2:])
        return lax.all_to_all(both_cores, "blk", 0, 0, tiled=True)

    def total_of(moved):
        return jnp.sum(moved.astype(F32), axis=0).reshape(moved.shape[1], 2, -1)

    pairs = group // LANES
    first_pairs = pairs - pairs // 3
    dq_a, dkv_a, sum_a, *grad_a = attend_back(
        sc, qkv, contexts, lse, grad_context, pieces, group, 0, first_pairs, inner, outer
    )
    keep_a, came_a = part_rows(*grad_a)
    if direct:
        part_a = jnp.concatenate([keep_a, came_a], axis=2)
        grad_context, part_a, chip = lax.optimization_barrier((grad_context, part_a, chip))
        part_a = over_plane(part_a)
    else:
        total_a = total_of(finish_part(keep_a, came_a))
    dq_b, dkv_b, sum_b, *grad_b = attend_back(
        sc, qkv, contexts, lse, grad_context, pieces, group, first_pairs, pairs - first_pairs, inner, outer
    )

    if direct:
        part_a, sum_b = lax.optimization_barrier((part_a, sum_b))
        chip = over_column(jnp.concatenate([chip, part_a], axis=1))
    q_sums = jnp.sum(jnp.concatenate([sum_a, sum_b], axis=0), axis=1)
    q_sums = lax.dynamic_update_slice_in_dim(jnp.zeros((width,), F32), q_sums, core * group, 0)
    grad_small = jnp.concatenate([q_sums.reshape(cores, blocks, rows), early_small], axis=2)
    room = 3 * (pairs - first_pairs) * LANES
    grad_small = jnp.pad(grad_small, ((0, 0), (0, 0), (0, room - grad_small.shape[2])))
    high = grad_small.astype(BF16)
    low_part = (grad_small - high.astype(F32)).astype(BF16)
    small_rows = jnp.pad(jnp.stack([high, low_part], axis=2), ((0, 0), (0, 0), (0, 6), (0, 0)))
    small_rows = jnp.where(core == 0, small_rows, small_rows[::-1])
    small_rows = small_rows.reshape(2, blocks // inner, inner, 8, room).transpose(0, 2, 1, 3, 4)

    dkv = (dkv_a, dkv_b)
    keep_b, came_b = part_rows(*grad_b, small_rows)
    keep_far, send_far = far_rows(dkv, weight)
    far_sib = swap(send_far, "head", 1)
    far_sum = (keep_far.astype(F32) + far_sib.astype(F32)).astype(BF16)
    moved_b = finish_part(keep_b, came_b)
    far_sum, dq_a, dq_b = lax.optimization_barrier((far_sum, dq_a, dq_b))
    far_in = swap(far_sum, "blk", 1)
    keep_near, send_near = near_rows((dq_a, dq_b), dkv, weight, grad_resid1)
    chip, send_near = lax.optimization_barrier((chip, send_near))
    near_sib = swap(send_near, "head", 1)
    grad_tokens = keep_near + near_sib.astype(F32) + far_in.astype(F32)

    if direct:
        sum_wback, sum_win, sum_wout, sum_wqkv, vectors = unpack(at_core, chip, moved_b, rows, parts)
        vectors = vectors[0] + vectors[1]
        vectors = vectors[: vectors.shape[0] // 2] + vectors[vectors.shape[0] // 2 :]
    else:
        total_b = total_of(moved_b)
        sum_wback = chip[: parts * rows].astype(F32)
        sum_win = chip[parts * rows : 2 * parts * rows].astype(F32)
        sum_win = sum_win.reshape(parts, rows, width).transpose(1, 0, 2).reshape(rows, ff)
        sum_wout = chip[2 * parts * rows : (2 * parts + 1) * rows].astype(F32)

        def columns_of(total):
            parts_of = lambda a: a.reshape(rows, -1, 3, LANES).transpose(0, 2, 1, 3).reshape(rows, 3, -1)
            return place(*(parts_of(total[:rows, s]) for s in (0, 1)), core == 1, 2)

        sum_wqkv = jnp.concatenate([columns_of(total_a), columns_of(total_b)], axis=3).reshape(rows, 3 * width)
        vectors = jnp.sum(total_b[rows : rows + 2], axis=(0, 1))

    def summed(slot, size=rows):
        return vectors[slot * rows : slot * rows + size]

    return (
        out[None],
        grad_tokens[None],
        sum_wqkv,
        summed(0),
        summed(1),
        sum_wout,
        summed(2),
        summed(4),
        summed(5),
        sum_win,
        summed(8, parts * rows),
        sum_wback,
        summed(3),
        summed(6),
        summed(7),
    )


def solution(mesh):
    split = P(("head", "blk"))
    matrix = P(("head", "blk"), None)
    rows = P("blk", "head", None)
    return jax.shard_map(
        per_device,
        mesh=mesh,
        in_specs=(
            rows,
            P(),
            P(),
            matrix,
            split,
            split,
            matrix,
            split,
            split,
            split,
            matrix,
            split,
            matrix,
            split,
            split,
            split,
            rows,
        ),
        out_specs=(
            rows,
            rows,
            matrix,
            split,
            split,
            matrix,
            split,
            split,
            split,
            matrix,
            split,
            matrix,
            split,
            split,
            split,
        ),
        check_vma=False,
    )
```
